1024 devices in a mesh: stream: 8 (over y_hi, core), cross: 128 (over x, y_lo, z).
Axes of the slice: x: 8, y: 8 (y_hi: 4, y_lo: 2; y = y_hi * 2 + y_lo), z: 8, core: 2. Of those that a mesh axis runs over, the one named last changes fastest.
Arguments:
- pressure: float32 [192, 1024, 128], P('stream', 'cross'), may hold values from -6 to 6
- geo_diag: float32 [3, 192, 1024, 128], P(None, 'stream', 'cross'), may hold values from 0.004 to 0.04
- geo_off: float32 [3, 192, 1024, 128], P(None, 'stream', 'cross'), may hold values from -0.008 to 0.008
- modes_first: float32 [24, 10, 10], P('stream'), may hold values from -2 to 2
- modes_second: float32 [128, 10, 10], P('cross'), may hold values from -2 to 2
- modes_third: float32 [16, 10, 10], replicated, may hold values from -2 to 2
- eigen_first: float32 [24, 10], P('stream'), may hold values from 0.3 to 3
- eigen_second: float32 [128, 10], P('cross'), may hold values from 0.3 to 3
- eigen_third: float32 [16, 10], replicated, may hold values from 0.3 to 3
Outputs:
- operator_out: float32 [192, 1024, 128], P('stream', 'cross')
- preconditioned: float32 [192, 1024, 128], P('stream', 'cross')
The draws below stay inside these ranges and needn't reach their ends.
All inputs are finite; a program needn't handle non-finite values.
Results may differ from the reference program's by a relative error of at most 0.00013.
Values sent between devices are 32-bit elements; how exact they have to be, the bound alone decides.
A program may use at most 32 MiB of HBM per device.

```python
import math
import jax
import jax.numpy as jnp
import numpy as np
from jax import lax

N1 = 8
M = 10
EZ = 16
EX = 24
EY = 128
PX = 192
PY = 1024
PZ = 128


def shard_levels(rng, dims, cuts, smallest, top_value):
    gain, own = 1.0, jax.random.fold_in(rng, 6)
    for position, shards_of in cuts:
        draws = jnp.exp(jax.random.uniform(jax.random.fold_in(own, position), (shards_of,), jnp.float32, smallest / len(cuts), top_value / len(cuts)))
        gain = gain * jnp.repeat(draws, dims[position] // shards_of).reshape([-1 if axis == position else 1 for axis in range(len(dims))])
    return gain


def scatter_about(own_key, dims, width, limit, pieces=(), kind=jnp.bfloat16):
    level = shard_levels(own_key, dims, pieces, -0.22, 0.18) if pieces else 1.0
    array = jax.random.normal(own_key, dims, jnp.float32) * width * level
    return jnp.minimum(jnp.maximum(array, -limit), limit).astype(kind)


def setup_inputs(seed: int = 0) -> dict:
    key_of = jax.random.split(jax.random.key(seed), 10)
    return {
        "pressure": scatter_about(key_of[0], (PX, PY, PZ), 1.0, 6.0, ((0, 8), (1, 128)), jnp.float32),
        "geo_diag": jnp.clip(jnp.exp(math.log(0.04) - 2.30258502 * jax.random.uniform(key_of[1], (3, PX, PY, PZ), jnp.float32) ** shard_levels(key_of[1], (3, PX, PY, PZ), ((1, 8), (2, 128)), -0.2, 0.2)), 0.004, 0.04),
        "geo_off": jnp.clip(jax.random.uniform(key_of[2], (3, PX, PY, PZ), jnp.float32, -0.008, 0.008) * shard_levels(key_of[2], (3, PX, PY, PZ), ((1, 8), (2, 128)), -0.4, 0.0), -0.008, 0.008),
        "modes_first": scatter_about(key_of[3], (EX, M, M), M ** -0.5, 2.0, ((0, 8),), jnp.float32),
        "modes_second": scatter_about(key_of[4], (EY, M, M), M ** -0.5, 2.0, ((0, 128),), jnp.float32),
        "modes_third": scatter_about(key_of[5], (EZ, M, M), M ** -0.5, 2.0, (), jnp.float32),
        "eigen_first": jnp.clip(jnp.exp(math.log(3.0) - 2.3025851 * jax.random.uniform(key_of[6], (EX, M), jnp.float32) ** shard_levels(key_of[6], (EX, M), ((0, 8),), -0.2, 0.2)), 0.3, 3.0),
        "eigen_second": jnp.clip(jnp.exp(math.log(3.0) - 2.3025851 * jax.random.uniform(key_of[7], (EY, M), jnp.float32) ** shard_levels(key_of[7], (EY, M), ((0, 128),), -0.2, 0.2)), 0.3, 3.0),
        "eigen_third": jnp.clip(jnp.exp(jax.random.uniform(key_of[8], (EZ, M), jnp.float32, math.log(0.3), math.log(3.0))), 0.3, 3.0),
    }


HIGHEST = lax.Precision.HIGHEST


def legendre_values(nodes, degree):
    table = np.zeros((nodes.shape[0], degree + 1))
    table[:, 0] = 1.0
    table[:, 1] = nodes
    for order in range(2, degree + 1):
        table[:, order] = ((2 * order - 1) * nodes * table[:, order - 1] - (order - 1) * table[:, order - 2]) / order
    return table


def derivative_table(points):
    degree = points - 1
    nodes = np.cos(np.pi * np.arange(points) / degree)
    for sweep in range(100):
        table = legendre_values(nodes, degree)
        nodes = nodes - (nodes * table[:, degree] - table[:, degree - 1]) / (points * table[:, degree])
    gll_nodes = nodes[::-1]
    legendre_at = legendre_values(gll_nodes, degree)[:, degree]
    diff_table = np.zeros((points, points))
    for first_index in range(points):
        for second_index in range(points):
            if first_index != second_index:
                diff_table[first_index, second_index] = legendre_at[first_index] / (
                    legendre_at[second_index] * (gll_nodes[first_index] - gll_nodes[second_index]))
    diff_table[0, 0] = -degree * (degree + 1) / 4.0
    diff_table[degree, degree] = degree * (degree + 1) / 4.0
    return diff_table


def group_size(blocks):
    return 16 if blocks % 16 == 0 else blocks


def along_first(source, matrix):
    nodes_count = matrix.shape[0]
    blocks = source.shape[0] // nodes_count
    shaped = source.reshape(blocks, nodes_count, source.shape[1], source.shape[2])
    result = jnp.einsum('ij,ajyz->aiyz', matrix, shaped, precision=HIGHEST)
    return result.reshape(source.shape)


def along_second(source, matrix):
    nodes_count = matrix.shape[0]
    blocks = source.shape[1] // nodes_count
    shaped = source.reshape(source.shape[0], blocks, nodes_count, source.shape[2])
    result = jnp.einsum('ij,xbjz->xbiz', matrix, shaped, precision=HIGHEST)
    return result.reshape(source.shape)


def along_third(source, matrix):
    nodes_count = matrix.shape[0]
    blocks = source.shape[2] // nodes_count
    grouped = group_size(blocks)
    kron_matrix = jnp.kron(jnp.eye(grouped, dtype=jnp.float32), matrix)
    shaped = source.reshape(source.shape[0], source.shape[1], blocks // grouped, grouped * nodes_count)
    result = jnp.einsum('xybl,kl->xybk', shaped, kron_matrix, precision=HIGHEST)
    return result.reshape(source.shape)


def modal_first(source, modes, backward):
    blocks = modes.shape[0]
    extent = modes.shape[1]
    shaped = source.reshape(blocks, extent, source.shape[1], source.shape[2])
    if backward:
        result = jnp.einsum('amp,apyz->amyz', modes, shaped, precision=HIGHEST)
    else:
        result = jnp.einsum('amp,amyz->apyz', modes, shaped, precision=HIGHEST)
    return result.reshape(source.shape)


def modal_second(source, modes, backward):
    blocks = modes.shape[0]
    extent = modes.shape[1]
    shaped = source.reshape(source.shape[0], blocks, extent, source.shape[2])
    if backward:
        result = jnp.einsum('bmp,xbpz->xbmz', modes, shaped, precision=HIGHEST)
    else:
        result = jnp.einsum('bmp,xbmz->xbpz', modes, shaped, precision=HIGHEST)
    return result.reshape(source.shape)


def modal_third(source, modes, backward):
    blocks = modes.shape[0]
    extent = modes.shape[1]
    grouped = group_size(blocks)
    identity = jnp.eye(grouped, dtype=jnp.float32)
    kron_modes = jnp.einsum('gh,bgmp->bgmhp', identity, modes.reshape(blocks // grouped, grouped, extent, extent),
                            precision=HIGHEST).reshape(blocks // grouped, grouped * extent, grouped * extent)
    shaped = source.reshape(source.shape[0], source.shape[1], blocks // grouped, grouped * extent)
    if backward:
        result = jnp.einsum('xybp,bmp->xybm', shaped, kron_modes, precision=HIGHEST)
    else:
        result = jnp.einsum('xybm,bmp->xybp', shaped, kron_modes, precision=HIGHEST)
    return result.reshape(source.shape)


def local_laplacian(pressure, geo_diag, geo_off, diff_matrix):
    grad_first = along_first(pressure, diff_matrix)
    grad_second = along_second(pressure, diff_matrix)
    grad_third = along_third(pressure, diff_matrix)
    flux_first = geo_diag[0] * grad_first + geo_off[0] * grad_second + geo_off[1] * grad_third
    flux_second = geo_off[0] * grad_first + geo_diag[1] * grad_second + geo_off[2] * grad_third
    flux_third = geo_off[1] * grad_first + geo_off[2] * grad_second + geo_diag[2] * grad_third
    transposed = diff_matrix.T
    return (along_first(flux_first, transposed) + along_second(flux_second, transposed)
            + along_third(flux_third, transposed))


def owner_sum_axis(source, dimension, offset, nodes_count):
    length = source.shape[dimension]
    broadcast_shape = [1] * source.ndim
    broadcast_shape[dimension] = length
    local_node = ((jnp.arange(length, dtype=jnp.int32) - offset) % nodes_count).reshape(broadcast_shape)
    zero_slab = jnp.zeros_like(lax.slice_in_dim(source, 0, 1, axis=dimension))
    previous = jnp.concatenate([zero_slab, lax.slice_in_dim(source, 0, length - 1, axis=dimension)], axis=dimension)
    following = jnp.concatenate([lax.slice_in_dim(source, 1, length, axis=dimension), zero_slab], axis=dimension)
    return (source + jnp.where(local_node == 0, previous, 0.0)
            + jnp.where(local_node == nodes_count - 1, following, 0.0))


def owner_sum(source, offset, nodes_count):
    summed = owner_sum_axis(source, 0, offset, nodes_count)
    summed = owner_sum_axis(summed, 1, offset, nodes_count)
    return owner_sum_axis(summed, 2, 0, nodes_count)


def with_blocks(section, dimension, blocks, extent):
    new_shape = list(section.shape)
    new_shape[dimension:dimension + 1] = [blocks, extent]
    return section.reshape(new_shape)


def extend_axis(padded, dimension, blocks, nodes_count):
    extent_all = blocks * nodes_count
    left_part = lax.slice_in_dim(padded, 0, extent_all, stride=nodes_count, axis=dimension)
    middle = lax.slice_in_dim(padded, 2, extent_all + 2, axis=dimension)
    right_part = lax.slice_in_dim(padded, nodes_count + 3, extent_all + 4, stride=nodes_count, axis=dimension)
    joined = jnp.concatenate([with_blocks(left_part, dimension, blocks, 1),
                              with_blocks(middle, dimension, blocks, nodes_count),
                              with_blocks(right_part, dimension, blocks, 1)], axis=dimension + 1)
    new_shape = list(padded.shape)
    new_shape[dimension] = blocks * (nodes_count + 2)
    return joined.reshape(new_shape)


def restrict_axis(source, dimension, blocks, extent):
    shaped = with_blocks(source, dimension, blocks, extent)
    kept_part = lax.slice_in_dim(shaped, 1, extent - 1, axis=dimension + 1)
    new_shape = list(source.shape)
    new_shape[dimension] = blocks * (extent - 2)
    return kept_part.reshape(new_shape)


def fast_solve(extended, modes_first, modes_second, modes_third, eigen_first, eigen_second, eigen_third):
    spectral = modal_first(extended, modes_first, False)
    spectral = modal_second(spectral, modes_second, False)
    spectral = modal_third(spectral, modes_third, False)
    denominator = eigen_first.reshape(-1, 1, 1) + eigen_second.reshape(1, -1, 1) + eigen_third.reshape(1, 1, -1)
    spectral = spectral / denominator
    solved = modal_first(spectral, modes_first, True)
    solved = modal_second(solved, modes_second, True)
    return modal_third(solved, modes_third, True)


def reference(pressure, geo_diag, geo_off, modes_first, modes_second, modes_third, eigen_first, eigen_second,
              eigen_third):
    diff_matrix = jnp.asarray(derivative_table(N1), dtype=jnp.float32)
    local_product = local_laplacian(pressure, geo_diag, geo_off, diff_matrix)
    operator_out = owner_sum(local_product, 0, N1)
    padded = jnp.pad(operator_out, 2)
    extended = extend_axis(padded, 0, EX, N1)
    extended = extend_axis(extended, 1, EY, N1)
    extended = extend_axis(extended, 2, EZ, N1)
    solved = fast_solve(extended, modes_first, modes_second, modes_third, eigen_first, eigen_second, eigen_third)
    restricted = restrict_axis(solved, 0, EX, N1 + 2)
    restricted = restrict_axis(restricted, 1, EY, N1 + 2)
    restricted = restrict_axis(restricted, 2, EZ, N1 + 2)
    preconditioned = owner_sum(restricted, 0, N1)
    return (operator_out, preconditioned)
```

```python
import jax
import jax.numpy as jnp
import numpy as np
from jax import lax
from jax.experimental import pallas as pl
from jax.experimental.pallas import tpu as pltpu
from jax.sharding import PartitionSpec as P

N1 = 8
M = 10
AB = 3
CB = 16
NF = AB * N1
OWN = NF * N1
HALO = 192
COLS = OWN + HALO
STEP = 104
ROWS = 320
DEEP = 384
WIDE = 256
F32 = jnp.float32
BF16 = jnp.bfloat16
HIGHEST = lax.Precision.HIGHEST
MESH = pl.DeviceIdType.MESH

SLOTS = ((0, -1), (0, 1), (-1, 0), (1, 0), (-1, -1), (-1, 1), (1, -1), (1, 1))
FIRST_AT = (0, 48, 96, 112, 128, 144, 160, 176)
FIRST_LEN = (48, 48, 16, 16, 16, 16, 16, 16)
LAST_AT = (0, 24, 48, 56, 64, 72, 80, 88)
LAST_LEN = (24, 24, 8, 8, 8, 8, 8, 8)
LAST_FROM = (0, 24, 48, 56, 48, 48, 56, 56)


def legendre_values(nodes, degree):
    table = np.zeros((nodes.shape[0], degree + 1))
    table[:, 0] = 1.0
    table[:, 1] = nodes
    for order in range(2, degree + 1):
        table[:, order] = (
            (2 * order - 1) * nodes * table[:, order - 1] - (order - 1) * table[:, order - 2]
        ) / order
    return table


def derivative_table(points):
    degree = points - 1
    nodes = np.cos(np.pi * np.arange(points) / degree)
    for sweep in range(100):
        table = legendre_values(nodes, degree)
        nodes = nodes - (nodes * table[:, degree] - table[:, degree - 1]) / (
            points * table[:, degree]
        )
    gll_nodes = nodes[::-1]
    legendre_at = legendre_values(gll_nodes, degree)[:, degree]
    diff_table = np.zeros((points, points))
    for first_index in range(points):
        for second_index in range(points):
            if first_index != second_index:
                diff_table[first_index, second_index] = legendre_at[first_index] / (
                    legendre_at[second_index] * (gll_nodes[first_index] - gll_nodes[second_index])
                )
    diff_table[0, 0] = -degree * (degree + 1) / 4.0
    diff_table[degree, degree] = degree * (degree + 1) / 4.0
    return diff_table


LAYER_NODE = [0, 1, 1, 2, 3, 4, 5, 6, 7, 8, 8, 9]


def tables():
    diff = derivative_table(N1).astype(np.float32)
    eye8 = np.eye(N1, dtype=np.float32)
    left = np.concatenate([np.kron(diff, eye8), np.kron(eye8, diff)], axis=0)
    third = np.kron(np.eye(CB, dtype=np.float32), diff.T)
    gather = np.zeros((CB * N1, WIDE), np.float32)
    scatter = np.zeros((WIDE, CB * N1), np.float32)
    for c in range(CB):
        for layer in range(12):
            at = c * N1 + layer - 2
            if 0 <= at < CB * N1:
                gather[at, LAYER_NODE[layer] * 16 + c] = 1.0
                if 0 < layer < 11:
                    scatter[LAYER_NODE[layer] * 16 + c, at] = 1.0
    pick_p = np.zeros((ROWS, 128), np.float32)
    pick_q = np.zeros((ROWS, 128), np.float32)
    for a in range(AB):
        for p in range(M):
            for q in range(M):
                pick_p[a * STEP + p * M + q, p] = 1.0
                pick_q[a * STEP + p * M + q, q] = 1.0
    first_layer = np.zeros(COLS, np.int32)
    second_layer = np.full(COLS, -1, np.int32)
    for f in range(NF):
        for j in range(N1):
            first_layer[f * N1 + j] = f + 2
            second_layer[f * N1 + j] = j + 2
    for slot, (side_s, side_c) in enumerate(SLOTS):
        for row in range(FIRST_LEN[slot]):
            col = OWN + FIRST_AT[slot] + row
            if side_s == 0:
                jj, f = divmod(row, NF)
                first_layer[col] = f + 2
                second_layer[col] = jj if side_c < 0 else 10 + jj
            else:
                l, j = divmod(row, N1)
                first_layer[col] = l if side_s < 0 else 26 + l
                if side_c == 0:
                    second_layer[col] = j + 2
                elif side_c < 0:
                    second_layer[col] = j - 6 if j >= 6 else -1
                else:
                    second_layer[col] = 10 + j if j < 2 else -1
    cols_first = np.zeros((128, COLS), np.float32)
    cols_second = np.zeros((128, COLS), np.float32)
    for col in range(COLS):
        for a in range(AB):
            layer = first_layer[col] - N1 * a
            if 0 <= layer < 12:
                cols_first[LAYER_NODE[layer] * 8 + a, col] = 1.0
        if second_layer[col] >= 0:
            cols_second[LAYER_NODE[second_layer[col]] * 8 + 3, col] = 1.0
    exact = [gather, scatter, pick_p, pick_q, cols_first, cols_second]
    return [left, left.T.copy(), third, third.T.copy()] + [t.astype(BF16) for t in exact]


def dot(a, b):
    return lax.dot_general(a, b, (((1,), (0,)), ((), ())), preferred_element_type=F32)


def split(value):
    high = value.astype(BF16)
    return high, (value - high.astype(F32)).astype(BF16)


def product(a, b):
    return dot(a[0], b[0]) + (dot(a[1], b[0]) + dot(a[0], b[1]))


def select(table, value):
    high, low = split(value)
    return dot(table, high), dot(table, low)


def iota(shape, dimension):
    return lax.broadcasted_iota(jnp.int32, shape, dimension)


def block_of(rows):
    return (rows >= STEP).astype(jnp.int32) + (rows >= 2 * STEP).astype(jnp.int32)


def kernel(*refs):
    hbm = refs[:19]
    op_ref, pre_ref = refs[19:21]
    vmem = refs[21:40]
    (
        own,
        stage,
        halo,
        stage_last,
        halo_last,
        assembled,
        solved,
        kept,
        modes3,
        modes12,
        eigen,
        load_sem,
        send_sem,
        recv_sem,
        send_last,
        recv_last,
    ) = refs[40:]
    (
        pressure,
        geo_diag,
        geo_off,
        modes_first,
        modes_second,
        modes_third,
        eigen_first,
        eigen_second,
        eigen_third,
        left,
        left_t,
        third,
        third_t,
        gather,
        scatter,
        pick_p,
        pick_q,
        cols_first,
        cols_second,
    ) = vmem
    n_s, n_c = lax.axis_size("stream"), lax.axis_size("cross")
    me_s, me_c = lax.axis_index("stream"), lax.axis_index("cross")

    def peer(side_s, side_c):
        return {
            "stream": lax.rem(me_s + side_s + n_s, n_s),
            "cross": lax.rem(me_c + side_c + n_c, n_c),
        }

    barrier = pltpu.get_barrier_semaphore()
    for side_s, side_c in SLOTS:
        pl.semaphore_signal(barrier, inc=1, device_id=peer(side_s, side_c), device_id_type=MESH)
    loads = [
        pltpu.make_async_copy(hbm[i], vmem[i], load_sem.at[i]) for i in range(19)
    ]
    order = [0, 9, 11, 1, 2, 10, 12, 3, 4, 5, 6, 7, 8, 13, 14, 15, 16, 17, 18]
    for i in order:
        loads[i].start()

    modes3[...] = jnp.zeros_like(modes3)
    modes12[...] = jnp.zeros_like(modes12)
    eigen[...] = jnp.zeros_like(eigen)

    for i in (0, 9, 11):
        loads[i].wait()
    pres = pressure[...].reshape(OWN, 128)
    pres_split = split(pres)
    left_split = split(left[...])
    third_split = split(third[...])
    per = N1 * N1
    along = [
        product(left_split, tuple(part[a * per : (a + 1) * per] for part in pres_split))
        for a in range(AB)
    ]
    grad_third = product(pres_split, third_split)
    for i in (1, 2, 10, 12):
        loads[i].wait()
    left_t_split = split(left_t[...])
    third_t_split = split(third_t[...])
    for a in range(AB):
        rows = pl.ds(a * N1, N1)
        d0, d1, d2 = (geo_diag[k, rows].reshape(per, 128) for k in range(3))
        o0, o1, o2 = (geo_off[k, rows].reshape(per, 128) for k in range(3))
        g1, g2 = along[a][:per], along[a][per:]
        g3 = grad_third[a * per : (a + 1) * per]
        flux_first = d0 * g1 + o0 * g2 + o1 * g3
        flux_second = o0 * g1 + d1 * g2 + o2 * g3
        flux_third = o1 * g1 + o2 * g2 + d2 * g3
        both = split(jnp.concatenate([flux_first, flux_second], axis=0))
        own[pl.ds(a * per, per), :] = product(left_t_split, both) + product(
            split(flux_third), third_t_split
        )
    for k, node in enumerate((6, 7, 0, 1)):
        stage[pl.ds(k * NF, NF), :] = own[pl.ds(node, NF, stride=N1), :]

    pl.semaphore_wait(barrier, len(SLOTS))
    first_from = (
        stage.at[pl.ds(0, 48), :],
        stage.at[pl.ds(48, 48), :],
        own.at[pl.ds(OWN - 16, 16), :],
        own.at[pl.ds(0, 16), :],
        own.at[pl.ds(OWN - 16, 16), :],
        own.at[pl.ds(OWN - 16, 16), :],
        own.at[pl.ds(0, 16), :],
        own.at[pl.ds(0, 16), :],
    )
    sends = {}
    for slot in (4, 5, 6, 7, 0, 1, 2, 3):
        side_s, side_c = SLOTS[slot]
        sends[slot] = pltpu.make_async_remote_copy(
            src_ref=first_from[slot],
            dst_ref=halo.at[pl.ds(FIRST_AT[slot], FIRST_LEN[slot]), :],
            send_sem=send_sem.at[slot],
            recv_sem=recv_sem.at[slot],
            device_id=peer(-side_s, -side_c),
            device_id_type=MESH,
        )
        sends[slot].start()

    at_s = {-1: me_s > 0, 1: me_s < n_s - 1}
    at_c = {-1: me_c > 0, 1: me_c < n_c - 1}

    def there(slot):
        side_s, side_c = SLOTS[slot]
        if side_s == 0:
            return at_c[side_c]
        if side_c == 0:
            return at_s[side_s]
        return jnp.logical_and(at_s[side_s], at_c[side_c])

    for i in (3, 4, 5, 6, 7, 8, 13, 14, 15, 16, 17, 18):
        loads[i].wait()
    for m in range(M):
        modes3[m * 16 : m * 16 + CB, 0:M] = modes_third[m]
        modes12[m * 8 : m * 8 + AB, 0:M] = modes_first[m]
        modes12[m * 8 + 3 : m * 8 + 4, 0:M] = modes_second[m]
    eigen[0:AB, 0:M] = eigen_first[...]
    eigen[8:9, 0:M] = eigen_second[...]
    eigen[16 : 16 + CB, 0:M] = eigen_third[...]

    spread = jnp.where(iota((128, WIDE), 0) == (iota((128, WIDE), 1) & 15), 1.0, 0.0).astype(F32)
    diagonal = jnp.dot(modes3[...], spread, precision=HIGHEST, preferred_element_type=F32)
    same = (iota((WIDE, WIDE), 0) & 15) == (iota((WIDE, WIDE), 1) >> 4)
    diagonal = jnp.where(same, diagonal, 0.0)
    fore = tuple(part.astype(BF16) for part in select(gather[...], diagonal))
    back = []
    for part in split(jnp.transpose(diagonal)):
        back.append(dot(part, scatter[...]).astype(BF16))

    take_p = pick_p[...].astype(F32)
    take_q = pick_q[...].astype(F32)
    nt = (((1,), (1,)), ((), ()))
    by_p = lax.dot_general(take_p, modes12[...], nt, precision=HIGHEST, preferred_element_type=F32)
    by_q = lax.dot_general(take_q, modes12[...], nt, precision=HIGHEST, preferred_element_type=F32)
    by_p = jnp.where(block_of(iota((ROWS, 128), 0)) == (iota((ROWS, 128), 1) & 7), by_p, 0.0)
    by_p_split, by_q_split = split(by_p), split(by_q)
    forward = (dot(by_p_split[0], cols_first[...]) + dot(by_p_split[1], cols_first[...])) * (
        dot(by_q_split[0], cols_second[...]) + dot(by_q_split[1], cols_second[...])
    )
    forward_own = forward[:, :OWN]
    cols = iota((1, COLS), 1)
    absent = jnp.zeros((1, COLS), jnp.int32)
    for slot in range(len(SLOTS)):
        begin = OWN + FIRST_AT[slot]
        inside = jnp.logical_and(cols >= begin, cols < begin + FIRST_LEN[slot])
        missing = 1 - there(slot).astype(jnp.int32)
        absent = absent + jnp.where(inside, missing, 0)
    forward_halo = jnp.where(absent > 0, 0.0, forward)[:, OWN:]
    own_split = split(forward_own)
    halo_split = split(forward_halo)

    relative = (iota((ROWS, WIDE), 1) >> 3) + 2 - N1 * block_of(iota((ROWS, WIDE), 0))
    keep = jnp.logical_and(relative != 0, relative != 11)
    square = jnp.where(keep, forward[:, :WIDE], 0.0)
    square = jnp.concatenate([square, jnp.zeros((DEEP - ROWS, WIDE), F32)], axis=0)
    kept[...] = jnp.transpose(square)
    back_own = split(kept[pl.ds(0, OWN), :])
    back_edge = split(
        jnp.concatenate(
            [
                kept[pl.ds(0, 8), :],
                kept[pl.ds(OWN - 8, 8), :],
            ],
            axis=0,
        )
    )
    back_far = split(
        jnp.concatenate(
            [kept[pl.ds(7 + 8 * f, 1), :] for f in range(NF)]
            + [kept[pl.ds(8 * f, 1), :] for f in range(NF)],
            axis=0,
        )
    )

    third_eigen = jnp.dot(
        eigen[16 : 16 + CB, :], spread, precision=HIGHEST, preferred_element_type=F32
    )
    third_eigen = jnp.where(
        iota((CB, WIDE), 0) == (iota((CB, WIDE), 1) >> 4), third_eigen, 0.0
    )
    lane_part = jnp.sum(third_eigen, axis=0, keepdims=True)
    inverse = []
    edges = [0, STEP, 2 * STEP, ROWS]
    for a in range(AB):
        rows = slice(edges[a], edges[a + 1])
        row_part = jnp.sum(
            take_p[rows] * eigen[a : a + 1, :] + take_q[rows] * eigen[8:9, :],
            axis=1,
            keepdims=True,
        )
        total = row_part + lane_part
        inverse.append(1.0 / jnp.where(total > 0.0, total, 1.0))
    inverse = jnp.concatenate(inverse, axis=0)

    own_third = product(split(own[...]), fore)
    spectral_own = product(own_split, split(own_third))

    for slot in range(len(SLOTS)):
        sends[slot].wait_recv()
    halo_third = product(split(halo[...]), fore)
    spectral = (spectral_own + product(halo_split, split(halo_third))) * inverse
    spectral = split(
        jnp.concatenate([spectral, jnp.zeros((DEEP - ROWS, WIDE), F32)], axis=0)
    )
    stage_last[pl.ds(0, 48), :] = product(split(product(back_far, spectral)), back)
    edge = product(split(product(back_edge, spectral)), back)
    stage_last[pl.ds(48, 8), :] = edge[8:16]
    stage_last[pl.ds(56, 8), :] = edge[0:8]
    last = {}
    for slot in (4, 5, 6, 7, 0, 1, 2, 3):
        side_s, side_c = SLOTS[slot]
        last[slot] = pltpu.make_async_remote_copy(
            src_ref=stage_last.at[pl.ds(LAST_FROM[slot], LAST_LEN[slot]), :],
            dst_ref=halo_last.at[pl.ds(LAST_AT[slot], LAST_LEN[slot]), :],
            send_sem=send_last.at[slot],
            recv_sem=recv_last.at[slot],
            device_id=peer(-side_s, -side_c),
            device_id_type=MESH,
        )
        last[slot].start()

    sub = iota((8, 128), 0)

    def shifted(tile, to_top):
        moved = pltpu.roll(tile, 1 if to_top else 7, 0)
        return jnp.where(sub == (0 if to_top else 7), moved, 0.0)

    assembled[...] = own[...]
    for slot, node, row in ((0, 0, 24), (1, 7, 48)):
        place = pl.ds(node, NF, stride=N1)
        got = jnp.where(there(slot), halo[pl.ds(row, NF), :], 0.0)
        assembled[place, :] = assembled[place, :] + got

    def layer_beside(slot, at_prev, at_next, side):
        rows = 8 if side < 0 else 0
        base = jnp.where(there(slot), halo[pl.ds(FIRST_AT[slot] + rows, 8), :], 0.0)
        corner = halo[pl.ds(FIRST_AT[at_prev] + rows, 8), :]
        base = base + jnp.where(there(at_prev), shifted(corner, True), 0.0)
        corner = halo[pl.ds(FIRST_AT[at_next] + rows, 8), :]
        return base + jnp.where(there(at_next), shifted(corner, False), 0.0)

    assembled[pl.ds(0, 8), :] = assembled[pl.ds(0, 8), :] + layer_beside(2, 4, 5, -1)
    assembled[pl.ds(OWN - 8, 8), :] = assembled[pl.ds(OWN - 8, 8), :] + layer_beside(3, 6, 7, 1)
    for a in range(AB - 1):
        at = (a * N1 + 7) * N1
        total = assembled[pl.ds(at, 8), :] + assembled[pl.ds(at + 8, 8), :]
        assembled[pl.ds(at, 8), :] = total
        assembled[pl.ds(at + 8, 8), :] = total
    value = assembled[...]
    lane = iota((OWN, 128), 1)
    from_left = jnp.where(jnp.logical_and((lane & 7) == 0, lane > 0), pltpu.roll(value, 1, 1), 0.0)
    from_right = jnp.where(
        jnp.logical_and((lane & 7) == 7, lane < 127), pltpu.roll(value, 127, 1), 0.0
    )
    op_ref[...] = (value + from_left + from_right).reshape(NF, N1, 128)

    solved[...] = product(split(product(back_own, spectral)), back)

    for slot in range(len(SLOTS)):
        last[slot].wait_recv()
    for slot, node, row in ((0, 0, 0), (1, 7, 24)):
        place = pl.ds(node, NF, stride=N1)
        got = jnp.where(there(slot), halo_last[pl.ds(row, NF), :], 0.0)
        solved[place, :] = solved[place, :] + got

    def layer_last(slot, at_prev, at_next):
        base = jnp.where(there(slot), halo_last[pl.ds(LAST_AT[slot], 8), :], 0.0)
        corner = halo_last[pl.ds(LAST_AT[at_prev], 8), :]
        base = base + jnp.where(there(at_prev), shifted(corner, True), 0.0)
        corner = halo_last[pl.ds(LAST_AT[at_next], 8), :]
        return base + jnp.where(there(at_next), shifted(corner, False), 0.0)

    solved[pl.ds(0, 8), :] = solved[pl.ds(0, 8), :] + layer_last(2, 4, 5)
    solved[pl.ds(OWN - 8, 8), :] = solved[pl.ds(OWN - 8, 8), :] + layer_last(3, 6, 7)
    pre_ref[...] = solved[...].reshape(NF, N1, 128)

    for slot in range(len(SLOTS)):
        sends[slot].wait_send()
        last[slot].wait_send()


def shards(*args):
    operands = list(args) + [jnp.asarray(t) for t in tables()]
    for i in (3, 4, 5):
        operands[i] = jnp.transpose(operands[i], (1, 0, 2))
    out = jax.ShapeDtypeStruct((NF, N1, CB * N1), F32)
    return pl.pallas_call(
        kernel,
        out_shape=(out, out),
        in_specs=[pl.BlockSpec(memory_space=pl.ANY)] * len(operands),
        out_specs=(pl.BlockSpec(memory_space=pltpu.VMEM),) * 2,
        scratch_shapes=[pltpu.VMEM(t.shape, t.dtype) for t in operands]
        + [
            pltpu.VMEM((OWN, 128), F32),
            pltpu.VMEM((96, 128), F32),
            pltpu.VMEM((HALO, 128), F32),
            pltpu.VMEM((64, 128), F32),
            pltpu.VMEM((96, 128), F32),
            pltpu.VMEM((OWN, 128), F32),
            pltpu.VMEM((OWN, 128), F32),
            pltpu.VMEM((WIDE, DEEP), F32),
            pltpu.VMEM((WIDE, 128), F32),
            pltpu.VMEM((128, 128), F32),
            pltpu.VMEM((32, 128), F32),
            pltpu.SemaphoreType.DMA((19,)),
            pltpu.SemaphoreType.DMA((8,)),
            pltpu.SemaphoreType.DMA((8,)),
            pltpu.SemaphoreType.DMA((8,)),
            pltpu.SemaphoreType.DMA((8,)),
        ],
        compiler_params=pltpu.CompilerParams(collective_id=0, has_side_effects=True),
        name="pressure_step",
    )(*operands)


def solution(mesh):
    in_specs = (
        P("stream", "cross", None),
        P(None, "stream", "cross", None),
        P(None, "stream", "cross", None),
        P("stream", None, None),
        P("cross", None, None),
        P(),
        P("stream", None),
        P("cross", None),
        P(),
    )
    out_specs = (P("stream", "cross", None), P("stream", "cross", None))
    return jax.shard_map(shards, mesh=mesh, in_specs=in_specs, out_specs=out_specs, check_vma=False)
```

```python
import functools

import jax
import jax.numpy as jnp
import numpy as np
from jax import lax
from jax.experimental import pallas as pl
from jax.experimental.pallas import tpu as pltpu
from jax.sharding import PartitionSpec as P

N1 = 8
M = 10
AB = 3
CB = 16
NF = AB * N1
OWN = NF * N1
HALO = 192
COLS = OWN + HALO
STEP = 104
ROWS = 320
DEEP = 384
WIDE = 256
F32 = jnp.float32
BF16 = jnp.bfloat16
HIGHEST = lax.Precision.HIGHEST
MESH = pl.DeviceIdType.MESH

SLOTS = ((0, -1), (0, 1), (-1, 0), (1, 0), (-1, -1), (-1, 1), (1, -1), (1, 1))
FIRST_AT = (0, 48, 96, 112, 128, 144, 160, 176)
FIRST_LEN = (48, 48, 16, 16, 16, 16, 16, 16)
LAST_AT = (0, 24, 48, 56, 64, 72, 80, 88)
LAST_LEN = (24, 24, 8, 8, 8, 8, 8, 8)
LAST_FROM = (0, 24, 48, 56, 48, 48, 56, 56)
FAR_FIRST = (4, 5, 6, 7, 0, 1, 2, 3)


def legendre_values(nodes, degree):
    table = np.zeros((nodes.shape[0], degree + 1))
    table[:, 0] = 1.0
    table[:, 1] = nodes
    for order in range(2, degree + 1):
        table[:, order] = (
            (2 * order - 1) * nodes * table[:, order - 1] - (order - 1) * table[:, order - 2]
        ) / order
    return table


def derivative_table(points):
    degree = points - 1
    nodes = np.cos(np.pi * np.arange(points) / degree)
    for sweep in range(100):
        table = legendre_values(nodes, degree)
        nodes = nodes - (nodes * table[:, degree] - table[:, degree - 1]) / (
            points * table[:, degree]
        )
    gll_nodes = nodes[::-1]
    legendre_at = legendre_values(gll_nodes, degree)[:, degree]
    diff_table = np.zeros((points, points))
    for first_index in range(points):
        for second_index in range(points):
            if first_index != second_index:
                diff_table[first_index, second_index] = legendre_at[first_index] / (
                    legendre_at[second_index] * (gll_nodes[first_index] - gll_nodes[second_index])
                )
    diff_table[0, 0] = -degree * (degree + 1) / 4.0
    diff_table[degree, degree] = degree * (degree + 1) / 4.0
    return diff_table


LAYER_NODE = [0, 1, 1, 2, 3, 4, 5, 6, 7, 8, 8, 9]


def tables():
    diff = derivative_table(N1).astype(np.float32)
    eye8 = np.eye(N1, dtype=np.float32)
    left = np.concatenate([np.kron(diff, eye8), np.kron(eye8, diff)], axis=0)
    third = np.kron(np.eye(CB, dtype=np.float32), diff.T)
    gather = np.zeros((CB * N1, WIDE), np.float32)
    scatter = np.zeros((WIDE, CB * N1), np.float32)
    for c in range(CB):
        for layer in range(12):
            at = c * N1 + layer - 2
            if 0 <= at < CB * N1:
                gather[at, LAYER_NODE[layer] * 16 + c] = 1.0
                if 0 < layer < 11:
                    scatter[LAYER_NODE[layer] * 16 + c, at] = 1.0
    pick_p = np.zeros((ROWS, 128), np.float32)
    pick_q = np.zeros((ROWS, 128), np.float32)
    for a in range(AB):
        for p in range(M):
            for q in range(M):
                pick_p[a * STEP + p * M + q, p] = 1.0
                pick_q[a * STEP + p * M + q, q] = 1.0
    first_layer = np.zeros(COLS, np.int32)
    second_layer = np.full(COLS, -1, np.int32)
    for f in range(NF):
        for j in range(N1):
            first_layer[f * N1 + j] = f + 2
            second_layer[f * N1 + j] = j + 2
    for slot, (side_s, side_c) in enumerate(SLOTS):
        for row in range(FIRST_LEN[slot]):
            col = OWN + FIRST_AT[slot] + row
            if side_s == 0:
                jj, f = divmod(row, NF)
                first_layer[col] = f + 2
                second_layer[col] = jj if side_c < 0 else 10 + jj
            else:
                l, j = divmod(row, N1)
                first_layer[col] = l if side_s < 0 else 26 + l
                if side_c == 0:
                    second_layer[col] = j + 2
                elif side_c < 0:
                    second_layer[col] = j - 6 if j >= 6 else -1
                else:
                    second_layer[col] = 10 + j if j < 2 else -1
    cols_first = np.zeros((128, COLS), np.float32)
    cols_second = np.zeros((128, COLS), np.float32)
    for col in range(COLS):
        for a in range(AB):
            layer = first_layer[col] - N1 * a
            if 0 <= layer < 12:
                cols_first[LAYER_NODE[layer] * 8 + a, col] = 1.0
        if second_layer[col] >= 0:
            cols_second[LAYER_NODE[second_layer[col]] * 8 + 3, col] = 1.0
    exact = [gather, scatter, pick_p, pick_q, cols_first, cols_second]
    return [left, left.T.copy(), third, third.T.copy()] + [t.astype(BF16) for t in exact]


def dot(a, b):
    return lax.dot_general(a, b, (((1,), (0,)), ((), ())), preferred_element_type=F32)


def split(value):
    high = value.astype(BF16)
    return high, (value - high.astype(F32)).astype(BF16)


def product(a, b):
    return dot(a[0], b[0]) + (dot(a[1], b[0]) + dot(a[0], b[1]))


def select(table, value):
    high, low = split(value)
    return dot(table, high), dot(table, low)


def iota(shape, dimension):
    return lax.broadcasted_iota(jnp.int32, shape, dimension)


def block_of(rows):
    return (rows >= STEP).astype(jnp.int32) + (rows >= 2 * STEP).astype(jnp.int32)


def kernel(*refs):
    hbm = refs[:19]
    op_ref, pre_ref = refs[19:21]
    vmem = refs[21:40]
    (
        own,
        stage,
        halo,
        stage_last,
        halo_last,
        assembled,
        solved,
        kept,
        modes3,
        modes12,
        eigen,
        load_sem,
        send_sem,
        recv_sem,
        send_last,
        recv_last,
    ) = refs[40:]
    (
        pressure,
        geo_diag,
        geo_off,
        modes_first,
        modes_second,
        modes_third,
        eigen_first,
        eigen_second,
        eigen_third,
        left,
        left_t,
        third,
        third_t,
        gather,
        scatter,
        pick_p,
        pick_q,
        cols_first,
        cols_second,
    ) = vmem
    n_s, n_c = lax.axis_size("stream"), lax.axis_size("cross")
    me_s, me_c = lax.axis_index("stream"), lax.axis_index("cross")

    def peer(side_s, side_c):
        return {
            "stream": lax.rem(me_s + side_s + n_s, n_s),
            "cross": lax.rem(me_c + side_c + n_c, n_c),
        }

    at_s = {-1: me_s > 0, 0: True, 1: me_s < n_s - 1}
    at_c = {-1: me_c > 0, 0: True, 1: me_c < n_c - 1}

    def there(side_s, side_c):
        if side_s == 0:
            return at_c[side_c]
        if side_c == 0:
            return at_s[side_s]
        return jnp.logical_and(at_s[side_s], at_c[side_c])

    def for_each(order, sign, act):
        for slot in order:
            side_s, side_c = SLOTS[slot]
            pl.when(there(sign * side_s, sign * side_c))(functools.partial(act, slot))

    halo[...] = jnp.zeros_like(halo)
    halo_last[...] = jnp.zeros_like(halo_last)
    barrier = pltpu.get_barrier_semaphore()

    def greet(slot):
        pl.semaphore_signal(barrier, inc=1, device_id=peer(*SLOTS[slot]), device_id_type=MESH)

    for_each(range(8), 1, greet)
    count_s = at_s[-1].astype(jnp.int32) + at_s[1].astype(jnp.int32)
    count_c = at_c[-1].astype(jnp.int32) + at_c[1].astype(jnp.int32)
    neighbours = count_s + count_c + count_s * count_c
    loads = [
        pltpu.make_async_copy(hbm[i], vmem[i], load_sem.at[i]) for i in range(19)
    ]
    order = [0, 9, 11, 1, 2, 10, 12, 3, 4, 5, 6, 7, 8, 13, 14, 15, 16, 17, 18]
    for i in order:
        loads[i].start()

    modes3[...] = jnp.zeros_like(modes3)
    modes12[...] = jnp.zeros_like(modes12)
    eigen[...] = jnp.zeros_like(eigen)

    for i in (0, 9, 11):
        loads[i].wait()
    pres = pressure[...].reshape(OWN, 128)
    pres_split = split(pres)
    left_split = split(left[...])
    third_split = split(third[...])
    per = N1 * N1
    along = [
        product(left_split, tuple(part[a * per : (a + 1) * per] for part in pres_split))
        for a in range(AB)
    ]
    grad_third = product(pres_split, third_split)
    for i in (1, 2, 10, 12):
        loads[i].wait()
    left_t_split = split(left_t[...])
    third_t_split = split(third_t[...])
    for a in range(AB):
        rows = pl.ds(a * N1, N1)
        d0, d1, d2 = (geo_diag[k, rows].reshape(per, 128) for k in range(3))
        o0, o1, o2 = (geo_off[k, rows].reshape(per, 128) for k in range(3))
        g1, g2 = along[a][:per], along[a][per:]
        g3 = grad_third[a * per : (a + 1) * per]
        flux_first = d0 * g1 + o0 * g2 + o1 * g3
        flux_second = o0 * g1 + d1 * g2 + o2 * g3
        flux_third = o1 * g1 + o2 * g2 + d2 * g3
        both = split(jnp.concatenate([flux_first, flux_second], axis=0))
        own[pl.ds(a * per, per), :] = product(left_t_split, both) + product(
            split(flux_third), third_t_split
        )
    for k, node in enumerate((6, 7, 0, 1)):
        stage[pl.ds(k * NF, NF), :] = own[pl.ds(node, NF, stride=N1), :]

    pl.semaphore_wait(barrier, neighbours)
    first_from = (
        stage.at[pl.ds(0, 48), :],
        stage.at[pl.ds(48, 48), :],
        own.at[pl.ds(OWN - 16, 16), :],
        own.at[pl.ds(0, 16), :],
        own.at[pl.ds(OWN - 16, 16), :],
        own.at[pl.ds(OWN - 16, 16), :],
        own.at[pl.ds(0, 16), :],
        own.at[pl.ds(0, 16), :],
    )
    sends = {}
    for slot, (side_s, side_c) in enumerate(SLOTS):
        sends[slot] = pltpu.make_async_remote_copy(
            src_ref=first_from[slot],
            dst_ref=halo.at[pl.ds(FIRST_AT[slot], FIRST_LEN[slot]), :],
            send_sem=send_sem.at[slot],
            recv_sem=recv_sem.at[slot],
            device_id=peer(-side_s, -side_c),
            device_id_type=MESH,
        )
    for_each(FAR_FIRST, -1, lambda slot: sends[slot].start())

    for i in (3, 4, 5, 6, 7, 8, 13, 14, 15, 16, 17, 18):
        loads[i].wait()
    for m in range(M):
        modes3[m * 16 : m * 16 + CB, 0:M] = modes_third[m]
        modes12[m * 8 : m * 8 + AB, 0:M] = modes_first[m]
        modes12[m * 8 + 3 : m * 8 + 4, 0:M] = modes_second[m]
    eigen[0:AB, 0:M] = eigen_first[...]
    eigen[8:9, 0:M] = eigen_second[...]
    eigen[16 : 16 + CB, 0:M] = eigen_third[...]

    spread = jnp.where(iota((128, WIDE), 0) == (iota((128, WIDE), 1) & 15), 1.0, 0.0).astype(F32)
    diagonal = jnp.dot(modes3[...], spread, precision=HIGHEST, preferred_element_type=F32)
    same = (iota((WIDE, WIDE), 0) & 15) == (iota((WIDE, WIDE), 1) >> 4)
    diagonal = jnp.where(same, diagonal, 0.0)
    fore = tuple(part.astype(BF16) for part in select(gather[...], diagonal))
    back = []
    for part in split(jnp.transpose(diagonal)):
        back.append(dot(part, scatter[...]).astype(BF16))

    take_p = pick_p[...].astype(F32)
    take_q = pick_q[...].astype(F32)
    nt = (((1,), (1,)), ((), ()))
    by_p = lax.dot_general(take_p, modes12[...], nt, precision=HIGHEST, preferred_element_type=F32)
    by_q = lax.dot_general(take_q, modes12[...], nt, precision=HIGHEST, preferred_element_type=F32)
    by_p = jnp.where(block_of(iota((ROWS, 128), 0)) == (iota((ROWS, 128), 1) & 7), by_p, 0.0)
    by_p_split, by_q_split = split(by_p), split(by_q)
    forward = (dot(by_p_split[0], cols_first[...]) + dot(by_p_split[1], cols_first[...])) * (
        dot(by_q_split[0], cols_second[...]) + dot(by_q_split[1], cols_second[...])
    )
    forward_own = forward[:, :OWN]
    forward_halo = forward[:, OWN:]
    own_split = split(forward_own)
    halo_split = split(forward_halo)

    relative = (iota((ROWS, WIDE), 1) >> 3) + 2 - N1 * block_of(iota((ROWS, WIDE), 0))
    keep = jnp.logical_and(relative != 0, relative != 11)
    square = jnp.where(keep, forward[:, :WIDE], 0.0)
    square = jnp.concatenate([square, jnp.zeros((DEEP - ROWS, WIDE), F32)], axis=0)
    kept[...] = jnp.transpose(square)
    back_own = split(kept[pl.ds(0, OWN), :])
    back_edge = split(
        jnp.concatenate(
            [
                kept[pl.ds(0, 8), :],
                kept[pl.ds(OWN - 8, 8), :],
            ],
            axis=0,
        )
    )
    back_far = split(
        jnp.concatenate(
            [kept[pl.ds(7 + 8 * f, 1), :] for f in range(NF)]
            + [kept[pl.ds(8 * f, 1), :] for f in range(NF)],
            axis=0,
        )
    )

    third_eigen = jnp.dot(
        eigen[16 : 16 + CB, :], spread, precision=HIGHEST, preferred_element_type=F32
    )
    third_eigen = jnp.where(
        iota((CB, WIDE), 0) == (iota((CB, WIDE), 1) >> 4), third_eigen, 0.0
    )
    lane_part = jnp.sum(third_eigen, axis=0, keepdims=True)
    inverse = []
    edges = [0, STEP, 2 * STEP, ROWS]
    for a in range(AB):
        rows = slice(edges[a], edges[a + 1])
        row_part = jnp.sum(
            take_p[rows] * eigen[a : a + 1, :] + take_q[rows] * eigen[8:9, :],
            axis=1,
            keepdims=True,
        )
        total = row_part + lane_part
        inverse.append(1.0 / jnp.where(total > 0.0, total, 1.0))
    inverse = jnp.concatenate(inverse, axis=0)

    own_third = product(split(own[...]), fore)
    spectral_own = product(own_split, split(own_third))

    for_each(range(8), 1, lambda slot: sends[slot].wait_recv())
    halo_third = product(split(halo[...]), fore)
    spectral = (spectral_own + product(halo_split, split(halo_third))) * inverse
    spectral = split(
        jnp.concatenate([spectral, jnp.zeros((DEEP - ROWS, WIDE), F32)], axis=0)
    )
    stage_last[pl.ds(0, 48), :] = product(split(product(back_far, spectral)), back)
    edge = product(split(product(back_edge, spectral)), back)
    stage_last[pl.ds(48, 8), :] = edge[8:16]
    stage_last[pl.ds(56, 8), :] = edge[0:8]
    last = {}
    for slot, (side_s, side_c) in enumerate(SLOTS):
        last[slot] = pltpu.make_async_remote_copy(
            src_ref=stage_last.at[pl.ds(LAST_FROM[slot], LAST_LEN[slot]), :],
            dst_ref=halo_last.at[pl.ds(LAST_AT[slot], LAST_LEN[slot]), :],
            send_sem=send_last.at[slot],
            recv_sem=recv_last.at[slot],
            device_id=peer(-side_s, -side_c),
            device_id_type=MESH,
        )
    for_each(FAR_FIRST, -1, lambda slot: last[slot].start())

    sub = iota((8, 128), 0)

    def shifted(tile, to_top):
        moved = pltpu.roll(tile, 1 if to_top else 7, 0)
        return jnp.where(sub == (0 if to_top else 7), moved, 0.0)

    assembled[...] = own[...]
    for node, row in ((0, 24), (7, 48)):
        place = pl.ds(node, NF, stride=N1)
        assembled[place, :] = assembled[place, :] + halo[pl.ds(row, NF), :]

    def layer_beside(slot, at_prev, at_next, side):
        rows = 8 if side < 0 else 0
        base = halo[pl.ds(FIRST_AT[slot] + rows, 8), :]
        base = base + shifted(halo[pl.ds(FIRST_AT[at_prev] + rows, 8), :], True)
        return base + shifted(halo[pl.ds(FIRST_AT[at_next] + rows, 8), :], False)

    assembled[pl.ds(0, 8), :] = assembled[pl.ds(0, 8), :] + layer_beside(2, 4, 5, -1)
    assembled[pl.ds(OWN - 8, 8), :] = assembled[pl.ds(OWN - 8, 8), :] + layer_beside(3, 6, 7, 1)
    for a in range(AB - 1):
        at = (a * N1 + 7) * N1
        total = assembled[pl.ds(at, 8), :] + assembled[pl.ds(at + 8, 8), :]
        assembled[pl.ds(at, 8), :] = total
        assembled[pl.ds(at + 8, 8), :] = total
    value = assembled[...]
    lane = iota((OWN, 128), 1)
    from_left = jnp.where(jnp.logical_and((lane & 7) == 0, lane > 0), pltpu.roll(value, 1, 1), 0.0)
    from_right = jnp.where(
        jnp.logical_and((lane & 7) == 7, lane < 127), pltpu.roll(value, 127, 1), 0.0
    )
    op_ref[...] = (value + from_left + from_right).reshape(NF, N1, 128)

    solved[...] = product(split(product(back_own, spectral)), back)

    for_each(range(8), 1, lambda slot: last[slot].wait_recv())
    for node, row in ((0, 0), (7, 24)):
        place = pl.ds(node, NF, stride=N1)
        solved[place, :] = solved[place, :] + halo_last[pl.ds(row, NF), :]

    def layer_last(slot, at_prev, at_next):
        base = halo_last[pl.ds(LAST_AT[slot], 8), :]
        base = base + shifted(halo_last[pl.ds(LAST_AT[at_prev], 8), :], True)
        return base + shifted(halo_last[pl.ds(LAST_AT[at_next], 8), :], False)

    solved[pl.ds(0, 8), :] = solved[pl.ds(0, 8), :] + layer_last(2, 4, 5)
    solved[pl.ds(OWN - 8, 8), :] = solved[pl.ds(OWN - 8, 8), :] + layer_last(3, 6, 7)
    pre_ref[...] = solved[...].reshape(NF, N1, 128)

    for_each(range(8), -1, lambda slot: sends[slot].wait_send())
    for_each(range(8), -1, lambda slot: last[slot].wait_send())


def shards(*args):
    operands = list(args) + [jnp.asarray(t) for t in tables()]
    for i in (3, 4, 5):
        operands[i] = jnp.transpose(operands[i], (1, 0, 2))
    out = jax.ShapeDtypeStruct((NF, N1, CB * N1), F32)
    return pl.pallas_call(
        kernel,
        out_shape=(out, out),
        in_specs=[pl.BlockSpec(memory_space=pl.ANY)] * len(operands),
        out_specs=(pl.BlockSpec(memory_space=pltpu.VMEM),) * 2,
        scratch_shapes=[pltpu.VMEM(t.shape, t.dtype) for t in operands]
        + [
            pltpu.VMEM((OWN, 128), F32),
            pltpu.VMEM((96, 128), F32),
            pltpu.VMEM((HALO, 128), F32),
            pltpu.VMEM((64, 128), F32),
            pltpu.VMEM((96, 128), F32),
            pltpu.VMEM((OWN, 128), F32),
            pltpu.VMEM((OWN, 128), F32),
            pltpu.VMEM((WIDE, DEEP), F32),
            pltpu.VMEM((WIDE, 128), F32),
            pltpu.VMEM((128, 128), F32),
            pltpu.VMEM((32, 128), F32),
            pltpu.SemaphoreType.DMA((19,)),
            pltpu.SemaphoreType.DMA((8,)),
            pltpu.SemaphoreType.DMA((8,)),
            pltpu.SemaphoreType.DMA((8,)),
            pltpu.SemaphoreType.DMA((8,)),
        ],
        compiler_params=pltpu.CompilerParams(collective_id=0, has_side_effects=True),
        name="pressure_step",
    )(*operands)


def solution(mesh):
    in_specs = (
        P("stream", "cross", None),
        P(None, "stream", "cross", None),
        P(None, "stream", "cross", None),
        P("stream", None, None),
        P("cross", None, None),
        P(),
        P("stream", None),
        P("cross", None),
        P(),
    )
    out_specs = (P("stream", "cross", None), P("stream", "cross", None))
    return jax.shard_map(shards, mesh=mesh, in_specs=in_specs, out_specs=out_specs, check_vma=False)
```

```python
import functools

import jax
import jax.numpy as jnp
import numpy as np
from jax import lax
from jax.experimental import pallas as pl
from jax.experimental.pallas import tpu as pltpu
from jax.sharding import PartitionSpec as P

N1 = 8
M = 10
AB = 3
CB = 16
NF = AB * N1
OWN = NF * N1
HALO = 192
COLS = OWN + HALO
STEP = 104
ROWS = 320
DEEP = 384
WIDE = 256
F32 = jnp.float32
BF16 = jnp.bfloat16
MESH = pl.DeviceIdType.MESH
N_IN = 17

SLOTS = ((0, -1), (0, 1), (-1, 0), (1, 0), (-1, -1), (-1, 1), (1, -1), (1, 1))
FIRST_AT = (0, 48, 96, 112, 128, 144, 160, 176)
FIRST_LEN = (48, 48, 16, 16, 16, 16, 16, 16)
LAST_AT = (0, 24, 48, 56, 64, 72, 80, 88)
LAST_LEN = (24, 24, 8, 8, 8, 8, 8, 8)
LAST_FROM = (0, 24, 48, 56, 48, 48, 56, 56)
FAR_FIRST = (4, 5, 6, 7, 0, 1, 2, 3)


def legendre_values(nodes, degree):
    table = np.zeros((nodes.shape[0], degree + 1))
    table[:, 0] = 1.0
    table[:, 1] = nodes
    for order in range(2, degree + 1):
        table[:, order] = (
            (2 * order - 1) * nodes * table[:, order - 1] - (order - 1) * table[:, order - 2]
        ) / order
    return table


def derivative_table(points):
    degree = points - 1
    nodes = np.cos(np.pi * np.arange(points) / degree)
    for sweep in range(100):
        table = legendre_values(nodes, degree)
        nodes = nodes - (nodes * table[:, degree] - table[:, degree - 1]) / (
            points * table[:, degree]
        )
    gll_nodes = nodes[::-1]
    legendre_at = legendre_values(gll_nodes, degree)[:, degree]
    diff_table = np.zeros((points, points))
    for first_index in range(points):
        for second_index in range(points):
            if first_index != second_index:
                diff_table[first_index, second_index] = legendre_at[first_index] / (
                    legendre_at[second_index] * (gll_nodes[first_index] - gll_nodes[second_index])
                )
    diff_table[0, 0] = -degree * (degree + 1) / 4.0
    diff_table[degree, degree] = degree * (degree + 1) / 4.0
    return diff_table


LAYER_NODE = [0, 1, 1, 2, 3, 4, 5, 6, 7, 8, 8, 9]


def halves(table):
    high = table.astype(BF16)
    return high, (table - high.astype(np.float32)).astype(BF16)


def tables():
    diff = derivative_table(N1).astype(np.float32)
    eye8 = np.eye(N1, dtype=np.float32)
    left = np.concatenate([np.kron(diff, eye8), np.kron(eye8, diff)], axis=0)
    high, low = halves(left)
    left_all = np.concatenate([high, high, low], axis=1)
    left_t = np.concatenate([high.T, low.T], axis=1)
    zero = np.zeros((CB * N1, CB * N1), BF16)
    thirds = []
    for matrix in (diff.T, diff):
        high, low = halves(np.kron(np.eye(CB, dtype=np.float32), matrix))
        thirds.append(np.block([[high, low], [high, zero]]))
    gather = np.zeros((CB * N1, CB * M), np.float32)
    for c in range(CB):
        for layer in range(12):
            at = c * N1 + layer - 2
            if 0 <= at < CB * N1:
                gather[at, LAYER_NODE[layer] * CB + c] = 1.0
    pick = np.zeros((ROWS, 128), np.float32)
    for a in range(AB):
        for p in range(M):
            for q in range(M):
                pick[a * STEP + p * M + q, p] = 1.0
                pick[a * STEP + p * M + q, 64 + q] = 1.0
    first_layer = np.zeros(COLS, np.int32)
    second_layer = np.full(COLS, -1, np.int32)
    for f in range(NF):
        for j in range(N1):
            first_layer[f * N1 + j] = f + 2
            second_layer[f * N1 + j] = j + 2
    for slot, (side_s, side_c) in enumerate(SLOTS):
        for row in range(FIRST_LEN[slot]):
            col = OWN + FIRST_AT[slot] + row
            if side_s == 0:
                jj, f = divmod(row, NF)
                first_layer[col] = f + 2
                second_layer[col] = jj if side_c < 0 else 10 + jj
            else:
                l, j = divmod(row, N1)
                first_layer[col] = l if side_s < 0 else 26 + l
                if side_c == 0:
                    second_layer[col] = j + 2
                elif side_c < 0:
                    second_layer[col] = j - 6 if j >= 6 else -1
                else:
                    second_layer[col] = 10 + j if j < 2 else -1
    cols_first = np.zeros((128, COLS), np.float32)
    cols_second = np.zeros((128, COLS), np.float32)
    for col in range(COLS):
        for a in range(AB):
            layer = first_layer[col] - N1 * a
            if 0 <= layer < 12:
                cols_first[LAYER_NODE[layer] * 8 + a, col] = 1.0
        if second_layer[col] >= 0:
            cols_second[LAYER_NODE[second_layer[col]] * 8 + 3, col] = 1.0
    exact = [t.astype(BF16) for t in (gather, pick, cols_first, cols_second)]
    return [left_all, left_t] + thirds + exact


def dot(a, b):
    return lax.dot_general(a, b, (((1,), (0,)), ((), ())), preferred_element_type=F32)


def split(value):
    high = value.astype(BF16)
    return high, (value - high.astype(F32)).astype(BF16)


def product(a, b):
    return dot(a[0], b[0]) + (dot(a[1], b[0]) + dot(a[0], b[1]))


def lane_product(a, table):
    both = dot(jnp.concatenate(a, axis=1), table)
    return both[:, :128] + both[:, 128:]


def wide_product(a, b):
    return dot(jnp.concatenate(a, axis=1), jnp.concatenate([b[0], b[0]], axis=0)) + dot(a[0], b[1])


def product_nt(a, b):
    def one(x, y):
        return lax.dot_general(x, y, (((1,), (1,)), ((), ())), preferred_element_type=F32)

    return one(a[0], b[0]) + (one(a[1], b[0]) + one(a[0], b[1]))


def iota(shape, dimension):
    return lax.broadcasted_iota(jnp.int32, shape, dimension)


def block_of(rows):
    return (rows >= STEP).astype(jnp.int32) + (rows >= 2 * STEP).astype(jnp.int32)


def kernel(*refs):
    hbm = refs[:N_IN]
    op_ref, pre_ref = refs[N_IN : N_IN + 2]
    vmem = refs[N_IN + 2 : 2 * N_IN + 2]
    (
        own,
        stage,
        halo,
        stage_last,
        halo_last,
        assembled,
        solved,
        kept,
        modes3,
        modes12,
        eigen,
        load_sem,
        send_sem,
        recv_sem,
        send_last,
        recv_last,
    ) = refs[2 * N_IN + 2 :]
    (
        pressure,
        geo_diag,
        geo_off,
        modes_first,
        modes_second,
        modes_third,
        eigen_first,
        eigen_second,
        eigen_third,
        left,
        left_t,
        third,
        third_t,
        gather,
        pick,
        cols_first,
        cols_second,
    ) = vmem
    n_s, n_c = lax.axis_size("stream"), lax.axis_size("cross")
    me_s, me_c = lax.axis_index("stream"), lax.axis_index("cross")

    def peer(side_s, side_c):
        return {
            "stream": lax.rem(me_s + side_s + n_s, n_s),
            "cross": lax.rem(me_c + side_c + n_c, n_c),
        }

    at_s = {-1: me_s > 0, 0: True, 1: me_s < n_s - 1}
    at_c = {-1: me_c > 0, 0: True, 1: me_c < n_c - 1}

    def there(side_s, side_c):
        if side_s == 0:
            return at_c[side_c]
        if side_c == 0:
            return at_s[side_s]
        return jnp.logical_and(at_s[side_s], at_c[side_c])

    def for_each(order, sign, act):
        for slot in order:
            side_s, side_c = SLOTS[slot]
            pl.when(there(sign * side_s, sign * side_c))(functools.partial(act, slot))

    halo[...] = jnp.zeros_like(halo)
    halo_last[...] = jnp.zeros_like(halo_last)
    barrier = pltpu.get_barrier_semaphore()

    def greet(slot):
        pl.semaphore_signal(barrier, inc=1, device_id=peer(*SLOTS[slot]), device_id_type=MESH)

    for_each(range(8), 1, greet)
    count_s = at_s[-1].astype(jnp.int32) + at_s[1].astype(jnp.int32)
    count_c = at_c[-1].astype(jnp.int32) + at_c[1].astype(jnp.int32)
    neighbours = count_s + count_c + count_s * count_c
    loads = [
        pltpu.make_async_copy(hbm[i], vmem[i], load_sem.at[i]) for i in range(N_IN)
    ]
    order = [0, 9, 11, 1, 2, 10, 12, 5, 13, 3, 4, 14, 15, 16, 6, 7, 8]
    for i in order:
        loads[i].start()

    modes3[...] = jnp.zeros_like(modes3)
    modes12[...] = jnp.zeros_like(modes12)
    eigen[...] = jnp.zeros_like(eigen)

    for i in (0, 9, 11):
        loads[i].wait()
    pres = split(pressure[...].reshape(OWN, 128))
    per = N1 * N1
    along = []
    for a in range(AB):
        high, low = (part[a * per : (a + 1) * per] for part in pres)
        along.append(dot(left[...], jnp.concatenate([high, low, high], axis=0)))
    grad_third = lane_product(pres, third[...])
    for i in (1, 2, 10, 12):
        loads[i].wait()
    for a in range(AB):
        rows = pl.ds(a * N1, N1)
        d0, d1, d2 = (geo_diag[k, rows].reshape(per, 128) for k in range(3))
        o0, o1, o2 = (geo_off[k, rows].reshape(per, 128) for k in range(3))
        g1, g2 = along[a][:per], along[a][per:]
        g3 = grad_third[a * per : (a + 1) * per]
        flux_first = d0 * g1 + o0 * g2 + o1 * g3
        flux_second = o0 * g1 + d1 * g2 + o2 * g3
        flux_third = o1 * g1 + o2 * g2 + d2 * g3
        high, low = split(jnp.concatenate([flux_first, flux_second], axis=0))
        own[pl.ds(a * per, per), :] = (
            dot(left_t[...], jnp.concatenate([high, high], axis=0))
            + dot(left_t[:, :128], low)
            + lane_product(split(flux_third), third_t[...])
        )
    for k, node in enumerate((6, 7, 0, 1)):
        stage[pl.ds(k * NF, NF), :] = own[pl.ds(node, NF, stride=N1), :]

    pl.semaphore_wait(barrier, neighbours)
    first_from = (
        stage.at[pl.ds(0, 48), :],
        stage.at[pl.ds(48, 48), :],
        own.at[pl.ds(OWN - 16, 16), :],
        own.at[pl.ds(0, 16), :],
        own.at[pl.ds(OWN - 16, 16), :],
        own.at[pl.ds(OWN - 16, 16), :],
        own.at[pl.ds(0, 16), :],
        own.at[pl.ds(0, 16), :],
    )
    sends = {}
    for slot, (side_s, side_c) in enumerate(SLOTS):
        sends[slot] = pltpu.make_async_remote_copy(
            src_ref=first_from[slot],
            dst_ref=halo.at[pl.ds(FIRST_AT[slot], FIRST_LEN[slot]), :],
            send_sem=send_sem.at[slot],
            recv_sem=recv_sem.at[slot],
            device_id=peer(-side_s, -side_c),
            device_id_type=MESH,
        )
    for_each(FAR_FIRST, -1, lambda slot: sends[slot].start())

    for i in order[7:]:
        loads[i].wait()
    for m in range(M):
        modes3[m * 16 : m * 16 + CB, 0:M] = modes_third[m]
        modes12[m * 8 : m * 8 + AB, 0:M] = modes_first[m]
        modes12[m * 8 + 3 : m * 8 + 4, 64 : 64 + M] = modes_second[m]
    for a in range(AB):
        eigen[a : a + 1, 0:M] = eigen_first[a : a + 1, :]
        eigen[a : a + 1, 64 : 64 + M] = eigen_second[...]
    eigen[8 : 8 + CB, 0:M] = eigen_third[...]

    spread = (iota((128, WIDE), 0) == (iota((128, WIDE), 1) & 15)).astype(F32).astype(BF16)
    same = (iota((CB * M, WIDE), 0) & 15) == (iota((CB * M, WIDE), 1) >> 4)
    fore = []
    back = []
    node, box = iota((128, WIDE), 0), iota((128, WIDE), 1) >> 4
    stays = jnp.logical_or(
        (node >> 3) == box, jnp.logical_or((node & 7) == 0, (node & 7) == 7)
    )
    for part in split(modes3[...]):
        diagonal = jnp.where(same, dot(part, spread), 0.0).astype(BF16)
        moved = dot(gather[...], diagonal)
        fore.append(moved.astype(BF16))
        back.append(jnp.where(stays, moved, 0.0).astype(BF16))

    both = jnp.concatenate(split(modes12[...]), axis=0)
    picked = lax.dot_general(
        pick[...], both, (((1,), (1,)), ((), ())), preferred_element_type=F32
    )
    at_block = block_of(iota((ROWS, WIDE), 0)) == (iota((ROWS, WIDE), 1) & 7)
    by_p = jnp.where(at_block, picked, 0.0).astype(BF16)
    by_q = picked.astype(BF16)
    forward = dot(by_p, jnp.concatenate([cols_first[...]] * 2, axis=0)) * dot(
        by_q, jnp.concatenate([cols_second[...]] * 2, axis=0)
    )
    own_split = split(forward[:, :OWN])
    halo_split = split(forward[:, OWN:])

    relative = (iota((ROWS, WIDE), 1) >> 3) + 2 - N1 * block_of(iota((ROWS, WIDE), 0))
    keep = jnp.logical_and(relative != 0, relative != 11)
    square = jnp.where(keep, forward[:, :WIDE], 0.0)
    square = jnp.concatenate([square, jnp.zeros((DEEP - ROWS, WIDE), F32)], axis=0)
    turned = jnp.transpose(square)
    for k in range(3):
        kept[k] = turned[:, k * 128 : (k + 1) * 128]

    def kept_rows(rows):
        return jnp.concatenate([kept[k, rows, :] for k in range(3)], axis=1)

    back_own = split(kept_rows(pl.ds(0, OWN)))
    back_edge = split(
        jnp.concatenate(
            [
                kept_rows(pl.ds(7, NF, stride=N1)),
                kept_rows(pl.ds(0, NF, stride=N1)),
                kept_rows(pl.ds(OWN - 8, 8)),
                kept_rows(pl.ds(0, 8)),
            ],
            axis=0,
        )
    )

    third_eigen = eigen[8 : 8 + CB, :]
    for shift in (16, 32, 64):
        third_eigen = third_eigen + pltpu.roll(third_eigen, shift, 1)
    third_eigen = jnp.concatenate([third_eigen, third_eigen], axis=1)
    own_box = iota((CB, WIDE), 0) == (iota((CB, WIDE), 1) >> 4)
    lane_part = jnp.sum(jnp.where(own_box, third_eigen, 0.0), axis=0, keepdims=True)
    inverse = []
    edges = [0, STEP, 2 * STEP, ROWS]
    for a in range(AB):
        rows = slice(edges[a], edges[a + 1])
        row_part = jnp.sum(
            pick[...].astype(F32)[rows] * eigen[a : a + 1, :], axis=1, keepdims=True
        )
        total = row_part + lane_part
        inverse.append(1.0 / jnp.where(total > 0.0, total, 1.0))
    inverse = jnp.concatenate(inverse, axis=0)

    own_third = wide_product(split(own[...]), fore)
    spectral_own = product(own_split, split(own_third))

    for_each(range(8), 1, lambda slot: sends[slot].wait_recv())
    halo_third = wide_product(split(halo[...]), fore)
    spectral = (spectral_own + product(halo_split, split(halo_third))) * inverse
    spectral = split(
        jnp.concatenate([spectral, jnp.zeros((DEEP - ROWS, WIDE), F32)], axis=0)
    )
    stage_last[...] = product_nt(split(product(back_edge, spectral)), back)
    last = {}
    for slot, (side_s, side_c) in enumerate(SLOTS):
        last[slot] = pltpu.make_async_remote_copy(
            src_ref=stage_last.at[pl.ds(LAST_FROM[slot], LAST_LEN[slot]), :],
            dst_ref=halo_last.at[pl.ds(LAST_AT[slot], LAST_LEN[slot]), :],
            send_sem=send_last.at[slot],
            recv_sem=recv_last.at[slot],
            device_id=peer(-side_s, -side_c),
            device_id_type=MESH,
        )
    for_each(FAR_FIRST, -1, lambda slot: last[slot].start())

    sub = iota((8, 128), 0)

    def shifted(tile, to_top):
        moved = pltpu.roll(tile, 1 if to_top else 7, 0)
        return jnp.where(sub == (0 if to_top else 7), moved, 0.0)

    assembled[...] = own[...]
    for node, row in ((0, 24), (7, 48)):
        place = pl.ds(node, NF, stride=N1)
        assembled[place, :] = assembled[place, :] + halo[pl.ds(row, NF), :]

    def layer_beside(slot, at_prev, at_next, side):
        rows = 8 if side < 0 else 0
        base = halo[pl.ds(FIRST_AT[slot] + rows, 8), :]
        base = base + shifted(halo[pl.ds(FIRST_AT[at_prev] + rows, 8), :], True)
        return base + shifted(halo[pl.ds(FIRST_AT[at_next] + rows, 8), :], False)

    assembled[pl.ds(0, 8), :] = assembled[pl.ds(0, 8), :] + layer_beside(2, 4, 5, -1)
    assembled[pl.ds(OWN - 8, 8), :] = assembled[pl.ds(OWN - 8, 8), :] + layer_beside(3, 6, 7, 1)
    for a in range(AB - 1):
        at = (a * N1 + 7) * N1
        total = assembled[pl.ds(at, 8), :] + assembled[pl.ds(at + 8, 8), :]
        assembled[pl.ds(at, 8), :] = total
        assembled[pl.ds(at + 8, 8), :] = total
    value = assembled[...]
    lane = iota((OWN, 128), 1)
    from_left = jnp.where(jnp.logical_and((lane & 7) == 0, lane > 0), pltpu.roll(value, 1, 1), 0.0)
    from_right = jnp.where(
        jnp.logical_and((lane & 7) == 7, lane < 127), pltpu.roll(value, 127, 1), 0.0
    )
    op_ref[...] = (value + from_left + from_right).reshape(NF, N1, 128)

    solved[...] = product_nt(split(product(back_own, spectral)), back)

    for_each(range(8), 1, lambda slot: last[slot].wait_recv())
    for node, row in ((0, 0), (7, 24)):
        place = pl.ds(node, NF, stride=N1)
        solved[place, :] = solved[place, :] + halo_last[pl.ds(row, NF), :]

    def layer_last(slot, at_prev, at_next):
        base = halo_last[pl.ds(LAST_AT[slot], 8), :]
        base = base + shifted(halo_last[pl.ds(LAST_AT[at_prev], 8), :], True)
        return base + shifted(halo_last[pl.ds(LAST_AT[at_next], 8), :], False)

    solved[pl.ds(0, 8), :] = solved[pl.ds(0, 8), :] + layer_last(2, 4, 5)
    solved[pl.ds(OWN - 8, 8), :] = solved[pl.ds(OWN - 8, 8), :] + layer_last(3, 6, 7)
    pre_ref[...] = solved[...].reshape(NF, N1, 128)

    for_each(range(8), -1, lambda slot: sends[slot].wait_send())
    for_each(range(8), -1, lambda slot: last[slot].wait_send())


def write_out(op_in, pre_in, op_out, pre_out, sem):
    copies = [
        pltpu.make_async_copy(source, target, sem.at[i])
        for i, (source, target) in enumerate(((op_in, op_out), (pre_in, pre_out)))
    ]
    for copy in copies:
        copy.start()
    for copy in copies:
        copy.wait()


def shards(*args):
    operands = list(args) + [jnp.asarray(t) for t in tables()]
    for i in (3, 4, 5):
        operands[i] = jnp.transpose(operands[i], (1, 0, 2))
    out = pltpu.VMEM((NF, N1, CB * N1), F32)
    held = pl.pallas_call(
        kernel,
        out_shape=(out, out),
        in_specs=[pl.BlockSpec(memory_space=pl.ANY)] * len(operands),
        out_specs=(pl.BlockSpec(memory_space=pltpu.VMEM),) * 2,
        scratch_shapes=[pltpu.VMEM(t.shape, t.dtype) for t in operands]
        + [
            pltpu.VMEM((OWN, 128), F32),
            pltpu.VMEM((96, 128), F32),
            pltpu.VMEM((HALO, 128), F32),
            pltpu.VMEM((64, 128), F32),
            pltpu.VMEM((96, 128), F32),
            pltpu.VMEM((OWN, 128), F32),
            pltpu.VMEM((OWN, 128), F32),
            pltpu.VMEM((3, WIDE, 128), F32),
            pltpu.VMEM((CB * M, 128), F32),
            pltpu.VMEM((128, 128), F32),
            pltpu.VMEM((32, 128), F32),
            pltpu.SemaphoreType.DMA((N_IN,)),
            pltpu.SemaphoreType.DMA((8,)),
            pltpu.SemaphoreType.DMA((8,)),
            pltpu.SemaphoreType.DMA((8,)),
            pltpu.SemaphoreType.DMA((8,)),
        ],
        compiler_params=pltpu.CompilerParams(collective_id=0, has_side_effects=True),
        name="pressure_step",
    )(*operands)
    held = [pltpu.with_memory_space_constraint(value, pltpu.VMEM) for value in held]
    out = jax.ShapeDtypeStruct((NF, N1, CB * N1), F32)
    return pl.pallas_call(
        write_out,
        out_shape=(out, out),
        in_specs=[pl.BlockSpec(memory_space=pltpu.VMEM)] * 2,
        out_specs=(pl.BlockSpec(memory_space=pl.ANY),) * 2,
        scratch_shapes=[pltpu.SemaphoreType.DMA((2,))],
        name="write_out",
    )(*held)


def solution(mesh):
    in_specs = (
        P("stream", "cross", None),
        P(None, "stream", "cross", None),
        P(None, "stream", "cross", None),
        P("stream", None, None),
        P("cross", None, None),
        P(),
        P("stream", None),
        P("cross", None),
        P(),
    )
    out_specs = (P("stream", "cross", None), P("stream", "cross", None))
    return jax.shard_map(shards, mesh=mesh, in_specs=in_specs, out_specs=out_specs, check_vma=False)
```

```python
import functools

import jax
import jax.numpy as jnp
import numpy as np
from jax import lax
from jax.experimental import pallas as pl
from jax.experimental.pallas import tpu as pltpu
from jax.sharding import PartitionSpec as P

N1 = 8
M = 10
AB = 3
CB = 16
NF = AB * N1
OWN = NF * N1
HALO = 192
COLS = OWN + HALO
STEP = 104
ROWS = 320
DEEP = 384
WIDE = 256
F32 = jnp.float32
BF16 = jnp.bfloat16
MESH = pl.DeviceIdType.MESH
N_IN = 17
RUN = 8
BEHIND = (1, 5, 7)
RELAY_LEN = 80

SLOTS = ((0, -1), (0, 1), (-1, 0), (1, 0), (-1, -1), (-1, 1), (1, -1), (1, 1))
FIRST_AT = (0, 48, 128, 144, 160, 96, 176, 112)
FIRST_LEN = (48, 48, 16, 16, 16, 16, 16, 16)
LAST_AT = (0, 24, 48, 56, 64, 72, 80, 88)
LAST_LEN = (24, 24, 8, 8, 8, 8, 8, 8)
LAST_FROM = (0, 24, 48, 56, 48, 48, 56, 56)
FAR_FIRST = (4, 5, 6, 7, 0, 1, 2, 3)


def legendre_values(nodes, degree):
    table = np.zeros((nodes.shape[0], degree + 1))
    table[:, 0] = 1.0
    table[:, 1] = nodes
    for order in range(2, degree + 1):
        table[:, order] = (
            (2 * order - 1) * nodes * table[:, order - 1] - (order - 1) * table[:, order - 2]
        ) / order
    return table


def derivative_table(points):
    degree = points - 1
    nodes = np.cos(np.pi * np.arange(points) / degree)
    for sweep in range(100):
        table = legendre_values(nodes, degree)
        nodes = nodes - (nodes * table[:, degree] - table[:, degree - 1]) / (
            points * table[:, degree]
        )
    gll_nodes = nodes[::-1]
    legendre_at = legendre_values(gll_nodes, degree)[:, degree]
    diff_table = np.zeros((points, points))
    for first_index in range(points):
        for second_index in range(points):
            if first_index != second_index:
                diff_table[first_index, second_index] = legendre_at[first_index] / (
                    legendre_at[second_index] * (gll_nodes[first_index] - gll_nodes[second_index])
                )
    diff_table[0, 0] = -degree * (degree + 1) / 4.0
    diff_table[degree, degree] = degree * (degree + 1) / 4.0
    return diff_table


LAYER_NODE = [0, 1, 1, 2, 3, 4, 5, 6, 7, 8, 8, 9]


def halves(table):
    high = table.astype(BF16)
    return high, (table - high.astype(np.float32)).astype(BF16)


def tables():
    diff = derivative_table(N1).astype(np.float32)
    eye8 = np.eye(N1, dtype=np.float32)
    left = np.concatenate([np.kron(diff, eye8), np.kron(eye8, diff)], axis=0)
    high, low = halves(left)
    left_all = np.concatenate([high, high, low], axis=1)
    left_t = np.concatenate([high.T, low.T], axis=1)
    zero = np.zeros((CB * N1, CB * N1), BF16)
    thirds = []
    for matrix in (diff.T, diff):
        high, low = halves(np.kron(np.eye(CB, dtype=np.float32), matrix))
        thirds.append(np.block([[high, low], [high, zero]]))
    gather = np.zeros((CB * N1, CB * M), np.float32)
    for c in range(CB):
        for layer in range(12):
            at = c * N1 + layer - 2
            if 0 <= at < CB * N1:
                gather[at, LAYER_NODE[layer] * CB + c] = 1.0
    pick = np.zeros((ROWS, 128), np.float32)
    for a in range(AB):
        for p in range(M):
            for q in range(M):
                pick[a * STEP + p * M + q, p] = 1.0
                pick[a * STEP + p * M + q, 64 + q] = 1.0
    first_layer = np.zeros(COLS, np.int32)
    second_layer = np.full(COLS, -1, np.int32)
    for f in range(NF):
        for j in range(N1):
            first_layer[f * N1 + j] = f + 2
            second_layer[f * N1 + j] = j + 2
    for slot, (side_s, side_c) in enumerate(SLOTS):
        for row in range(FIRST_LEN[slot]):
            col = OWN + FIRST_AT[slot] + row
            if side_s == 0:
                jj, f = divmod(row, NF)
                first_layer[col] = f + 2
                second_layer[col] = jj if side_c < 0 else 10 + jj
            else:
                l, j = divmod(row, N1)
                first_layer[col] = l if side_s < 0 else 26 + l
                if side_c == 0:
                    second_layer[col] = j + 2
                elif side_c < 0:
                    second_layer[col] = j - 6 if j >= 6 else -1
                else:
                    second_layer[col] = 10 + j if j < 2 else -1
    cols_first = np.zeros((128, COLS), np.float32)
    cols_second = np.zeros((128, COLS), np.float32)
    for col in range(COLS):
        for a in range(AB):
            layer = first_layer[col] - N1 * a
            if 0 <= layer < 12:
                cols_first[LAYER_NODE[layer] * 8 + a, col] = 1.0
        if second_layer[col] >= 0:
            cols_second[LAYER_NODE[second_layer[col]] * 8 + 3, col] = 1.0
    exact = [t.astype(BF16) for t in (gather, pick, cols_first, cols_second)]
    return [left_all, left_t] + thirds + exact


def dot(a, b):
    return lax.dot_general(a, b, (((1,), (0,)), ((), ())), preferred_element_type=F32)


def split(value):
    high = value.astype(BF16)
    return high, (value - high.astype(F32)).astype(BF16)


def product(a, b):
    return dot(a[0], b[0]) + (dot(a[1], b[0]) + dot(a[0], b[1]))


def lane_product(a, table):
    both = dot(jnp.concatenate(a, axis=1), table)
    return both[:, :128] + both[:, 128:]


def wide_product(a, b):
    return dot(jnp.concatenate(a, axis=1), jnp.concatenate([b[0], b[0]], axis=0)) + dot(a[0], b[1])


def product_nt(a, b):
    def one(x, y):
        return lax.dot_general(x, y, (((1,), (1,)), ((), ())), preferred_element_type=F32)

    return one(a[0], b[0]) + (one(a[1], b[0]) + one(a[0], b[1]))


def iota(shape, dimension):
    return lax.broadcasted_iota(jnp.int32, shape, dimension)


def block_of(rows):
    return (rows >= STEP).astype(jnp.int32) + (rows >= 2 * STEP).astype(jnp.int32)


def kernel(*refs):
    hbm = refs[:N_IN]
    op_ref, pre_ref = refs[N_IN : N_IN + 2]
    vmem = refs[N_IN + 2 : 2 * N_IN + 2]
    (
        own,
        stage,
        halo,
        stage_last,
        halo_last,
        assembled,
        solved,
        kept,
        modes3,
        modes12,
        eigen,
        load_sem,
        send_sem,
        recv_sem,
        send_last,
        recv_last,
        relay,
        relay_sem,
        forward_sem,
    ) = refs[2 * N_IN + 2 :]
    (
        pressure,
        geo_diag,
        geo_off,
        modes_first,
        modes_second,
        modes_third,
        eigen_first,
        eigen_second,
        eigen_third,
        left,
        left_t,
        third,
        third_t,
        gather,
        pick,
        cols_first,
        cols_second,
    ) = vmem
    n_s, n_c = lax.axis_size("stream"), lax.axis_size("cross")
    me_s, me_c = lax.axis_index("stream"), lax.axis_index("cross")

    def peer(side_s, side_c):
        return {
            "stream": lax.rem(me_s + side_s + n_s, n_s),
            "cross": lax.rem(me_c + side_c + n_c, n_c),
        }

    at_s = {-1: me_s > 0, 0: True, 1: me_s < n_s - 1}
    at_c = {-1: me_c > 0, 0: True, 1: me_c < n_c - 1}

    is_last = jnp.logical_and(lax.rem(me_c, RUN) == RUN - 1, me_c < n_c - 1)
    is_start = jnp.logical_and(lax.rem(me_c, RUN) == 0, me_c > 0)
    is_relay = jnp.logical_and(lax.rem(me_c, RUN) == 1, me_c + RUN - 1 < n_c)

    def both(first, second):
        return second if first is True else jnp.logical_and(first, second)

    def there(side_s, side_c):
        if side_s == 0:
            return at_c[side_c]
        if side_c == 0:
            return at_s[side_s]
        return jnp.logical_and(at_s[side_s], at_c[side_c])

    def for_each(order, sign, act):
        for slot in order:
            side_s, side_c = SLOTS[slot]
            pl.when(there(sign * side_s, sign * side_c))(functools.partial(act, slot))

    def to_relay(act):
        for slot in BEHIND:
            pl.when(both(at_s[-SLOTS[slot][0]], is_start))(functools.partial(act, slot))

    def at_relay(act):
        for slot in BEHIND:
            pl.when(both(at_s[SLOTS[slot][0]], is_relay))(functools.partial(act, slot))

    halo[...] = jnp.zeros_like(halo)
    halo_last[...] = jnp.zeros_like(halo_last)
    relay[...] = jnp.zeros_like(relay)
    barrier = pltpu.get_barrier_semaphore()

    def greet(side_s, side_c):
        pl.semaphore_signal(barrier, inc=1, device_id=peer(side_s, side_c), device_id_type=MESH)

    pl.when(is_last)(functools.partial(greet, 0, 2 - RUN))
    for side_s, side_c in SLOTS:
        here = there(side_s, side_c)
        if side_c > 0:
            here = jnp.logical_and(here, jnp.logical_not(is_last))
        pl.when(here)(functools.partial(greet, side_s, side_c))
    at_relay(lambda slot: greet(SLOTS[slot][0], RUN - 1))
    count_s = at_s[-1].astype(jnp.int32) + at_s[1].astype(jnp.int32)
    count_c = at_c[-1].astype(jnp.int32) + at_c[1].astype(jnp.int32)
    neighbours = count_s + count_c + count_s * count_c + is_relay.astype(jnp.int32)
    loads = [
        pltpu.make_async_copy(hbm[i], vmem[i], load_sem.at[i]) for i in range(N_IN)
    ]
    order = [0, 9, 11, 1, 2, 10, 12, 5, 13, 3, 4, 14, 15, 16, 6, 7, 8]
    for i in order:
        loads[i].start()

    modes3[...] = jnp.zeros_like(modes3)
    modes12[...] = jnp.zeros_like(modes12)
    eigen[...] = jnp.zeros_like(eigen)

    for i in (0, 9, 11):
        loads[i].wait()
    pres = split(pressure[...].reshape(OWN, 128))
    per = N1 * N1
    along = []
    for a in range(AB):
        high, low = (part[a * per : (a + 1) * per] for part in pres)
        along.append(dot(left[...], jnp.concatenate([high, low, high], axis=0)))
    grad_third = lane_product(pres, third[...])
    for i in (1, 2, 10, 12):
        loads[i].wait()
    for a in range(AB):
        rows = pl.ds(a * N1, N1)
        d0, d1, d2 = (geo_diag[k, rows].reshape(per, 128) for k in range(3))
        o0, o1, o2 = (geo_off[k, rows].reshape(per, 128) for k in range(3))
        g1, g2 = along[a][:per], along[a][per:]
        g3 = grad_third[a * per : (a + 1) * per]
        flux_first = d0 * g1 + o0 * g2 + o1 * g3
        flux_second = o0 * g1 + d1 * g2 + o2 * g3
        flux_third = o1 * g1 + o2 * g2 + d2 * g3
        high, low = split(jnp.concatenate([flux_first, flux_second], axis=0))
        own[pl.ds(a * per, per), :] = (
            dot(left_t[...], jnp.concatenate([high, high], axis=0))
            + dot(left_t[:, :128], low)
            + lane_product(split(flux_third), third_t[...])
        )
    for k, node in enumerate((6, 7, 0, 1)):
        stage[pl.ds(k * NF, NF), :] = own[pl.ds(node, NF, stride=N1), :]

    pl.semaphore_wait(barrier, neighbours)
    first_from = (
        stage.at[pl.ds(0, 48), :],
        stage.at[pl.ds(48, 48), :],
        own.at[pl.ds(OWN - 16, 16), :],
        own.at[pl.ds(0, 16), :],
        own.at[pl.ds(OWN - 16, 16), :],
        own.at[pl.ds(OWN - 16, 16), :],
        own.at[pl.ds(0, 16), :],
        own.at[pl.ds(0, 16), :],
    )
    sends = {}
    for slot, (side_s, side_c) in enumerate(SLOTS):
        sends[slot] = pltpu.make_async_remote_copy(
            src_ref=first_from[slot],
            dst_ref=halo.at[pl.ds(FIRST_AT[slot], FIRST_LEN[slot]), :],
            send_sem=send_sem.at[slot],
            recv_sem=recv_sem.at[slot],
            device_id=peer(-side_s, -side_c),
            device_id_type=MESH,
        )
    relayed = {}
    for slot in BEHIND:
        relayed[slot] = pltpu.make_async_remote_copy(
            src_ref=first_from[slot],
            dst_ref=relay.at[pl.ds(FIRST_AT[slot] - 48, FIRST_LEN[slot]), :],
            send_sem=send_sem.at[slot],
            recv_sem=relay_sem.at[BEHIND.index(slot)],
            device_id=peer(-SLOTS[slot][0], 1 - RUN),
            device_id_type=MESH,
        )
    handed = pltpu.make_async_remote_copy(
        src_ref=relay,
        dst_ref=halo.at[pl.ds(48, RELAY_LEN), :],
        send_sem=forward_sem.at[0],
        recv_sem=forward_sem.at[1],
        device_id=peer(0, RUN - 2),
        device_id_type=MESH,
    )
    at_relay(lambda slot: relayed[slot].wait_recv())
    pl.when(is_relay)(handed.start)
    for slot in FAR_FIRST:
        side_s, side_c = SLOTS[slot]
        here = there(-side_s, -side_c)
        if slot in BEHIND:
            here = jnp.logical_and(here, jnp.logical_not(is_start))
        pl.when(here)(sends[slot].start)
    to_relay(lambda slot: relayed[slot].start())

    for i in order[7:]:
        loads[i].wait()
    for m in range(M):
        modes3[m * 16 : m * 16 + CB, 0:M] = modes_third[m]
        modes12[m * 8 : m * 8 + AB, 0:M] = modes_first[m]
        modes12[m * 8 + 3 : m * 8 + 4, 64 : 64 + M] = modes_second[m]
    for a in range(AB):
        eigen[a : a + 1, 0:M] = eigen_first[a : a + 1, :]
        eigen[a : a + 1, 64 : 64 + M] = eigen_second[...]
    eigen[8 : 8 + CB, 0:M] = eigen_third[...]

    spread = (iota((128, WIDE), 0) == (iota((128, WIDE), 1) & 15)).astype(F32).astype(BF16)
    same = (iota((CB * M, WIDE), 0) & 15) == (iota((CB * M, WIDE), 1) >> 4)
    fore = []
    back = []
    node, box = iota((128, WIDE), 0), iota((128, WIDE), 1) >> 4
    stays = jnp.logical_or(
        (node >> 3) == box, jnp.logical_or((node & 7) == 0, (node & 7) == 7)
    )
    for part in split(modes3[...]):
        diagonal = jnp.where(same, dot(part, spread), 0.0).astype(BF16)
        moved = dot(gather[...], diagonal)
        fore.append(moved.astype(BF16))
        back.append(jnp.where(stays, moved, 0.0).astype(BF16))

    modes_parts = jnp.concatenate(split(modes12[...]), axis=0)
    picked = lax.dot_general(
        pick[...], modes_parts, (((1,), (1,)), ((), ())), preferred_element_type=F32
    )
    at_block = block_of(iota((ROWS, WIDE), 0)) == (iota((ROWS, WIDE), 1) & 7)
    by_p = jnp.where(at_block, picked, 0.0).astype(BF16)
    by_q = picked.astype(BF16)
    forward = dot(by_p, jnp.concatenate([cols_first[...]] * 2, axis=0)) * dot(
        by_q, jnp.concatenate([cols_second[...]] * 2, axis=0)
    )
    own_split = split(forward[:, :OWN])
    halo_split = split(forward[:, OWN:])

    relative = (iota((ROWS, WIDE), 1) >> 3) + 2 - N1 * block_of(iota((ROWS, WIDE), 0))
    keep = jnp.logical_and(relative != 0, relative != 11)
    square = jnp.where(keep, forward[:, :WIDE], 0.0)
    square = jnp.concatenate([square, jnp.zeros((DEEP - ROWS, WIDE), F32)], axis=0)
    turned = jnp.transpose(square)
    for k in range(3):
        kept[k] = turned[:, k * 128 : (k + 1) * 128]

    def kept_rows(rows):
        return jnp.concatenate([kept[k, rows, :] for k in range(3)], axis=1)

    back_own = split(kept_rows(pl.ds(0, OWN)))
    back_edge = split(
        jnp.concatenate(
            [
                kept_rows(pl.ds(7, NF, stride=N1)),
                kept_rows(pl.ds(0, NF, stride=N1)),
                kept_rows(pl.ds(OWN - 8, 8)),
                kept_rows(pl.ds(0, 8)),
            ],
            axis=0,
        )
    )

    third_eigen = eigen[8 : 8 + CB, :]
    for shift in (16, 32, 64):
        third_eigen = third_eigen + pltpu.roll(third_eigen, shift, 1)
    third_eigen = jnp.concatenate([third_eigen, third_eigen], axis=1)
    own_box = iota((CB, WIDE), 0) == (iota((CB, WIDE), 1) >> 4)
    lane_part = jnp.sum(jnp.where(own_box, third_eigen, 0.0), axis=0, keepdims=True)
    inverse = []
    edges = [0, STEP, 2 * STEP, ROWS]
    for a in range(AB):
        rows = slice(edges[a], edges[a + 1])
        row_part = jnp.sum(
            pick[...].astype(F32)[rows] * eigen[a : a + 1, :], axis=1, keepdims=True
        )
        total = row_part + lane_part
        inverse.append(1.0 / jnp.where(total > 0.0, total, 1.0))
    inverse = jnp.concatenate(inverse, axis=0)

    own_third = wide_product(split(own[...]), fore)
    spectral_own = product(own_split, split(own_third))

    for slot in range(8):
        here = there(*SLOTS[slot])
        if slot in BEHIND:
            here = jnp.logical_and(here, jnp.logical_not(is_last))
        pl.when(here)(sends[slot].wait_recv)
    pl.when(is_last)(handed.wait_recv)
    halo_third = wide_product(split(halo[...]), fore)
    spectral = (spectral_own + product(halo_split, split(halo_third))) * inverse
    spectral = split(
        jnp.concatenate([spectral, jnp.zeros((DEEP - ROWS, WIDE), F32)], axis=0)
    )
    stage_last[...] = product_nt(split(product(back_edge, spectral)), back)
    last = {}
    for slot, (side_s, side_c) in enumerate(SLOTS):
        last[slot] = pltpu.make_async_remote_copy(
            src_ref=stage_last.at[pl.ds(LAST_FROM[slot], LAST_LEN[slot]), :],
            dst_ref=halo_last.at[pl.ds(LAST_AT[slot], LAST_LEN[slot]), :],
            send_sem=send_last.at[slot],
            recv_sem=recv_last.at[slot],
            device_id=peer(-side_s, -side_c),
            device_id_type=MESH,
        )
    for_each(FAR_FIRST, -1, lambda slot: last[slot].start())

    sub = iota((8, 128), 0)

    def shifted(tile, to_top):
        moved = pltpu.roll(tile, 1 if to_top else 7, 0)
        return jnp.where(sub == (0 if to_top else 7), moved, 0.0)

    assembled[...] = own[...]
    for node, row in ((0, 24), (7, 48)):
        place = pl.ds(node, NF, stride=N1)
        assembled[place, :] = assembled[place, :] + halo[pl.ds(row, NF), :]

    def layer_beside(slot, at_prev, at_next, side):
        rows = 8 if side < 0 else 0
        base = halo[pl.ds(FIRST_AT[slot] + rows, 8), :]
        base = base + shifted(halo[pl.ds(FIRST_AT[at_prev] + rows, 8), :], True)
        return base + shifted(halo[pl.ds(FIRST_AT[at_next] + rows, 8), :], False)

    assembled[pl.ds(0, 8), :] = assembled[pl.ds(0, 8), :] + layer_beside(2, 4, 5, -1)
    assembled[pl.ds(OWN - 8, 8), :] = assembled[pl.ds(OWN - 8, 8), :] + layer_beside(3, 6, 7, 1)
    for a in range(AB - 1):
        at = (a * N1 + 7) * N1
        total = assembled[pl.ds(at, 8), :] + assembled[pl.ds(at + 8, 8), :]
        assembled[pl.ds(at, 8), :] = total
        assembled[pl.ds(at + 8, 8), :] = total
    value = assembled[...]
    lane = iota((OWN, 128), 1)
    from_left = jnp.where(jnp.logical_and((lane & 7) == 0, lane > 0), pltpu.roll(value, 1, 1), 0.0)
    from_right = jnp.where(
        jnp.logical_and((lane & 7) == 7, lane < 127), pltpu.roll(value, 127, 1), 0.0
    )
    op_ref[...] = (value + from_left + from_right).reshape(NF, N1, 128)

    solved[...] = product_nt(split(product(back_own, spectral)), back)

    for_each(range(8), 1, lambda slot: last[slot].wait_recv())
    for node, row in ((0, 0), (7, 24)):
        place = pl.ds(node, NF, stride=N1)
        solved[place, :] = solved[place, :] + halo_last[pl.ds(row, NF), :]

    def layer_last(slot, at_prev, at_next):
        base = halo_last[pl.ds(LAST_AT[slot], 8), :]
        base = base + shifted(halo_last[pl.ds(LAST_AT[at_prev], 8), :], True)
        return base + shifted(halo_last[pl.ds(LAST_AT[at_next], 8), :], False)

    solved[pl.ds(0, 8), :] = solved[pl.ds(0, 8), :] + layer_last(2, 4, 5)
    solved[pl.ds(OWN - 8, 8), :] = solved[pl.ds(OWN - 8, 8), :] + layer_last(3, 6, 7)
    pre_ref[...] = solved[...].reshape(NF, N1, 128)

    for_each(range(8), -1, lambda slot: sends[slot].wait_send())
    for_each(range(8), -1, lambda slot: last[slot].wait_send())
    pl.when(is_relay)(handed.wait_send)


def write_out(op_in, pre_in, op_out, pre_out, sem):
    copies = [
        pltpu.make_async_copy(source, target, sem.at[i])
        for i, (source, target) in enumerate(((op_in, op_out), (pre_in, pre_out)))
    ]
    for copy in copies:
        copy.start()
    for copy in copies:
        copy.wait()


def shards(*args):
    operands = list(args) + [jnp.asarray(t) for t in tables()]
    for i in (3, 4, 5):
        operands[i] = jnp.transpose(operands[i], (1, 0, 2))
    out = pltpu.VMEM((NF, N1, CB * N1), F32)
    held = pl.pallas_call(
        kernel,
        out_shape=(out, out),
        in_specs=[pl.BlockSpec(memory_space=pl.ANY)] * len(operands),
        out_specs=(pl.BlockSpec(memory_space=pltpu.VMEM),) * 2,
        scratch_shapes=[pltpu.VMEM(t.shape, t.dtype) for t in operands]
        + [
            pltpu.VMEM((OWN, 128), F32),
            pltpu.VMEM((96, 128), F32),
            pltpu.VMEM((HALO, 128), F32),
            pltpu.VMEM((64, 128), F32),
            pltpu.VMEM((96, 128), F32),
            pltpu.VMEM((OWN, 128), F32),
            pltpu.VMEM((OWN, 128), F32),
            pltpu.VMEM((3, WIDE, 128), F32),
            pltpu.VMEM((CB * M, 128), F32),
            pltpu.VMEM((128, 128), F32),
            pltpu.VMEM((32, 128), F32),
            pltpu.SemaphoreType.DMA((N_IN,)),
            pltpu.SemaphoreType.DMA((8,)),
            pltpu.SemaphoreType.DMA((8,)),
            pltpu.SemaphoreType.DMA((8,)),
            pltpu.SemaphoreType.DMA((8,)),
            pltpu.VMEM((RELAY_LEN, 128), F32),
            pltpu.SemaphoreType.DMA((3,)),
            pltpu.SemaphoreType.DMA((2,)),
        ],
        compiler_params=pltpu.CompilerParams(collective_id=0, has_side_effects=True),
        name="pressure_step",
    )(*operands)
    held = [pltpu.with_memory_space_constraint(value, pltpu.VMEM) for value in held]
    out = jax.ShapeDtypeStruct((NF, N1, CB * N1), F32)
    return pl.pallas_call(
        write_out,
        out_shape=(out, out),
        in_specs=[pl.BlockSpec(memory_space=pltpu.VMEM)] * 2,
        out_specs=(pl.BlockSpec(memory_space=pl.ANY),) * 2,
        scratch_shapes=[pltpu.SemaphoreType.DMA((2,))],
        name="write_out",
    )(*held)


def solution(mesh):
    in_specs = (
        P("stream", "cross", None),
        P(None, "stream", "cross", None),
        P(None, "stream", "cross", None),
        P("stream", None, None),
        P("cross", None, None),
        P(),
        P("stream", None),
        P("cross", None),
        P(),
    )
    out_specs = (P("stream", "cross", None), P("stream", "cross", None))
    return jax.shard_map(shards, mesh=mesh, in_specs=in_specs, out_specs=out_specs, check_vma=False)
```

```python
import functools

import jax
import jax.numpy as jnp
import numpy as np
from jax import lax
from jax.experimental import pallas as pl
from jax.experimental.pallas import tpu as pltpu
from jax.sharding import PartitionSpec as P

N1 = 8
M = 10
AB = 3
CB = 16
NF = AB * N1
OWN = NF * N1
HALO = 192
COLS = OWN + HALO
STEP = 104
ROWS = 320
DEEP = 384
WIDE = 256
F32 = jnp.float32
BF16 = jnp.bfloat16
MESH = pl.DeviceIdType.MESH
N_IN = 17
RUN = 8
BEHIND = (1, 5, 7)
RELAY_LEN = 80

SLOTS = ((0, -1), (0, 1), (-1, 0), (1, 0), (-1, -1), (-1, 1), (1, -1), (1, 1))
FIRST_AT = (0, 48, 128, 144, 160, 96, 176, 112)
FIRST_LEN = (48, 48, 16, 16, 16, 16, 16, 16)
LAST_AT = (0, 24, 48, 56, 64, 72, 80, 88)
LAST_LEN = (24, 24, 8, 8, 8, 8, 8, 8)
LAST_FROM = (0, 24, 48, 56, 48, 48, 56, 56)
FAR_FIRST = (4, 5, 6, 7, 0, 1, 2, 3)


def legendre_values(nodes, degree):
    table = np.zeros((nodes.shape[0], degree + 1))
    table[:, 0] = 1.0
    table[:, 1] = nodes
    for order in range(2, degree + 1):
        table[:, order] = (
            (2 * order - 1) * nodes * table[:, order - 1] - (order - 1) * table[:, order - 2]
        ) / order
    return table


def derivative_table(points):
    degree = points - 1
    nodes = np.cos(np.pi * np.arange(points) / degree)
    for sweep in range(100):
        table = legendre_values(nodes, degree)
        nodes = nodes - (nodes * table[:, degree] - table[:, degree - 1]) / (
            points * table[:, degree]
        )
    gll_nodes = nodes[::-1]
    legendre_at = legendre_values(gll_nodes, degree)[:, degree]
    diff_table = np.zeros((points, points))
    for first_index in range(points):
        for second_index in range(points):
            if first_index != second_index:
                diff_table[first_index, second_index] = legendre_at[first_index] / (
                    legendre_at[second_index] * (gll_nodes[first_index] - gll_nodes[second_index])
                )
    diff_table[0, 0] = -degree * (degree + 1) / 4.0
    diff_table[degree, degree] = degree * (degree + 1) / 4.0
    return diff_table


LAYER_NODE = [0, 1, 1, 2, 3, 4, 5, 6, 7, 8, 8, 9]


def halves(table):
    high = table.astype(BF16)
    return high, (table - high.astype(np.float32)).astype(BF16)


def tables():
    diff = derivative_table(N1).astype(np.float32)
    eye8 = np.eye(N1, dtype=np.float32)
    left = np.concatenate([np.kron(diff, eye8), np.kron(eye8, diff)], axis=0)
    high, low = halves(left)
    left_all = np.concatenate([high, high, low], axis=1)
    left_t = np.concatenate([high.T, low.T], axis=1)
    zero = np.zeros((CB * N1, CB * N1), BF16)
    thirds = []
    for matrix in (diff.T, diff):
        high, low = halves(np.kron(np.eye(CB, dtype=np.float32), matrix))
        thirds.append(np.block([[high, low], [high, zero]]))
    gather = np.zeros((CB * N1, CB * M), np.float32)
    for c in range(CB):
        for layer in range(12):
            at = c * N1 + layer - 2
            if 0 <= at < CB * N1:
                gather[at, LAYER_NODE[layer] * CB + c] = 1.0
    pick = np.zeros((ROWS, 128), np.float32)
    for a in range(AB):
        for p in range(M):
            for q in range(M):
                pick[a * STEP + p * M + q, p] = 1.0
                pick[a * STEP + p * M + q, 64 + q] = 1.0
    first_layer = np.zeros(COLS, np.int32)
    second_layer = np.full(COLS, -1, np.int32)
    for f in range(NF):
        for j in range(N1):
            first_layer[f * N1 + j] = f + 2
            second_layer[f * N1 + j] = j + 2
    for slot, (side_s, side_c) in enumerate(SLOTS):
        for row in range(FIRST_LEN[slot]):
            col = OWN + FIRST_AT[slot] + row
            if side_s == 0:
                jj, f = divmod(row, NF)
                first_layer[col] = f + 2
                second_layer[col] = jj if side_c < 0 else 10 + jj
            else:
                l, j = divmod(row, N1)
                first_layer[col] = l if side_s < 0 else 26 + l
                if side_c == 0:
                    second_layer[col] = j + 2
                elif side_c < 0:
                    second_layer[col] = j - 6 if j >= 6 else -1
                else:
                    second_layer[col] = 10 + j if j < 2 else -1
    cols_first = np.zeros((128, COLS), np.float32)
    cols_second = np.zeros((128, COLS), np.float32)
    for col in range(COLS):
        for a in range(AB):
            layer = first_layer[col] - N1 * a
            if 0 <= layer < 12:
                cols_first[LAYER_NODE[layer] * 8 + a, col] = 1.0
        if second_layer[col] >= 0:
            cols_second[LAYER_NODE[second_layer[col]] * 8 + 3, col] = 1.0
    exact = [t.astype(BF16) for t in (gather, pick, cols_first, cols_second)]
    return [left_all, left_t] + thirds + exact


def dot(a, b):
    return lax.dot_general(a, b, (((1,), (0,)), ((), ())), preferred_element_type=F32)


def split(value):
    high = value.astype(BF16)
    return high, (value - high.astype(F32)).astype(BF16)


def product(a, b):
    return dot(a[0], b[0]) + (dot(a[1], b[0]) + dot(a[0], b[1]))


def lane_product(a, table):
    both = dot(jnp.concatenate(a, axis=1), table)
    return both[:, :128] + both[:, 128:]


def wide_product(a, b):
    return dot(jnp.concatenate(a, axis=1), jnp.concatenate([b[0], b[0]], axis=0)) + dot(a[0], b[1])


def product_nt(a, b):
    def one(x, y):
        return lax.dot_general(x, y, (((1,), (1,)), ((), ())), preferred_element_type=F32)

    return one(a[0], b[0]) + (one(a[1], b[0]) + one(a[0], b[1]))


def iota(shape, dimension):
    return lax.broadcasted_iota(jnp.int32, shape, dimension)


def block_of(rows):
    return (rows >= STEP).astype(jnp.int32) + (rows >= 2 * STEP).astype(jnp.int32)


def kernel(*refs):
    hbm = refs[:N_IN]
    op_ref, pre_ref = refs[N_IN : N_IN + 2]
    vmem = refs[N_IN + 2 : 2 * N_IN + 2]
    (
        own,
        stage,
        halo,
        stage_last,
        halo_last,
        assembled,
        solved,
        kept,
        modes3,
        modes12,
        eigen,
        load_sem,
        send_sem,
        recv_sem,
        send_last,
        recv_last,
        relay,
        relay_sem,
        forward_sem,
        ready_sem,
    ) = refs[2 * N_IN + 2 :]
    (
        pressure,
        geo_diag,
        geo_off,
        modes_first,
        modes_second,
        modes_third,
        eigen_first,
        eigen_second,
        eigen_third,
        left,
        left_t,
        third,
        third_t,
        gather,
        pick,
        cols_first,
        cols_second,
    ) = vmem
    n_s, n_c = lax.axis_size("stream"), lax.axis_size("cross")
    me_s, me_c = lax.axis_index("stream"), lax.axis_index("cross")

    def peer(side_s, side_c):
        return {
            "stream": lax.rem(me_s + side_s + n_s, n_s),
            "cross": lax.rem(me_c + side_c + n_c, n_c),
        }

    at_s = {-1: me_s > 0, 0: True, 1: me_s < n_s - 1}
    at_c = {-1: me_c > 0, 0: True, 1: me_c < n_c - 1}

    is_last = jnp.logical_and(lax.rem(me_c, RUN) == RUN - 1, me_c < n_c - 1)
    is_start = jnp.logical_and(lax.rem(me_c, RUN) == 0, me_c > 0)
    is_relay = jnp.logical_and(lax.rem(me_c, RUN) == 1, me_c + RUN - 1 < n_c)

    def there(side_s, side_c):
        if side_s == 0:
            return at_c[side_c]
        if side_c == 0:
            return at_s[side_s]
        return jnp.logical_and(at_s[side_s], at_c[side_c])

    def both(first, second):
        return second if first is True else jnp.logical_and(first, second)

    def when(act, *conditions):
        pl.when(functools.reduce(both, conditions, True))(act)

    def for_each(order, sign, act):
        for slot in order:
            side_s, side_c = SLOTS[slot]
            when(functools.partial(act, slot), there(sign * side_s, sign * side_c))

    not_last = jnp.logical_not(is_last)
    not_start = jnp.logical_not(is_start)

    halo[...] = jnp.zeros_like(halo)
    halo_last[...] = jnp.zeros_like(halo_last)
    relay[...] = jnp.zeros_like(relay)
    barrier = pltpu.get_barrier_semaphore()

    def greet(side_s, side_c):
        pl.semaphore_signal(barrier, inc=1, device_id=peer(side_s, side_c), device_id_type=MESH)

    def hello(side_s, side_c, *conditions):
        when(functools.partial(greet, side_s, side_c), at_s[side_s], *conditions)

    hello(0, 2 - RUN, is_last)
    hello(-1, 0)
    hello(1, 0)
    hello(0, 1, at_c[1], not_last)
    for side_s in (0, -1, 1):
        hello(side_s, -1, is_start)
        hello(side_s, RUN - 1, is_relay)
    count_s = at_s[-1].astype(jnp.int32) + at_s[1].astype(jnp.int32)
    neighbours = (
        count_s
        + jnp.logical_and(at_c[-1], not_start).astype(jnp.int32)
        + (1 + count_s) * jnp.logical_or(is_last, is_start).astype(jnp.int32)
        + is_relay.astype(jnp.int32)
    )
    loads = [
        pltpu.make_async_copy(hbm[i], vmem[i], load_sem.at[i]) for i in range(N_IN)
    ]
    order = [0, 9, 11, 1, 2, 10, 12, 5, 13, 3, 4, 14, 15, 16, 6, 7, 8]
    for i in order:
        loads[i].start()

    modes3[...] = jnp.zeros_like(modes3)
    modes12[...] = jnp.zeros_like(modes12)
    eigen[...] = jnp.zeros_like(eigen)

    for i in (0, 9, 11):
        loads[i].wait()
    pres = split(pressure[...].reshape(OWN, 128))
    per = N1 * N1
    along = []
    for a in range(AB):
        high, low = (part[a * per : (a + 1) * per] for part in pres)
        along.append(dot(left[...], jnp.concatenate([high, low, high], axis=0)))
    grad_third = lane_product(pres, third[...])
    for i in (1, 2, 10, 12):
        loads[i].wait()
    for a in range(AB):
        rows = pl.ds(a * N1, N1)
        d0, d1, d2 = (geo_diag[k, rows].reshape(per, 128) for k in range(3))
        o0, o1, o2 = (geo_off[k, rows].reshape(per, 128) for k in range(3))
        g1, g2 = along[a][:per], along[a][per:]
        g3 = grad_third[a * per : (a + 1) * per]
        flux_first = d0 * g1 + o0 * g2 + o1 * g3
        flux_second = o0 * g1 + d1 * g2 + o2 * g3
        flux_third = o1 * g1 + o2 * g2 + d2 * g3
        high, low = split(jnp.concatenate([flux_first, flux_second], axis=0))
        own[pl.ds(a * per, per), :] = (
            dot(left_t[...], jnp.concatenate([high, high], axis=0))
            + dot(left_t[:, :128], low)
            + lane_product(split(flux_third), third_t[...])
        )
    for k, node in enumerate((6, 7, 0, 1)):
        stage[pl.ds(k * NF, NF), :] = own[pl.ds(node, NF, stride=N1), :]

    pl.semaphore_wait(barrier, neighbours)
    first_from = (
        stage.at[pl.ds(0, 48), :],
        stage.at[pl.ds(48, 48), :],
        own.at[pl.ds(OWN - 16, 16), :],
        own.at[pl.ds(0, 16), :],
        own.at[pl.ds(OWN - 16, 16), :],
        own.at[pl.ds(OWN - 16, 16), :],
        own.at[pl.ds(0, 16), :],
        own.at[pl.ds(0, 16), :],
    )
    sends = {}
    for slot, (side_s, side_c) in enumerate(SLOTS):
        sends[slot] = pltpu.make_async_remote_copy(
            src_ref=first_from[slot],
            dst_ref=halo.at[pl.ds(FIRST_AT[slot], FIRST_LEN[slot]), :],
            send_sem=send_sem.at[slot],
            recv_sem=recv_sem.at[slot],
            device_id=peer(-side_s, -side_c),
            device_id_type=MESH,
        )
    relayed = {}
    for slot in BEHIND:
        relayed[slot] = pltpu.make_async_remote_copy(
            src_ref=first_from[slot],
            dst_ref=relay.at[pl.ds(FIRST_AT[slot] - 48, FIRST_LEN[slot]), :],
            send_sem=send_sem.at[slot],
            recv_sem=relay_sem.at[BEHIND.index(slot)],
            device_id=peer(-SLOTS[slot][0], 1 - RUN),
            device_id_type=MESH,
        )
    handed = pltpu.make_async_remote_copy(
        src_ref=relay,
        dst_ref=halo.at[pl.ds(48, RELAY_LEN), :],
        send_sem=forward_sem.at[0],
        recv_sem=forward_sem.at[1],
        device_id=peer(0, RUN - 2),
        device_id_type=MESH,
    )
    onward = {}
    for slot in (4, 5, 6, 7):
        side_s, side_c = SLOTS[slot]
        onward[slot] = pltpu.make_async_remote_copy(
            src_ref=halo.at[pl.ds(FIRST_AT[2 if side_s < 0 else 3], 16), :],
            dst_ref=halo.at[pl.ds(FIRST_AT[slot], 16), :],
            send_sem=send_sem.at[slot],
            recv_sem=recv_sem.at[slot],
            device_id=peer(0, -side_c),
            device_id_type=MESH,
        )
    for slot in BEHIND:
        when(relayed[slot].wait_recv, is_relay, at_s[SLOTS[slot][0]])
    when(handed.start, is_relay)

    def say_ready():
        pl.semaphore_signal(ready_sem, inc=1, device_id=peer(0, -1), device_id_type=MESH)

    def hear_ready():
        pl.semaphore_wait(ready_sem, 1)

    when(say_ready, at_c[-1], not_start)
    when(sends[2].start, at_s[1])
    when(sends[3].start, at_s[-1])
    when(sends[1].start, at_c[-1], not_start)
    for slot in (4, 6, 0):
        when(sends[slot].start, is_last, at_s[-SLOTS[slot][0]])
    for slot in BEHIND:
        when(relayed[slot].start, is_start, at_s[-SLOTS[slot][0]])
    when(hear_ready, at_c[1], not_last)
    when(sends[0].start, at_c[1], not_last)

    def hand_on(turn):
        for source in (2, 3):
            side = SLOTS[source][0]
            when(sends[source].wait_recv, turn, at_s[side])
            for slot in (4, 5, 6, 7):
                side_s, side_c = SLOTS[slot]
                if side_s == side:
                    allowed = not_last if side_c < 0 else not_start
                    when(onward[slot].start, turn, at_s[side], at_c[-side_c], allowed)

    hand_on(not_last)

    for i in order[7:]:
        loads[i].wait()
    for m in range(M):
        modes3[m * 16 : m * 16 + CB, 0:M] = modes_third[m]
        modes12[m * 8 : m * 8 + AB, 0:M] = modes_first[m]
        modes12[m * 8 + 3 : m * 8 + 4, 64 : 64 + M] = modes_second[m]
    for a in range(AB):
        eigen[a : a + 1, 0:M] = eigen_first[a : a + 1, :]
        eigen[a : a + 1, 64 : 64 + M] = eigen_second[...]
    eigen[8 : 8 + CB, 0:M] = eigen_third[...]

    spread = (iota((128, WIDE), 0) == (iota((128, WIDE), 1) & 15)).astype(F32).astype(BF16)
    same = (iota((CB * M, WIDE), 0) & 15) == (iota((CB * M, WIDE), 1) >> 4)
    fore = []
    back = []
    node, box = iota((128, WIDE), 0), iota((128, WIDE), 1) >> 4
    stays = jnp.logical_or(
        (node >> 3) == box, jnp.logical_or((node & 7) == 0, (node & 7) == 7)
    )
    for part in split(modes3[...]):
        diagonal = jnp.where(same, dot(part, spread), 0.0).astype(BF16)
        moved = dot(gather[...], diagonal)
        fore.append(moved.astype(BF16))
        back.append(jnp.where(stays, moved, 0.0).astype(BF16))

    modes_parts = jnp.concatenate(split(modes12[...]), axis=0)
    picked = lax.dot_general(
        pick[...], modes_parts, (((1,), (1,)), ((), ())), preferred_element_type=F32
    )
    at_block = block_of(iota((ROWS, WIDE), 0)) == (iota((ROWS, WIDE), 1) & 7)
    by_p = jnp.where(at_block, picked, 0.0).astype(BF16)
    by_q = picked.astype(BF16)
    forward = dot(by_p, jnp.concatenate([cols_first[...]] * 2, axis=0)) * dot(
        by_q, jnp.concatenate([cols_second[...]] * 2, axis=0)
    )
    own_split = split(forward[:, :OWN])
    halo_split = split(forward[:, OWN:])

    relative = (iota((ROWS, WIDE), 1) >> 3) + 2 - N1 * block_of(iota((ROWS, WIDE), 0))
    keep = jnp.logical_and(relative != 0, relative != 11)
    square = jnp.where(keep, forward[:, :WIDE], 0.0)
    square = jnp.concatenate([square, jnp.zeros((DEEP - ROWS, WIDE), F32)], axis=0)
    turned = jnp.transpose(square)
    for k in range(3):
        kept[k] = turned[:, k * 128 : (k + 1) * 128]

    def kept_rows(rows):
        return jnp.concatenate([kept[k, rows, :] for k in range(3)], axis=1)

    back_own = split(kept_rows(pl.ds(0, OWN)))
    back_edge = split(
        jnp.concatenate(
            [
                kept_rows(pl.ds(7, NF, stride=N1)),
                kept_rows(pl.ds(0, NF, stride=N1)),
                kept_rows(pl.ds(OWN - 8, 8)),
                kept_rows(pl.ds(0, 8)),
            ],
            axis=0,
        )
    )

    third_eigen = eigen[8 : 8 + CB, :]
    for shift in (16, 32, 64):
        third_eigen = third_eigen + pltpu.roll(third_eigen, shift, 1)
    third_eigen = jnp.concatenate([third_eigen, third_eigen], axis=1)
    own_box = iota((CB, WIDE), 0) == (iota((CB, WIDE), 1) >> 4)
    lane_part = jnp.sum(jnp.where(own_box, third_eigen, 0.0), axis=0, keepdims=True)
    inverse = []
    edges = [0, STEP, 2 * STEP, ROWS]
    for a in range(AB):
        rows = slice(edges[a], edges[a + 1])
        row_part = jnp.sum(
            pick[...].astype(F32)[rows] * eigen[a : a + 1, :], axis=1, keepdims=True
        )
        total = row_part + lane_part
        inverse.append(1.0 / jnp.where(total > 0.0, total, 1.0))
    inverse = jnp.concatenate(inverse, axis=0)

    own_third = wide_product(split(own[...]), fore)
    spectral_own = product(own_split, split(own_third))

    hand_on(is_last)
    for slot in (0, 1, 4, 5, 6, 7):
        arrives = not_last if slot in BEHIND else True
        when(sends[slot].wait_recv, there(*SLOTS[slot]), arrives)
    pl.when(is_last)(handed.wait_recv)
    halo_third = wide_product(split(halo[...]), fore)
    spectral = (spectral_own + product(halo_split, split(halo_third))) * inverse
    spectral = split(
        jnp.concatenate([spectral, jnp.zeros((DEEP - ROWS, WIDE), F32)], axis=0)
    )
    stage_last[...] = product_nt(split(product(back_edge, spectral)), back)
    last = {}
    for slot, (side_s, side_c) in enumerate(SLOTS):
        last[slot] = pltpu.make_async_remote_copy(
            src_ref=stage_last.at[pl.ds(LAST_FROM[slot], LAST_LEN[slot]), :],
            dst_ref=halo_last.at[pl.ds(LAST_AT[slot], LAST_LEN[slot]), :],
            send_sem=send_last.at[slot],
            recv_sem=recv_last.at[slot],
            device_id=peer(-side_s, -side_c),
            device_id_type=MESH,
        )
    for_each(FAR_FIRST, -1, lambda slot: last[slot].start())

    sub = iota((8, 128), 0)

    def shifted(tile, to_top):
        moved = pltpu.roll(tile, 1 if to_top else 7, 0)
        return jnp.where(sub == (0 if to_top else 7), moved, 0.0)

    assembled[...] = own[...]
    for node, row in ((0, 24), (7, 48)):
        place = pl.ds(node, NF, stride=N1)
        assembled[place, :] = assembled[place, :] + halo[pl.ds(row, NF), :]

    def layer_beside(slot, at_prev, at_next, side):
        rows = 8 if side < 0 else 0
        base = halo[pl.ds(FIRST_AT[slot] + rows, 8), :]
        base = base + shifted(halo[pl.ds(FIRST_AT[at_prev] + rows, 8), :], True)
        return base + shifted(halo[pl.ds(FIRST_AT[at_next] + rows, 8), :], False)

    assembled[pl.ds(0, 8), :] = assembled[pl.ds(0, 8), :] + layer_beside(2, 4, 5, -1)
    assembled[pl.ds(OWN - 8, 8), :] = assembled[pl.ds(OWN - 8, 8), :] + layer_beside(3, 6, 7, 1)
    for a in range(AB - 1):
        at = (a * N1 + 7) * N1
        total = assembled[pl.ds(at, 8), :] + assembled[pl.ds(at + 8, 8), :]
        assembled[pl.ds(at, 8), :] = total
        assembled[pl.ds(at + 8, 8), :] = total
    value = assembled[...]
    lane = iota((OWN, 128), 1)
    from_left = jnp.where(jnp.logical_and((lane & 7) == 0, lane > 0), pltpu.roll(value, 1, 1), 0.0)
    from_right = jnp.where(
        jnp.logical_and((lane & 7) == 7, lane < 127), pltpu.roll(value, 127, 1), 0.0
    )
    op_ref[...] = (value + from_left + from_right).reshape(NF, N1, 128)

    solved[...] = product_nt(split(product(back_own, spectral)), back)

    for_each(range(8), 1, lambda slot: last[slot].wait_recv())
    for node, row in ((0, 0), (7, 24)):
        place = pl.ds(node, NF, stride=N1)
        solved[place, :] = solved[place, :] + halo_last[pl.ds(row, NF), :]

    def layer_last(slot, at_prev, at_next):
        base = halo_last[pl.ds(LAST_AT[slot], 8), :]
        base = base + shifted(halo_last[pl.ds(LAST_AT[at_prev], 8), :], True)
        return base + shifted(halo_last[pl.ds(LAST_AT[at_next], 8), :], False)

    solved[pl.ds(0, 8), :] = solved[pl.ds(0, 8), :] + layer_last(2, 4, 5)
    solved[pl.ds(OWN - 8, 8), :] = solved[pl.ds(OWN - 8, 8), :] + layer_last(3, 6, 7)
    pre_ref[...] = solved[...].reshape(NF, N1, 128)

    for_each(range(4), -1, lambda slot: sends[slot].wait_send())
    for slot in (4, 5, 6, 7):
        side_s, side_c = SLOTS[slot]
        direct = is_last if side_c < 0 else is_start
        straight = both(at_s[-side_s], direct)
        passed = both(at_s[side_s], jnp.logical_and(at_c[-side_c], jnp.logical_not(direct)))
        when(sends[slot].wait_send, jnp.logical_or(straight, passed))
    for_each(range(8), -1, lambda slot: last[slot].wait_send())
    pl.when(is_relay)(handed.wait_send)


def write_out(op_in, pre_in, op_out, pre_out, sem):
    copies = [
        pltpu.make_async_copy(source, target, sem.at[i])
        for i, (source, target) in enumerate(((op_in, op_out), (pre_in, pre_out)))
    ]
    for copy in copies:
        copy.start()
    for copy in copies:
        copy.wait()


def shards(*args):
    operands = list(args) + [jnp.asarray(t) for t in tables()]
    for i in (3, 4, 5):
        operands[i] = jnp.transpose(operands[i], (1, 0, 2))
    out = pltpu.VMEM((NF, N1, CB * N1), F32)
    held = pl.pallas_call(
        kernel,
        out_shape=(out, out),
        in_specs=[pl.BlockSpec(memory_space=pl.ANY)] * len(operands),
        out_specs=(pl.BlockSpec(memory_space=pltpu.VMEM),) * 2,
        scratch_shapes=[pltpu.VMEM(t.shape, t.dtype) for t in operands]
        + [
            pltpu.VMEM((OWN, 128), F32),
            pltpu.VMEM((96, 128), F32),
            pltpu.VMEM((HALO, 128), F32),
            pltpu.VMEM((64, 128), F32),
            pltpu.VMEM((96, 128), F32),
            pltpu.VMEM((OWN, 128), F32),
            pltpu.VMEM((OWN, 128), F32),
            pltpu.VMEM((3, WIDE, 128), F32),
            pltpu.VMEM((CB * M, 128), F32),
            pltpu.VMEM((128, 128), F32),
            pltpu.VMEM((32, 128), F32),
            pltpu.SemaphoreType.DMA((N_IN,)),
            pltpu.SemaphoreType.DMA((8,)),
            pltpu.SemaphoreType.DMA((8,)),
            pltpu.SemaphoreType.DMA((8,)),
            pltpu.SemaphoreType.DMA((8,)),
            pltpu.VMEM((RELAY_LEN, 128), F32),
            pltpu.SemaphoreType.DMA((3,)),
            pltpu.SemaphoreType.DMA((2,)),
            pltpu.SemaphoreType.REGULAR,
        ],
        compiler_params=pltpu.CompilerParams(collective_id=0, has_side_effects=True),
        name="pressure_step",
    )(*operands)
    held = [pltpu.with_memory_space_constraint(value, pltpu.VMEM) for value in held]
    out = jax.ShapeDtypeStruct((NF, N1, CB * N1), F32)
    return pl.pallas_call(
        write_out,
        out_shape=(out, out),
        in_specs=[pl.BlockSpec(memory_space=pltpu.VMEM)] * 2,
        out_specs=(pl.BlockSpec(memory_space=pl.ANY),) * 2,
        scratch_shapes=[pltpu.SemaphoreType.DMA((2,))],
        name="write_out",
    )(*held)


def solution(mesh):
    in_specs = (
        P("stream", "cross", None),
        P(None, "stream", "cross", None),
        P(None, "stream", "cross", None),
        P("stream", None, None),
        P("cross", None, None),
        P(),
        P("stream", None),
        P("cross", None),
        P(),
    )
    out_specs = (P("stream", "cross", None), P("stream", "cross", None))
    return jax.shard_map(shards, mesh=mesh, in_specs=in_specs, out_specs=out_specs, check_vma=False)
```

```python
import functools

import jax
import jax.numpy as jnp
import numpy as np
from jax import lax
from jax.experimental import pallas as pl
from jax.experimental.pallas import tpu as pltpu
from jax.sharding import PartitionSpec as P

N1 = 8
M = 10
AB = 3
CB = 16
NF = AB * N1
OWN = NF * N1
HALO = 192
COLS = OWN + HALO
STEP = 104
ROWS = 320
DEEP = 384
WIDE = 256
F32 = jnp.float32
BF16 = jnp.bfloat16
MESH = pl.DeviceIdType.MESH
N_IN = 11
RUN = 8
BEHIND = (1, 5, 7)
RELAY_LEN = 80

SLOTS = ((0, -1), (0, 1), (-1, 0), (1, 0), (-1, -1), (-1, 1), (1, -1), (1, 1))
FIRST_AT = (0, 48, 128, 144, 160, 96, 176, 112)
FIRST_LEN = (48, 48, 16, 16, 16, 16, 16, 16)
LAST_AT = (0, 24, 48, 56, 64, 72, 80, 88)
LAST_LEN = (24, 24, 8, 8, 8, 8, 8, 8)
LAST_FROM = (0, 24, 48, 56, 48, 48, 56, 56)
FAR_FIRST = (4, 5, 6, 7, 0, 1, 2, 3)


def legendre_values(nodes, degree):
    table = np.zeros((nodes.shape[0], degree + 1))
    table[:, 0] = 1.0
    table[:, 1] = nodes
    for order in range(2, degree + 1):
        table[:, order] = (
            (2 * order - 1) * nodes * table[:, order - 1] - (order - 1) * table[:, order - 2]
        ) / order
    return table


def derivative_table(points):
    degree = points - 1
    nodes = np.cos(np.pi * np.arange(points) / degree)
    for sweep in range(100):
        table = legendre_values(nodes, degree)
        nodes = nodes - (nodes * table[:, degree] - table[:, degree - 1]) / (
            points * table[:, degree]
        )
    gll_nodes = nodes[::-1]
    legendre_at = legendre_values(gll_nodes, degree)[:, degree]
    diff_table = np.zeros((points, points))
    for first_index in range(points):
        for second_index in range(points):
            if first_index != second_index:
                diff_table[first_index, second_index] = legendre_at[first_index] / (
                    legendre_at[second_index] * (gll_nodes[first_index] - gll_nodes[second_index])
                )
    diff_table[0, 0] = -degree * (degree + 1) / 4.0
    diff_table[degree, degree] = degree * (degree + 1) / 4.0
    return diff_table


LAYER_NODE = [0, 1, 1, 2, 3, 4, 5, 6, 7, 8, 8, 9]


def halves(table):
    high = table.astype(BF16)
    return high, (table - high.astype(np.float32)).astype(BF16)


def tables():
    diff = derivative_table(N1).astype(np.float32)
    eye8 = np.eye(N1, dtype=np.float32)
    left = np.concatenate([np.kron(diff, eye8), np.kron(eye8, diff)], axis=0)
    high, low = halves(left)
    left_all = np.concatenate([high, high, low], axis=1)
    left_t = np.concatenate([high.T, low.T], axis=1)
    zero = np.zeros((CB * N1, CB * N1), BF16)
    thirds = []
    for matrix in (diff.T, diff):
        high, low = halves(np.kron(np.eye(CB, dtype=np.float32), matrix))
        thirds.append(np.block([[high, low], [high, zero]]))
    gather = np.zeros((CB * N1, CB * M), np.float32)
    for c in range(CB):
        for layer in range(12):
            at = c * N1 + layer - 2
            if 0 <= at < CB * N1:
                gather[at, LAYER_NODE[layer] * CB + c] = 1.0
    pick = np.zeros((ROWS, 128), np.float32)
    for a in range(AB):
        for p in range(M):
            for q in range(M):
                pick[a * STEP + p * M + q, p] = 1.0
                pick[a * STEP + p * M + q, 64 + q] = 1.0
    first_layer = np.zeros(COLS, np.int32)
    second_layer = np.full(COLS, -1, np.int32)
    for f in range(NF):
        for j in range(N1):
            first_layer[f * N1 + j] = f + 2
            second_layer[f * N1 + j] = j + 2
    for slot, (side_s, side_c) in enumerate(SLOTS):
        for row in range(FIRST_LEN[slot]):
            col = OWN + FIRST_AT[slot] + row
            if side_s == 0:
                jj, f = divmod(row, NF)
                first_layer[col] = f + 2
                second_layer[col] = jj if side_c < 0 else 10 + jj
            else:
                l, j = divmod(row, N1)
                first_layer[col] = l if side_s < 0 else 26 + l
                if side_c == 0:
                    second_layer[col] = j + 2
                elif side_c < 0:
                    second_layer[col] = j - 6 if j >= 6 else -1
                else:
                    second_layer[col] = 10 + j if j < 2 else -1
    cols_first = np.zeros((128, COLS), np.float32)
    cols_second = np.zeros((128, COLS), np.float32)
    for col in range(COLS):
        for a in range(AB):
            layer = first_layer[col] - N1 * a
            if 0 <= layer < 12:
                cols_first[LAYER_NODE[layer] * 8 + a, col] = 1.0
        if second_layer[col] >= 0:
            cols_second[LAYER_NODE[second_layer[col]] * 8 + 3, col] = 1.0
    exact = [t.astype(BF16) for t in (gather, pick, cols_first, cols_second)]
    left_all = np.concatenate([left_all, np.zeros((128, 64), BF16)], axis=1)
    near = np.concatenate([left_all, left_t] + thirds, axis=0)
    gather, pick, cols_first, cols_second = exact
    gather = np.concatenate([gather, np.zeros((128, 96), BF16)], axis=1)
    wide = [t[:, k : k + 128] for t in (gather, cols_first, cols_second) for k in range(0, t.shape[1], 128)]
    return [near, np.concatenate([pick] + wide, axis=0)]


def dot(a, b):
    return lax.dot_general(a, b, (((1,), (0,)), ((), ())), preferred_element_type=F32)


def split(value):
    high = value.astype(BF16)
    return high, (value - high.astype(F32)).astype(BF16)


def product(a, b):
    rows = a[0].shape[0]
    both = dot(jnp.concatenate(a, axis=0), b[0])
    return both[:rows] + (both[rows:] + dot(a[0], b[1]))


def lane_product(a, table):
    both = dot(jnp.concatenate(a, axis=1), table)
    return both[:, :128] + both[:, 128:]


def wide_product(a, b):
    return dot(jnp.concatenate(a, axis=1), jnp.concatenate([b[0], b[0]], axis=0)) + dot(a[0], b[1])


def dot_nt(a, b):
    return lax.dot_general(a, b, (((1,), (1,)), ((), ())), preferred_element_type=F32)


def product_nt(a, b):
    rows = a[0].shape[0]
    both = dot_nt(jnp.concatenate(a, axis=0), b[0])
    return both[:rows] + (both[rows:] + dot_nt(a[0], b[1]))


def iota(shape, dimension):
    return lax.broadcasted_iota(jnp.int32, shape, dimension)


def block_of(rows):
    return (rows >= STEP).astype(jnp.int32) + (rows >= 2 * STEP).astype(jnp.int32)


def kernel(*refs):
    hbm = refs[:N_IN]
    op_ref, pre_ref = refs[N_IN : N_IN + 2]
    vmem = refs[N_IN + 2 : 2 * N_IN + 2]
    (
        own,
        stage,
        halo,
        stage_last,
        halo_last,
        assembled,
        solved,
        kept,
        modes3,
        modes12,
        eigen,
        load_sem,
        send_sem,
        recv_sem,
        recv_last,
        relay,
        relay_sem,
        forward_sem,
        ready_sem,
    ) = refs[2 * N_IN + 2 :]
    (
        pressure,
        geo_diag,
        geo_off,
        modes_first,
        modes_second,
        modes_third,
        eigen_first,
        eigen_second,
        eigen_third,
        near,
        far,
    ) = vmem
    left, left_t = near.at[0:128, 0:192], near.at[128:192, :]
    third, third_t = near.at[192:448, :], near.at[448:704, :]
    pick = far.at[0:ROWS, :]

    def table(first, count):
        parts = [far[ROWS + 128 * k : ROWS + 128 * (k + 1), :] for k in range(first, first + count)]
        return jnp.concatenate(parts, axis=1)

    n_s, n_c = lax.axis_size("stream"), lax.axis_size("cross")
    me_s, me_c = lax.axis_index("stream"), lax.axis_index("cross")

    def peer(side_s, side_c):
        return {
            "stream": lax.rem(me_s + side_s + n_s, n_s),
            "cross": lax.rem(me_c + side_c + n_c, n_c),
        }

    at_s = {-1: me_s > 0, 0: True, 1: me_s < n_s - 1}
    at_c = {-1: me_c > 0, 0: True, 1: me_c < n_c - 1}

    is_last = jnp.logical_and(lax.rem(me_c, RUN) == RUN - 1, me_c < n_c - 1)
    is_start = jnp.logical_and(lax.rem(me_c, RUN) == 0, me_c > 0)
    is_relay = jnp.logical_and(lax.rem(me_c, RUN) == 1, me_c + RUN - 1 < n_c)

    def there(side_s, side_c):
        if side_s == 0:
            return at_c[side_c]
        if side_c == 0:
            return at_s[side_s]
        return jnp.logical_and(at_s[side_s], at_c[side_c])

    def both(first, second):
        return second if first is True else jnp.logical_and(first, second)

    def when(act, *conditions):
        pl.when(functools.reduce(both, conditions, True))(act)

    def for_each(order, sign, act):
        for slot in order:
            side_s, side_c = SLOTS[slot]
            when(functools.partial(act, slot), there(sign * side_s, sign * side_c))

    not_last = jnp.logical_not(is_last)
    not_start = jnp.logical_not(is_start)

    halo[...] = jnp.zeros_like(halo)
    halo_last[...] = jnp.zeros_like(halo_last)
    relay[...] = jnp.zeros_like(relay)
    barrier = pltpu.get_barrier_semaphore()

    def greet(side_s, side_c):
        pl.semaphore_signal(barrier, inc=1, device_id=peer(side_s, side_c), device_id_type=MESH)

    def hello(side_s, side_c, *conditions):
        when(functools.partial(greet, side_s, side_c), at_s[side_s], *conditions)

    hello(0, 2 - RUN, is_last)
    hello(-1, 0)
    hello(1, 0)
    hello(0, 1, at_c[1], not_last)
    for side_s in (0, -1, 1):
        hello(side_s, -1, is_start)
        hello(side_s, RUN - 1, is_relay)
    count_s = at_s[-1].astype(jnp.int32) + at_s[1].astype(jnp.int32)
    neighbours = (
        count_s
        + jnp.logical_and(at_c[-1], not_start).astype(jnp.int32)
        + (1 + count_s) * jnp.logical_or(is_last, is_start).astype(jnp.int32)
        + is_relay.astype(jnp.int32)
    )
    loads = [
        pltpu.make_async_copy(hbm[i], vmem[i], load_sem.at[i]) for i in range(N_IN)
    ]
    order = [0, 9, 1, 2, 5, 3, 4, 10, 6, 7, 8]
    for i in order:
        loads[i].start()

    modes3[...] = jnp.zeros_like(modes3)
    modes12[...] = jnp.zeros_like(modes12)
    eigen[...] = jnp.zeros_like(eigen)

    loads[0].wait()

    def say_ready():
        pl.semaphore_signal(ready_sem, inc=1, device_id=peer(0, -1), device_id_type=MESH)

    def hear_ready():
        pl.semaphore_wait(ready_sem, 1)

    pl.semaphore_wait(barrier, neighbours)
    when(say_ready, at_c[-1], not_start)
    loads[9].wait()
    pres = split(pressure[...].reshape(OWN, 128))
    per = N1 * N1
    along = []
    for a in range(AB):
        high, low = (part[a * per : (a + 1) * per] for part in pres)
        along.append(dot(left[...], jnp.concatenate([high, low, high], axis=0)))
    grad_third = lane_product(pres, third[...])
    for i in (1, 2):
        loads[i].wait()
    for a in range(AB):
        rows = pl.ds(a * N1, N1)
        d0, d1, d2 = (geo_diag[k, rows].reshape(per, 128) for k in range(3))
        o0, o1, o2 = (geo_off[k, rows].reshape(per, 128) for k in range(3))
        g1, g2 = along[a][:per], along[a][per:]
        g3 = grad_third[a * per : (a + 1) * per]
        flux_first = d0 * g1 + o0 * g2 + o1 * g3
        flux_second = o0 * g1 + d1 * g2 + o2 * g3
        flux_third = o1 * g1 + o2 * g2 + d2 * g3
        high, low = split(jnp.concatenate([flux_first, flux_second], axis=0))
        own[pl.ds(a * per, per), :] = (
            dot(left_t[...], jnp.concatenate([high, high], axis=0))
            + dot(left_t[:, :128], low)
            + lane_product(split(flux_third), third_t[...])
        )
    for k, node in enumerate((6, 7, 0, 1)):
        stage[pl.ds(k * NF, NF), :] = own[pl.ds(node, NF, stride=N1), :]

    first_from = (
        stage.at[pl.ds(0, 48), :],
        stage.at[pl.ds(48, 48), :],
        own.at[pl.ds(OWN - 16, 16), :],
        own.at[pl.ds(0, 16), :],
        own.at[pl.ds(OWN - 16, 16), :],
        own.at[pl.ds(OWN - 16, 16), :],
        own.at[pl.ds(0, 16), :],
        own.at[pl.ds(0, 16), :],
    )
    sends = {}
    for slot, (side_s, side_c) in enumerate(SLOTS):
        sends[slot] = pltpu.make_async_remote_copy(
            src_ref=first_from[slot],
            dst_ref=halo.at[pl.ds(FIRST_AT[slot], FIRST_LEN[slot]), :],
            send_sem=send_sem.at[slot],
            recv_sem=recv_sem.at[slot],
            device_id=peer(-side_s, -side_c),
            device_id_type=MESH,
        )
    relayed = {}
    for slot in BEHIND:
        relayed[slot] = pltpu.make_async_remote_copy(
            src_ref=first_from[slot],
            dst_ref=relay.at[pl.ds(FIRST_AT[slot] - 48, FIRST_LEN[slot]), :],
            send_sem=send_sem.at[slot],
            recv_sem=relay_sem.at[BEHIND.index(slot)],
            device_id=peer(-SLOTS[slot][0], 1 - RUN),
            device_id_type=MESH,
        )
    handed = pltpu.make_async_remote_copy(
        src_ref=relay,
        dst_ref=halo.at[pl.ds(48, RELAY_LEN), :],
        send_sem=forward_sem.at[0],
        recv_sem=forward_sem.at[1],
        device_id=peer(0, RUN - 2),
        device_id_type=MESH,
    )
    onward = {}
    for slot in (4, 5, 6, 7):
        side_s, side_c = SLOTS[slot]
        onward[slot] = pltpu.make_async_remote_copy(
            src_ref=halo.at[pl.ds(FIRST_AT[2 if side_s < 0 else 3], 16), :],
            dst_ref=halo.at[pl.ds(FIRST_AT[slot], 16), :],
            send_sem=send_sem.at[slot],
            recv_sem=recv_sem.at[slot],
            device_id=peer(0, -side_c),
            device_id_type=MESH,
        )
    for slot in BEHIND:
        when(relayed[slot].wait_recv, is_relay, at_s[SLOTS[slot][0]])
    when(handed.start, is_relay)

    when(sends[2].start, at_s[1])
    when(sends[3].start, at_s[-1])
    when(sends[1].start, at_c[-1], not_start)
    for slot in (4, 6, 0):
        when(sends[slot].start, is_last, at_s[-SLOTS[slot][0]])
    for slot in BEHIND:
        when(relayed[slot].start, is_start, at_s[-SLOTS[slot][0]])
    when(hear_ready, at_c[1], not_last)
    when(sends[0].start, at_c[1], not_last)

    def hand_on(turn):
        for source in (2, 3):
            side = SLOTS[source][0]
            when(sends[source].wait_recv, turn, at_s[side])
            for slot in (4, 5, 6, 7):
                side_s, side_c = SLOTS[slot]
                if side_s == side:
                    allowed = not_last if side_c < 0 else not_start
                    when(onward[slot].start, turn, at_s[side], at_c[-side_c], allowed)

    hand_on(not_last)

    for i in order[4:]:
        loads[i].wait()
    for m in range(M):
        modes3[m * 16 : m * 16 + CB, 0:M] = modes_third[m]
        modes12[m * 8 : m * 8 + AB, 0:M] = modes_first[m]
        modes12[m * 8 + 3 : m * 8 + 4, 64 : 64 + M] = modes_second[m]
    for a in range(AB):
        eigen[a : a + 1, 0:M] = eigen_first[a : a + 1, :]
        eigen[a : a + 1, 64 : 64 + M] = eigen_second[...]
    eigen[8 : 8 + CB, 0:M] = eigen_third[...]

    spread = (iota((128, WIDE), 0) == (iota((128, WIDE), 1) & 15)).astype(F32).astype(BF16)
    same = (iota((CB * M, WIDE), 0) & 15) == (iota((CB * M, WIDE), 1) >> 4)
    fore = []
    back = []
    node, box = iota((128, WIDE), 0), iota((128, WIDE), 1) >> 4
    stays = jnp.logical_or(
        (node >> 3) == box, jnp.logical_or((node & 7) == 0, (node & 7) == 7)
    )
    for part in split(modes3[...]):
        diagonal = jnp.where(same, dot(part, spread), 0.0).astype(BF16)
        moved = dot(table(0, 2)[:, : CB * M], diagonal)
        fore.append(moved.astype(BF16))
        back.append(jnp.where(stays, moved, 0.0).astype(BF16))

    modes_parts = jnp.concatenate(split(modes12[...]), axis=0)
    picked = lax.dot_general(
        pick[...], modes_parts, (((1,), (1,)), ((), ())), preferred_element_type=F32
    )
    at_block = block_of(iota((ROWS, WIDE), 0)) == (iota((ROWS, WIDE), 1) & 7)
    by_p = jnp.where(at_block, picked, 0.0).astype(BF16)
    by_q = picked.astype(BF16)
    forward = dot(by_p, jnp.concatenate([table(2, 3)] * 2, axis=0)) * dot(
        by_q, jnp.concatenate([table(5, 3)] * 2, axis=0)
    )
    own_split = split(forward[:, :OWN])
    halo_split = split(forward[:, OWN:])

    relative = (iota((ROWS, WIDE), 1) >> 3) + 2 - N1 * block_of(iota((ROWS, WIDE), 0))
    keep = jnp.logical_and(relative != 0, relative != 11)
    square = jnp.where(keep, forward[:, :WIDE], 0.0)
    square = jnp.concatenate([square, jnp.zeros((DEEP - ROWS, WIDE), F32)], axis=0)
    turned = jnp.transpose(square)
    for k in range(3):
        kept[k] = turned[:, k * 128 : (k + 1) * 128]

    def kept_rows(rows):
        return jnp.concatenate([kept[k, rows, :] for k in range(3)], axis=1)

    back_own = split(kept_rows(pl.ds(0, OWN)))
    back_edge = split(
        jnp.concatenate(
            [
                kept_rows(pl.ds(7, NF, stride=N1)),
                kept_rows(pl.ds(0, NF, stride=N1)),
                kept_rows(pl.ds(OWN - 8, 8)),
                kept_rows(pl.ds(0, 8)),
            ],
            axis=0,
        )
    )

    third_eigen = eigen[8 : 8 + CB, :]
    for shift in (16, 32, 64):
        third_eigen = third_eigen + pltpu.roll(third_eigen, shift, 1)
    third_eigen = jnp.concatenate([third_eigen, third_eigen], axis=1)
    own_box = iota((CB, WIDE), 0) == (iota((CB, WIDE), 1) >> 4)
    lane_part = jnp.sum(jnp.where(own_box, third_eigen, 0.0), axis=0, keepdims=True)
    inverse = []
    edges = [0, STEP, 2 * STEP, ROWS]
    for a in range(AB):
        rows = slice(edges[a], edges[a + 1])
        row_part = jnp.sum(
            pick[...].astype(F32)[rows] * eigen[a : a + 1, :], axis=1, keepdims=True
        )
        total = row_part + lane_part
        inverse.append(1.0 / jnp.where(total > 0.0, total, 1.0))
    inverse = jnp.concatenate(inverse, axis=0)

    own_third = wide_product(split(own[...]), fore)
    spectral_own = product(own_split, split(own_third))

    hand_on(is_last)
    for_each(range(4), -1, lambda slot: sends[slot].wait_send())
    for slot in (4, 5, 6, 7):
        side_s, side_c = SLOTS[slot]
        direct = is_last if side_c < 0 else is_start
        straight = both(at_s[-side_s], direct)
        passed = both(at_s[side_s], jnp.logical_and(at_c[-side_c], jnp.logical_not(direct)))
        when(sends[slot].wait_send, jnp.logical_or(straight, passed))
    for slot in (0, 1, 4, 5, 6, 7):
        arrives = not_last if slot in BEHIND else True
        when(sends[slot].wait_recv, there(*SLOTS[slot]), arrives)
    pl.when(is_last)(handed.wait_recv)
    halo_third = wide_product(split(halo[...]), fore)
    spectral = (spectral_own + product(halo_split, split(halo_third))) * inverse
    spectral = split(
        jnp.concatenate([spectral, jnp.zeros((DEEP - ROWS, WIDE), F32)], axis=0)
    )
    stage_last[...] = product_nt(split(product(back_edge, spectral)), back)
    last = {}
    for slot, (side_s, side_c) in enumerate(SLOTS):
        last[slot] = pltpu.make_async_remote_copy(
            src_ref=stage_last.at[pl.ds(LAST_FROM[slot], LAST_LEN[slot]), :],
            dst_ref=halo_last.at[pl.ds(LAST_AT[slot], LAST_LEN[slot]), :],
            send_sem=send_sem.at[slot],
            recv_sem=recv_last.at[slot],
            device_id=peer(-side_s, -side_c),
            device_id_type=MESH,
        )
    for_each(FAR_FIRST, -1, lambda slot: last[slot].start())

    sub = iota((8, 128), 0)

    def shifted(tile, to_top):
        moved = pltpu.roll(tile, 1 if to_top else 7, 0)
        return jnp.where(sub == (0 if to_top else 7), moved, 0.0)

    assembled[...] = own[...]
    for node, row in ((0, 24), (7, 48)):
        place = pl.ds(node, NF, stride=N1)
        assembled[place, :] = assembled[place, :] + halo[pl.ds(row, NF), :]

    def layer_beside(slot, at_prev, at_next, side):
        rows = 8 if side < 0 else 0
        base = halo[pl.ds(FIRST_AT[slot] + rows, 8), :]
        base = base + shifted(halo[pl.ds(FIRST_AT[at_prev] + rows, 8), :], True)
        return base + shifted(halo[pl.ds(FIRST_AT[at_next] + rows, 8), :], False)

    assembled[pl.ds(0, 8), :] = assembled[pl.ds(0, 8), :] + layer_beside(2, 4, 5, -1)
    assembled[pl.ds(OWN - 8, 8), :] = assembled[pl.ds(OWN - 8, 8), :] + layer_beside(3, 6, 7, 1)
    for a in range(AB - 1):
        at = (a * N1 + 7) * N1
        total = assembled[pl.ds(at, 8), :] + assembled[pl.ds(at + 8, 8), :]
        assembled[pl.ds(at, 8), :] = total
        assembled[pl.ds(at + 8, 8), :] = total
    value = assembled[...]
    lane = iota((OWN, 128), 1)
    from_left = jnp.where(jnp.logical_and((lane & 7) == 0, lane > 0), pltpu.roll(value, 1, 1), 0.0)
    from_right = jnp.where(
        jnp.logical_and((lane & 7) == 7, lane < 127), pltpu.roll(value, 127, 1), 0.0
    )
    op_ref[...] = (value + from_left + from_right).reshape(NF, N1, 128)

    solved[...] = product_nt(split(product(back_own, spectral)), back)

    for_each(range(8), 1, lambda slot: last[slot].wait_recv())
    for node, row in ((0, 0), (7, 24)):
        place = pl.ds(node, NF, stride=N1)
        solved[place, :] = solved[place, :] + halo_last[pl.ds(row, NF), :]

    def layer_last(slot, at_prev, at_next):
        base = halo_last[pl.ds(LAST_AT[slot], 8), :]
        base = base + shifted(halo_last[pl.ds(LAST_AT[at_prev], 8), :], True)
        return base + shifted(halo_last[pl.ds(LAST_AT[at_next], 8), :], False)

    solved[pl.ds(0, 8), :] = solved[pl.ds(0, 8), :] + layer_last(2, 4, 5)
    solved[pl.ds(OWN - 8, 8), :] = solved[pl.ds(OWN - 8, 8), :] + layer_last(3, 6, 7)
    pre_ref[...] = solved[...].reshape(NF, N1, 128)

    for_each(range(8), -1, lambda slot: last[slot].wait_send())
    pl.when(is_relay)(handed.wait_send)


def write_out(op_in, pre_in, op_out, pre_out, sem):
    copies = [
        pltpu.make_async_copy(source, target, sem.at[i])
        for i, (source, target) in enumerate(((op_in, op_out), (pre_in, pre_out)))
    ]
    for copy in copies:
        copy.start()
    for copy in copies:
        copy.wait()


def shards(*args):
    operands = list(args) + [jnp.asarray(t) for t in tables()]
    for i in (3, 4, 5):
        operands[i] = jnp.transpose(operands[i], (1, 0, 2))
    out = pltpu.VMEM((NF, N1, CB * N1), F32)
    held = pl.pallas_call(
        kernel,
        out_shape=(out, out),
        in_specs=[pl.BlockSpec(memory_space=pl.ANY)] * len(operands),
        out_specs=(pl.BlockSpec(memory_space=pltpu.VMEM),) * 2,
        scratch_shapes=[pltpu.VMEM(t.shape, t.dtype) for t in operands]
        + [
            pltpu.VMEM((OWN, 128), F32),
            pltpu.VMEM((96, 128), F32),
            pltpu.VMEM((HALO, 128), F32),
            pltpu.VMEM((64, 128), F32),
            pltpu.VMEM((96, 128), F32),
            pltpu.VMEM((OWN, 128), F32),
            pltpu.VMEM((OWN, 128), F32),
            pltpu.VMEM((3, WIDE, 128), F32),
            pltpu.VMEM((CB * M, 128), F32),
            pltpu.VMEM((128, 128), F32),
            pltpu.VMEM((32, 128), F32),
            pltpu.SemaphoreType.DMA((N_IN,)),
            pltpu.SemaphoreType.DMA((8,)),
            pltpu.SemaphoreType.DMA((8,)),
            pltpu.SemaphoreType.DMA((8,)),
            pltpu.VMEM((RELAY_LEN, 128), F32),
            pltpu.SemaphoreType.DMA((3,)),
            pltpu.SemaphoreType.DMA((2,)),
            pltpu.SemaphoreType.REGULAR,
        ],
        compiler_params=pltpu.CompilerParams(collective_id=0, has_side_effects=True),
        name="pressure_step",
    )(*operands)
    held = [pltpu.with_memory_space_constraint(value, pltpu.VMEM) for value in held]
    out = jax.ShapeDtypeStruct((NF, N1, CB * N1), F32)
    return pl.pallas_call(
        write_out,
        out_shape=(out, out),
        in_specs=[pl.BlockSpec(memory_space=pltpu.VMEM)] * 2,
        out_specs=(pl.BlockSpec(memory_space=pl.ANY),) * 2,
        scratch_shapes=[pltpu.SemaphoreType.DMA((2,))],
        name="write_out",
    )(*held)


def solution(mesh):
    in_specs = (
        P("stream", "cross", None),
        P(None, "stream", "cross", None),
        P(None, "stream", "cross", None),
        P("stream", None, None),
        P("cross", None, None),
        P(),
        P("stream", None),
        P("cross", None),
        P(),
    )
    out_specs = (P("stream", "cross", None), P("stream", "cross", None))
    return jax.shard_map(shards, mesh=mesh, in_specs=in_specs, out_specs=out_specs, check_vma=False)
```

```python
import functools

import jax
import jax.numpy as jnp
import numpy as np
from jax import lax
from jax.experimental import pallas as pl
from jax.experimental.pallas import tpu as pltpu
from jax.sharding import PartitionSpec as P

N1 = 8
M = 10
AB = 3
CB = 16
NF = AB * N1
OWN = NF * N1
HALO = 192
COLS = OWN + HALO
STEP = 104
ROWS = 320
DEEP = 384
WIDE = 256
F32 = jnp.float32
BF16 = jnp.bfloat16
MESH = pl.DeviceIdType.MESH
N_IN = 11
RUN = 8
BEHIND = (1, 5, 7)
RELAY_LEN = 80

SLOTS = ((0, -1), (0, 1), (-1, 0), (1, 0), (-1, -1), (-1, 1), (1, -1), (1, 1))
FIRST_AT = (0, 48, 128, 144, 160, 96, 176, 112)
FIRST_LEN = (48, 48, 16, 16, 16, 16, 16, 16)
LAST_AT = (0, 24, 48, 56, 64, 72, 80, 88)
LAST_LEN = (24, 24, 8, 8, 8, 8, 8, 8)
LAST_FROM = (0, 24, 48, 56, 48, 48, 56, 56)
FAR_FIRST = (4, 5, 6, 7, 0, 1, 2, 3)


def legendre_values(nodes, degree):
    table = np.zeros((nodes.shape[0], degree + 1))
    table[:, 0] = 1.0
    table[:, 1] = nodes
    for order in range(2, degree + 1):
        table[:, order] = (
            (2 * order - 1) * nodes * table[:, order - 1] - (order - 1) * table[:, order - 2]
        ) / order
    return table


def derivative_table(points):
    degree = points - 1
    nodes = np.cos(np.pi * np.arange(points) / degree)
    for sweep in range(100):
        table = legendre_values(nodes, degree)
        nodes = nodes - (nodes * table[:, degree] - table[:, degree - 1]) / (
            points * table[:, degree]
        )
    gll_nodes = nodes[::-1]
    legendre_at = legendre_values(gll_nodes, degree)[:, degree]
    diff_table = np.zeros((points, points))
    for first_index in range(points):
        for second_index in range(points):
            if first_index != second_index:
                diff_table[first_index, second_index] = legendre_at[first_index] / (
                    legendre_at[second_index] * (gll_nodes[first_index] - gll_nodes[second_index])
                )
    diff_table[0, 0] = -degree * (degree + 1) / 4.0
    diff_table[degree, degree] = degree * (degree + 1) / 4.0
    return diff_table


LAYER_NODE = [0, 1, 1, 2, 3, 4, 5, 6, 7, 8, 8, 9]


def halves(table):
    high = table.astype(BF16)
    return high, (table - high.astype(np.float32)).astype(BF16)


def tables():
    diff = derivative_table(N1).astype(np.float32)
    eye8 = np.eye(N1, dtype=np.float32)
    left = np.concatenate([np.kron(diff, eye8), np.kron(eye8, diff)], axis=0)
    high, low = halves(left)
    left_all = np.concatenate([high, high, low], axis=1)
    left_t = np.concatenate([high.T, low.T], axis=1)
    zero = np.zeros((CB * N1, CB * N1), BF16)
    thirds = []
    for matrix in (diff.T, diff):
        high, low = halves(np.kron(np.eye(CB, dtype=np.float32), matrix))
        thirds.append(np.block([[high, low], [high, zero]]))
    gather = np.zeros((CB * N1, CB * M), np.float32)
    for c in range(CB):
        for layer in range(12):
            at = c * N1 + layer - 2
            if 0 <= at < CB * N1:
                gather[at, LAYER_NODE[layer] * CB + c] = 1.0
    pick = np.zeros((ROWS, 128), np.float32)
    for a in range(AB):
        for p in range(M):
            for q in range(M):
                pick[a * STEP + p * M + q, p] = 1.0
                pick[a * STEP + p * M + q, 64 + q] = 1.0
    first_layer = np.zeros(COLS, np.int32)
    second_layer = np.full(COLS, -1, np.int32)
    for f in range(NF):
        for j in range(N1):
            first_layer[f * N1 + j] = f + 2
            second_layer[f * N1 + j] = j + 2
    for slot, (side_s, side_c) in enumerate(SLOTS):
        for row in range(FIRST_LEN[slot]):
            col = OWN + FIRST_AT[slot] + row
            if side_s == 0:
                jj, f = divmod(row, NF)
                first_layer[col] = f + 2
                second_layer[col] = jj if side_c < 0 else 10 + jj
            else:
                l, j = divmod(row, N1)
                first_layer[col] = l if side_s < 0 else 26 + l
                if side_c == 0:
                    second_layer[col] = j + 2
                elif side_c < 0:
                    second_layer[col] = j - 6 if j >= 6 else -1
                else:
                    second_layer[col] = 10 + j if j < 2 else -1
    cols_first = np.zeros((128, COLS), np.float32)
    cols_second = np.zeros((128, COLS), np.float32)
    for col in range(COLS):
        for a in range(AB):
            layer = first_layer[col] - N1 * a
            if 0 <= layer < 12:
                cols_first[LAYER_NODE[layer] * 8 + a, col] = 1.0
        if second_layer[col] >= 0:
            cols_second[LAYER_NODE[second_layer[col]] * 8 + 3, col] = 1.0
    exact = [t.astype(BF16) for t in (gather, pick, cols_first, cols_second)]
    left_all = np.concatenate([left_all, np.zeros((128, 64), BF16)], axis=1)
    near = np.concatenate([left_all, left_t] + thirds, axis=0)
    gather, pick, cols_first, cols_second = exact
    gather = np.concatenate([gather, np.zeros((128, 96), BF16)], axis=1)
    wide = [t[:, k : k + 128] for t in (gather, cols_first, cols_second) for k in range(0, t.shape[1], 128)]
    return [near, np.concatenate([pick] + wide, axis=0)]


def dot(a, b):
    return lax.dot_general(a, b, (((1,), (0,)), ((), ())), preferred_element_type=F32)


def split(value):
    high = value.astype(BF16)
    return high, (value - high.astype(F32)).astype(BF16)


def product(a, b):
    rows = a[0].shape[0]
    both = dot(jnp.concatenate(a, axis=0), b[0])
    return both[:rows] + (both[rows:] + dot(a[0], b[1]))


def lane_product(a, table):
    both = dot(jnp.concatenate(a, axis=1), table)
    return both[:, :128] + both[:, 128:]


def wide_product(a, b):
    return dot(jnp.concatenate(a, axis=1), jnp.concatenate([b[0], b[0]], axis=0)) + dot(a[0], b[1])


def dot_nt(a, b):
    return lax.dot_general(a, b, (((1,), (1,)), ((), ())), preferred_element_type=F32)


def product_nt(a, b):
    rows = a[0].shape[0]
    both = dot_nt(jnp.concatenate(a, axis=0), b[0])
    return both[:rows] + (both[rows:] + dot_nt(a[0], b[1]))


def iota(shape, dimension):
    return lax.broadcasted_iota(jnp.int32, shape, dimension)


def block_of(rows):
    return (rows >= STEP).astype(jnp.int32) + (rows >= 2 * STEP).astype(jnp.int32)


def kernel(*refs):
    hbm = refs[:N_IN]
    op_ref, pre_ref = refs[N_IN : N_IN + 2]
    vmem = refs[N_IN + 2 : 2 * N_IN + 2]
    (
        own,
        stage,
        halo,
        stage_last,
        halo_last,
        assembled,
        solved,
        kept,
        modes3,
        modes12,
        eigen,
        load_sem,
        send_sem,
        recv_sem,
        recv_last,
        relay,
        relay_sem,
        forward_sem,
        ready_sem,
    ) = refs[2 * N_IN + 2 :]
    (
        pressure,
        geo_diag,
        geo_off,
        modes_first,
        modes_second,
        modes_third,
        eigen_first,
        eigen_second,
        eigen_third,
        near,
        far,
    ) = vmem
    left, left_t = near.at[0:128, 0:192], near.at[128:192, :]
    third, third_t = near.at[192:448, :], near.at[448:704, :]
    pick = far.at[0:ROWS, :]

    def table(first, count):
        parts = [far[ROWS + 128 * k : ROWS + 128 * (k + 1), :] for k in range(first, first + count)]
        return jnp.concatenate(parts, axis=1)

    n_s, n_c = lax.axis_size("stream"), lax.axis_size("cross")
    me_s, me_c = lax.axis_index("stream"), lax.axis_index("cross")

    def peer(side_s, side_c):
        return {
            "stream": lax.rem(me_s + side_s + n_s, n_s),
            "cross": lax.rem(me_c + side_c + n_c, n_c),
        }

    at_s = {-1: me_s > 0, 0: True, 1: me_s < n_s - 1}
    at_c = {-1: me_c > 0, 0: True, 1: me_c < n_c - 1}

    is_last = jnp.logical_and(lax.rem(me_c, RUN) == RUN - 1, me_c < n_c - 1)
    is_start = jnp.logical_and(lax.rem(me_c, RUN) == 0, me_c > 0)
    is_relay = jnp.logical_and(lax.rem(me_c, RUN) == 0, me_c + RUN < n_c)

    def there(side_s, side_c):
        if side_s == 0:
            return at_c[side_c]
        if side_c == 0:
            return at_s[side_s]
        return jnp.logical_and(at_s[side_s], at_c[side_c])

    def both(first, second):
        return second if first is True else jnp.logical_and(first, second)

    def when(act, *conditions):
        pl.when(functools.reduce(both, conditions, True))(act)

    def for_each(order, sign, act):
        for slot in order:
            side_s, side_c = SLOTS[slot]
            when(functools.partial(act, slot), there(sign * side_s, sign * side_c))

    not_last = jnp.logical_not(is_last)
    not_start = jnp.logical_not(is_start)

    halo[...] = jnp.zeros_like(halo)
    halo_last[...] = jnp.zeros_like(halo_last)
    relay[...] = jnp.zeros_like(relay)
    barrier = pltpu.get_barrier_semaphore()

    def greet(side_s, side_c):
        pl.semaphore_signal(barrier, inc=1, device_id=peer(side_s, side_c), device_id_type=MESH)

    def hello(side_s, side_c, *conditions):
        when(functools.partial(greet, side_s, side_c), at_s[side_s], *conditions)

    hello(0, RUN - 1, is_relay)
    hello(-1, 0)
    hello(1, 0)
    hello(0, 1, at_c[1], not_last)
    for side_s in (0, -1, 1):
        hello(side_s, -1, is_start)
        hello(side_s, RUN, is_relay)
    count_s = at_s[-1].astype(jnp.int32) + at_s[1].astype(jnp.int32)
    neighbours = (
        count_s
        + jnp.logical_and(at_c[-1], not_start).astype(jnp.int32)
        + (1 + count_s) * jnp.logical_or(is_last, is_start).astype(jnp.int32)
        + is_last.astype(jnp.int32)
    )
    loads = [
        pltpu.make_async_copy(hbm[i], vmem[i], load_sem.at[i]) for i in range(N_IN)
    ]
    order = [0, 9, 1, 2, 5, 3, 4, 10, 6, 7, 8]
    for i in order:
        loads[i].start()

    modes3[...] = jnp.zeros_like(modes3)
    modes12[...] = jnp.zeros_like(modes12)
    eigen[...] = jnp.zeros_like(eigen)

    loads[0].wait()

    def say_ready(kind):
        to = peer(0, (-1, 1 - RUN)[kind])
        pl.semaphore_signal(ready_sem.at[kind], inc=1, device_id=to, device_id_type=MESH)

    def hear_ready(kind):
        pl.semaphore_wait(ready_sem.at[kind], 1)

    pl.semaphore_wait(barrier, neighbours)
    when(functools.partial(say_ready, 1), is_last)
    when(functools.partial(say_ready, 0), at_c[-1], not_start)
    loads[9].wait()
    pres = split(pressure[...].reshape(OWN, 128))
    per = N1 * N1
    along = []
    for a in range(AB):
        high, low = (part[a * per : (a + 1) * per] for part in pres)
        along.append(dot(left[...], jnp.concatenate([high, low, high], axis=0)))
    grad_third = lane_product(pres, third[...])
    for i in (1, 2):
        loads[i].wait()
    for a in range(AB):
        rows = pl.ds(a * N1, N1)
        d0, d1, d2 = (geo_diag[k, rows].reshape(per, 128) for k in range(3))
        o0, o1, o2 = (geo_off[k, rows].reshape(per, 128) for k in range(3))
        g1, g2 = along[a][:per], along[a][per:]
        g3 = grad_third[a * per : (a + 1) * per]
        flux_first = d0 * g1 + o0 * g2 + o1 * g3
        flux_second = o0 * g1 + d1 * g2 + o2 * g3
        flux_third = o1 * g1 + o2 * g2 + d2 * g3
        high, low = split(jnp.concatenate([flux_first, flux_second], axis=0))
        own[pl.ds(a * per, per), :] = (
            dot(left_t[...], jnp.concatenate([high, high], axis=0))
            + dot(left_t[:, :128], low)
            + lane_product(split(flux_third), third_t[...])
        )
    for k, node in enumerate((6, 7, 0, 1)):
        stage[pl.ds(k * NF, NF), :] = own[pl.ds(node, NF, stride=N1), :]

    first_from = (
        stage.at[pl.ds(0, 48), :],
        stage.at[pl.ds(48, 48), :],
        own.at[pl.ds(OWN - 16, 16), :],
        own.at[pl.ds(0, 16), :],
        own.at[pl.ds(OWN - 16, 16), :],
        own.at[pl.ds(OWN - 16, 16), :],
        own.at[pl.ds(0, 16), :],
        own.at[pl.ds(0, 16), :],
    )
    sends = {}
    for slot, (side_s, side_c) in enumerate(SLOTS):
        sends[slot] = pltpu.make_async_remote_copy(
            src_ref=first_from[slot],
            dst_ref=halo.at[pl.ds(FIRST_AT[slot], FIRST_LEN[slot]), :],
            send_sem=send_sem.at[slot],
            recv_sem=recv_sem.at[slot],
            device_id=peer(-side_s, -side_c),
            device_id_type=MESH,
        )
    relayed = {}
    for slot in BEHIND:
        relayed[slot] = pltpu.make_async_remote_copy(
            src_ref=first_from[slot],
            dst_ref=relay.at[pl.ds(FIRST_AT[slot] - 48, FIRST_LEN[slot]), :],
            send_sem=send_sem.at[slot],
            recv_sem=relay_sem.at[BEHIND.index(slot)],
            device_id=peer(-SLOTS[slot][0], -RUN),
            device_id_type=MESH,
        )
    handed = pltpu.make_async_remote_copy(
        src_ref=relay,
        dst_ref=halo.at[pl.ds(48, RELAY_LEN), :],
        send_sem=forward_sem.at[0],
        recv_sem=forward_sem.at[1],
        device_id=peer(0, RUN - 1),
        device_id_type=MESH,
    )
    onward = {}
    for slot in (4, 5, 6, 7):
        side_s, side_c = SLOTS[slot]
        onward[slot] = pltpu.make_async_remote_copy(
            src_ref=halo.at[pl.ds(FIRST_AT[2 if side_s < 0 else 3], 16), :],
            dst_ref=halo.at[pl.ds(FIRST_AT[slot], 16), :],
            send_sem=send_sem.at[slot],
            recv_sem=recv_sem.at[slot],
            device_id=peer(0, -side_c),
            device_id_type=MESH,
        )
    when(sends[2].start, at_s[1])
    when(sends[3].start, at_s[-1])
    when(sends[1].start, at_c[-1], not_start)
    for slot in (4, 6, 0):
        when(sends[slot].start, is_last, at_s[-SLOTS[slot][0]])
    for slot in BEHIND:
        when(relayed[slot].start, is_start, at_s[-SLOTS[slot][0]])
    when(functools.partial(hear_ready, 0), at_c[1], not_last)
    when(sends[0].start, at_c[1], not_last)

    def hand_on(turn):
        for source in (2, 3):
            side = SLOTS[source][0]
            when(sends[source].wait_recv, turn, at_s[side])
            for slot in (4, 5, 6, 7):
                side_s, side_c = SLOTS[slot]
                if side_s == side:
                    allowed = not_last if side_c < 0 else not_start
                    when(onward[slot].start, turn, at_s[side], at_c[-side_c], allowed)

    hand_on(not_last)
    for slot in BEHIND:
        when(relayed[slot].wait_recv, is_relay, at_s[SLOTS[slot][0]])
    when(functools.partial(hear_ready, 1), is_relay)
    when(handed.start, is_relay)

    for i in order[4:]:
        loads[i].wait()
    for m in range(M):
        modes3[m * 16 : m * 16 + CB, 0:M] = modes_third[m]
        modes12[m * 8 : m * 8 + AB, 0:M] = modes_first[m]
        modes12[m * 8 + 3 : m * 8 + 4, 64 : 64 + M] = modes_second[m]
    for a in range(AB):
        eigen[a : a + 1, 0:M] = eigen_first[a : a + 1, :]
        eigen[a : a + 1, 64 : 64 + M] = eigen_second[...]
    eigen[8 : 8 + CB, 0:M] = eigen_third[...]

    spread = (iota((128, WIDE), 0) == (iota((128, WIDE), 1) & 15)).astype(F32).astype(BF16)
    same = (iota((CB * M, WIDE), 0) & 15) == (iota((CB * M, WIDE), 1) >> 4)
    fore = []
    back = []
    node, box = iota((128, WIDE), 0), iota((128, WIDE), 1) >> 4
    stays = jnp.logical_or(
        (node >> 3) == box, jnp.logical_or((node & 7) == 0, (node & 7) == 7)
    )
    for part in split(modes3[...]):
        diagonal = jnp.where(same, dot(part, spread), 0.0).astype(BF16)
        moved = dot(table(0, 2)[:, : CB * M], diagonal)
        fore.append(moved.astype(BF16))
        back.append(jnp.where(stays, moved, 0.0).astype(BF16))

    modes_parts = jnp.concatenate(split(modes12[...]), axis=0)
    picked = lax.dot_general(
        pick[...], modes_parts, (((1,), (1,)), ((), ())), preferred_element_type=F32
    )
    at_block = block_of(iota((ROWS, WIDE), 0)) == (iota((ROWS, WIDE), 1) & 7)
    by_p = jnp.where(at_block, picked, 0.0).astype(BF16)
    by_q = picked.astype(BF16)
    forward = dot(by_p, jnp.concatenate([table(2, 3)] * 2, axis=0)) * dot(
        by_q, jnp.concatenate([table(5, 3)] * 2, axis=0)
    )
    own_split = split(forward[:, :OWN])
    halo_split = split(forward[:, OWN:])

    relative = (iota((ROWS, WIDE), 1) >> 3) + 2 - N1 * block_of(iota((ROWS, WIDE), 0))
    keep = jnp.logical_and(relative != 0, relative != 11)
    square = jnp.where(keep, forward[:, :WIDE], 0.0)
    square = jnp.concatenate([square, jnp.zeros((DEEP - ROWS, WIDE), F32)], axis=0)
    turned = jnp.transpose(square)
    for k in range(3):
        kept[k] = turned[:, k * 128 : (k + 1) * 128]

    def kept_rows(rows):
        return jnp.concatenate([kept[k, rows, :] for k in range(3)], axis=1)

    back_own = split(kept_rows(pl.ds(0, OWN)))
    back_edge = split(
        jnp.concatenate(
            [
                kept_rows(pl.ds(7, NF, stride=N1)),
                kept_rows(pl.ds(0, NF, stride=N1)),
                kept_rows(pl.ds(OWN - 8, 8)),
                kept_rows(pl.ds(0, 8)),
            ],
            axis=0,
        )
    )

    third_eigen = eigen[8 : 8 + CB, :]
    for shift in (16, 32, 64):
        third_eigen = third_eigen + pltpu.roll(third_eigen, shift, 1)
    third_eigen = jnp.concatenate([third_eigen, third_eigen], axis=1)
    own_box = iota((CB, WIDE), 0) == (iota((CB, WIDE), 1) >> 4)
    lane_part = jnp.sum(jnp.where(own_box, third_eigen, 0.0), axis=0, keepdims=True)
    inverse = []
    edges = [0, STEP, 2 * STEP, ROWS]
    for a in range(AB):
        rows = slice(edges[a], edges[a + 1])
        row_part = jnp.sum(
            pick[...].astype(F32)[rows] * eigen[a : a + 1, :], axis=1, keepdims=True
        )
        total = row_part + lane_part
        inverse.append(1.0 / jnp.where(total > 0.0, total, 1.0))
    inverse = jnp.concatenate(inverse, axis=0)

    own_third = wide_product(split(own[...]), fore)
    spectral_own = product(own_split, split(own_third))

    hand_on(is_last)
    for_each(range(4), -1, lambda slot: sends[slot].wait_send())
    for slot in (4, 5, 6, 7):
        side_s, side_c = SLOTS[slot]
        direct = is_last if side_c < 0 else is_start
        straight = both(at_s[-side_s], direct)
        passed = both(at_s[side_s], jnp.logical_and(at_c[-side_c], jnp.logical_not(direct)))
        when(sends[slot].wait_send, jnp.logical_or(straight, passed))
    for slot in (0, 1, 4, 5, 6, 7):
        arrives = not_last if slot in BEHIND else True
        when(sends[slot].wait_recv, there(*SLOTS[slot]), arrives)
    pl.when(is_last)(handed.wait_recv)
    halo_third = wide_product(split(halo[...]), fore)
    spectral = (spectral_own + product(halo_split, split(halo_third))) * inverse
    spectral = split(
        jnp.concatenate([spectral, jnp.zeros((DEEP - ROWS, WIDE), F32)], axis=0)
    )
    stage_last[...] = product_nt(split(product(back_edge, spectral)), back)
    last = {}
    for slot, (side_s, side_c) in enumerate(SLOTS):
        last[slot] = pltpu.make_async_remote_copy(
            src_ref=stage_last.at[pl.ds(LAST_FROM[slot], LAST_LEN[slot]), :],
            dst_ref=halo_last.at[pl.ds(LAST_AT[slot], LAST_LEN[slot]), :],
            send_sem=send_sem.at[slot],
            recv_sem=recv_last.at[slot],
            device_id=peer(-side_s, -side_c),
            device_id_type=MESH,
        )
    for_each(FAR_FIRST, -1, lambda slot: last[slot].start())

    sub = iota((8, 128), 0)

    def shifted(tile, to_top):
        moved = pltpu.roll(tile, 1 if to_top else 7, 0)
        return jnp.where(sub == (0 if to_top else 7), moved, 0.0)

    assembled[...] = own[...]
    for node, row in ((0, 24), (7, 48)):
        place = pl.ds(node, NF, stride=N1)
        assembled[place, :] = assembled[place, :] + halo[pl.ds(row, NF), :]

    def layer_beside(slot, at_prev, at_next, side):
        rows = 8 if side < 0 else 0
        base = halo[pl.ds(FIRST_AT[slot] + rows, 8), :]
        base = base + shifted(halo[pl.ds(FIRST_AT[at_prev] + rows, 8), :], True)
        return base + shifted(halo[pl.ds(FIRST_AT[at_next] + rows, 8), :], False)

    assembled[pl.ds(0, 8), :] = assembled[pl.ds(0, 8), :] + layer_beside(2, 4, 5, -1)
    assembled[pl.ds(OWN - 8, 8), :] = assembled[pl.ds(OWN - 8, 8), :] + layer_beside(3, 6, 7, 1)
    for a in range(AB - 1):
        at = (a * N1 + 7) * N1
        total = assembled[pl.ds(at, 8), :] + assembled[pl.ds(at + 8, 8), :]
        assembled[pl.ds(at, 8), :] = total
        assembled[pl.ds(at + 8, 8), :] = total
    value = assembled[...]
    lane = iota((OWN, 128), 1)
    from_left = jnp.where(jnp.logical_and((lane & 7) == 0, lane > 0), pltpu.roll(value, 1, 1), 0.0)
    from_right = jnp.where(
        jnp.logical_and((lane & 7) == 7, lane < 127), pltpu.roll(value, 127, 1), 0.0
    )
    op_ref[...] = (value + from_left + from_right).reshape(NF, N1, 128)

    solved[...] = product_nt(split(product(back_own, spectral)), back)

    for_each(range(8), 1, lambda slot: last[slot].wait_recv())
    for node, row in ((0, 0), (7, 24)):
        place = pl.ds(node, NF, stride=N1)
        solved[place, :] = solved[place, :] + halo_last[pl.ds(row, NF), :]

    def layer_last(slot, at_prev, at_next):
        base = halo_last[pl.ds(LAST_AT[slot], 8), :]
        base = base + shifted(halo_last[pl.ds(LAST_AT[at_prev], 8), :], True)
        return base + shifted(halo_last[pl.ds(LAST_AT[at_next], 8), :], False)

    solved[pl.ds(0, 8), :] = solved[pl.ds(0, 8), :] + layer_last(2, 4, 5)
    solved[pl.ds(OWN - 8, 8), :] = solved[pl.ds(OWN - 8, 8), :] + layer_last(3, 6, 7)
    pre_ref[...] = solved[...].reshape(NF, N1, 128)

    for_each(range(8), -1, lambda slot: last[slot].wait_send())
    pl.when(is_relay)(handed.wait_send)


def write_out(op_in, pre_in, op_out, pre_out, sem):
    copies = [
        pltpu.make_async_copy(source, target, sem.at[i])
        for i, (source, target) in enumerate(((op_in, op_out), (pre_in, pre_out)))
    ]
    for copy in copies:
        copy.start()
    for copy in copies:
        copy.wait()


def shards(*args):
    operands = list(args) + [jnp.asarray(t) for t in tables()]
    for i in (3, 4, 5):
        operands[i] = jnp.transpose(operands[i], (1, 0, 2))
    out = pltpu.VMEM((NF, N1, CB * N1), F32)
    held = pl.pallas_call(
        kernel,
        out_shape=(out, out),
        in_specs=[pl.BlockSpec(memory_space=pl.ANY)] * len(operands),
        out_specs=(pl.BlockSpec(memory_space=pltpu.VMEM),) * 2,
        scratch_shapes=[pltpu.VMEM(t.shape, t.dtype) for t in operands]
        + [
            pltpu.VMEM((OWN, 128), F32),
            pltpu.VMEM((96, 128), F32),
            pltpu.VMEM((HALO, 128), F32),
            pltpu.VMEM((64, 128), F32),
            pltpu.VMEM((96, 128), F32),
            pltpu.VMEM((OWN, 128), F32),
            pltpu.VMEM((OWN, 128), F32),
            pltpu.VMEM((3, WIDE, 128), F32),
            pltpu.VMEM((CB * M, 128), F32),
            pltpu.VMEM((128, 128), F32),
            pltpu.VMEM((32, 128), F32),
            pltpu.SemaphoreType.DMA((N_IN,)),
            pltpu.SemaphoreType.DMA((8,)),
            pltpu.SemaphoreType.DMA((8,)),
            pltpu.SemaphoreType.DMA((8,)),
            pltpu.VMEM((RELAY_LEN, 128), F32),
            pltpu.SemaphoreType.DMA((3,)),
            pltpu.SemaphoreType.DMA((2,)),
            pltpu.SemaphoreType.REGULAR((2,)),
        ],
        compiler_params=pltpu.CompilerParams(collective_id=0, has_side_effects=True),
        name="pressure_step",
    )(*operands)
    held = [pltpu.with_memory_space_constraint(value, pltpu.VMEM) for value in held]
    out = jax.ShapeDtypeStruct((NF, N1, CB * N1), F32)
    return pl.pallas_call(
        write_out,
        out_shape=(out, out),
        in_specs=[pl.BlockSpec(memory_space=pltpu.VMEM)] * 2,
        out_specs=(pl.BlockSpec(memory_space=pl.ANY),) * 2,
        scratch_shapes=[pltpu.SemaphoreType.DMA((2,))],
        name="write_out",
    )(*held)


def solution(mesh):
    in_specs = (
        P("stream", "cross", None),
        P(None, "stream", "cross", None),
        P(None, "stream", "cross", None),
        P("stream", None, None),
        P("cross", None, None),
        P(),
        P("stream", None),
        P("cross", None),
        P(),
    )
    out_specs = (P("stream", "cross", None), P("stream", "cross", None))
    return jax.shard_map(shards, mesh=mesh, in_specs=in_specs, out_specs=out_specs, check_vma=False)
```

```python
import functools

import jax
import jax.numpy as jnp
import numpy as np
from jax import lax
from jax.experimental import pallas as pl
from jax.experimental.pallas import tpu as pltpu
from jax.sharding import PartitionSpec as P

N1 = 8
M = 10
AB = 3
CB = 16
NF = AB * N1
OWN = NF * N1
HALO = 192
COLS = OWN + HALO
STEP = 104
ROWS = 320
DEEP = 384
WIDE = 256
F32 = jnp.float32
BF16 = jnp.bfloat16
MESH = pl.DeviceIdType.MESH
N_IN = 11
RUN = 8
BEHIND = (1, 5, 7)
RELAY_LEN = 80

SLOTS = ((0, -1), (0, 1), (-1, 0), (1, 0), (-1, -1), (-1, 1), (1, -1), (1, 1))
FIRST_AT = (0, 48, 128, 144, 160, 96, 176, 112)
FIRST_LEN = (48, 48, 16, 16, 16, 16, 16, 16)
LAST_AT = (0, 24, 48, 56, 64, 72, 80, 88)
LAST_LEN = (24, 24, 8, 8, 8, 8, 8, 8)
LAST_FROM = (0, 24, 48, 56, 48, 48, 56, 56)
FAR_FIRST = (4, 5, 6, 7, 0, 1, 2, 3)


def legendre_values(nodes, degree):
    table = np.zeros((nodes.shape[0], degree + 1))
    table[:, 0] = 1.0
    table[:, 1] = nodes
    for order in range(2, degree + 1):
        table[:, order] = (
            (2 * order - 1) * nodes * table[:, order - 1] - (order - 1) * table[:, order - 2]
        ) / order
    return table


def derivative_table(points):
    degree = points - 1
    nodes = np.cos(np.pi * np.arange(points) / degree)
    for sweep in range(100):
        table = legendre_values(nodes, degree)
        nodes = nodes - (nodes * table[:, degree] - table[:, degree - 1]) / (
            points * table[:, degree]
        )
    gll_nodes = nodes[::-1]
    legendre_at = legendre_values(gll_nodes, degree)[:, degree]
    diff_table = np.zeros((points, points))
    for first_index in range(points):
        for second_index in range(points):
            if first_index != second_index:
                diff_table[first_index, second_index] = legendre_at[first_index] / (
                    legendre_at[second_index] * (gll_nodes[first_index] - gll_nodes[second_index])
                )
    diff_table[0, 0] = -degree * (degree + 1) / 4.0
    diff_table[degree, degree] = degree * (degree + 1) / 4.0
    return diff_table


LAYER_NODE = [0, 1, 1, 2, 3, 4, 5, 6, 7, 8, 8, 9]


def halves(table):
    high = table.astype(BF16)
    return high, (table - high.astype(np.float32)).astype(BF16)


def tables():
    diff = derivative_table(N1).astype(np.float32)
    eye8 = np.eye(N1, dtype=np.float32)
    left = np.concatenate([np.kron(diff, eye8), np.kron(eye8, diff)], axis=0)
    high, low = halves(left)
    left_all = np.concatenate([high, high, low], axis=1)
    left_t = np.concatenate([high.T, low.T], axis=1)
    zero = np.zeros((CB * N1, CB * N1), BF16)
    thirds = []
    for matrix in (diff.T, diff):
        high, low = halves(np.kron(np.eye(CB, dtype=np.float32), matrix))
        thirds.append(np.block([[high, low], [high, zero]]))
    gather = np.zeros((CB * N1, CB * M), np.float32)
    for c in range(CB):
        for layer in range(12):
            at = c * N1 + layer - 2
            if 0 <= at < CB * N1:
                gather[at, LAYER_NODE[layer] * CB + c] = 1.0
    pick = np.zeros((ROWS, 128), np.float32)
    for a in range(AB):
        for p in range(M):
            for q in range(M):
                pick[a * STEP + p * M + q, p] = 1.0
                pick[a * STEP + p * M + q, 64 + q] = 1.0
    first_layer = np.zeros(COLS, np.int32)
    second_layer = np.full(COLS, -1, np.int32)
    for f in range(NF):
        for j in range(N1):
            first_layer[f * N1 + j] = f + 2
            second_layer[f * N1 + j] = j + 2
    for slot, (side_s, side_c) in enumerate(SLOTS):
        for row in range(FIRST_LEN[slot]):
            col = OWN + FIRST_AT[slot] + row
            if side_s == 0:
                jj, f = divmod(row, NF)
                first_layer[col] = f + 2
                second_layer[col] = jj if side_c < 0 else 10 + jj
            else:
                l, j = divmod(row, N1)
                first_layer[col] = l if side_s < 0 else 26 + l
                if side_c == 0:
                    second_layer[col] = j + 2
                elif side_c < 0:
                    second_layer[col] = j - 6 if j >= 6 else -1
                else:
                    second_layer[col] = 10 + j if j < 2 else -1
    cols_first = np.zeros((128, COLS), np.float32)
    cols_second = np.zeros((128, COLS), np.float32)
    for col in range(COLS):
        for a in range(AB):
            layer = first_layer[col] - N1 * a
            if 0 <= layer < 12:
                cols_first[LAYER_NODE[layer] * 8 + a, col] = 1.0
        if second_layer[col] >= 0:
            cols_second[LAYER_NODE[second_layer[col]] * 8 + 3, col] = 1.0
    exact = [t.astype(BF16) for t in (gather, pick, cols_first, cols_second)]
    left_all = np.concatenate([left_all, np.zeros((128, 64), BF16)], axis=1)
    near = np.concatenate([left_all, left_t] + thirds, axis=0)
    gather, pick, cols_first, cols_second = exact
    gather = np.concatenate([gather, np.zeros((128, 96), BF16)], axis=1)
    wide = [t[:, k : k + 128] for t in (gather, cols_first, cols_second) for k in range(0, t.shape[1], 128)]
    return [near, np.concatenate([pick] + wide, axis=0)]


def dot(a, b):
    return lax.dot_general(a, b, (((1,), (0,)), ((), ())), preferred_element_type=F32)


def split(value):
    high = value.astype(BF16)
    return high, (value - high.astype(F32)).astype(BF16)


def product(a, b):
    rows = a[0].shape[0]
    both = dot(jnp.concatenate(a, axis=0), b[0])
    return both[:rows] + (both[rows:] + dot(a[0], b[1]))


def lane_product(a, table):
    both = dot(jnp.concatenate(a, axis=1), table)
    return both[:, :128] + both[:, 128:]


def wide_product(a, b):
    return dot(jnp.concatenate(a, axis=1), jnp.concatenate([b[0], b[0]], axis=0)) + dot(a[0], b[1])


def dot_nt(a, b):
    return lax.dot_general(a, b, (((1,), (1,)), ((), ())), preferred_element_type=F32)


def product_nt(a, b):
    rows = a[0].shape[0]
    both = dot_nt(jnp.concatenate(a, axis=0), b[0])
    return both[:rows] + (both[rows:] + dot_nt(a[0], b[1]))


def iota(shape, dimension):
    return lax.broadcasted_iota(jnp.int32, shape, dimension)


def block_of(rows):
    return (rows >= STEP).astype(jnp.int32) + (rows >= 2 * STEP).astype(jnp.int32)


def kernel(*refs):
    hbm = refs[:N_IN]
    op_ref, pre_ref = refs[N_IN : N_IN + 2]
    vmem = refs[N_IN + 2 : 2 * N_IN + 2]
    (
        own,
        stage,
        halo,
        stage_last,
        halo_last,
        assembled,
        solved,
        kept,
        modes3,
        modes12,
        eigen,
        load_sem,
        send_sem,
        recv_sem,
        send_last,
        recv_last,
        relay,
        relay_sem,
        forward_sem,
        ready_sem,
    ) = refs[2 * N_IN + 2 :]
    (
        pressure,
        geo_diag,
        geo_off,
        modes_first,
        modes_second,
        modes_third,
        eigen_first,
        eigen_second,
        eigen_third,
        near,
        far,
    ) = vmem
    left, left_t = near.at[0:128, 0:192], near.at[128:192, :]
    third, third_t = near.at[192:448, :], near.at[448:704, :]
    pick = far.at[0:ROWS, :]

    def table(first, count):
        parts = [far[ROWS + 128 * k : ROWS + 128 * (k + 1), :] for k in range(first, first + count)]
        return jnp.concatenate(parts, axis=1)

    n_s, n_c = lax.axis_size("stream"), lax.axis_size("cross")
    me_s, me_c = lax.axis_index("stream"), lax.axis_index("cross")

    def peer(side_s, side_c):
        return {
            "stream": lax.rem(me_s + side_s + n_s, n_s),
            "cross": lax.rem(me_c + side_c + n_c, n_c),
        }

    at_s = {-1: me_s > 0, 0: True, 1: me_s < n_s - 1}
    at_c = {-1: me_c > 0, 0: True, 1: me_c < n_c - 1}

    is_last = jnp.logical_and(lax.rem(me_c, RUN) == RUN - 1, me_c < n_c - 1)
    is_start = jnp.logical_and(lax.rem(me_c, RUN) == 0, me_c > 0)
    is_relay = jnp.logical_and(lax.rem(me_c, RUN) == 0, me_c + RUN < n_c)

    def there(side_s, side_c):
        if side_s == 0:
            return at_c[side_c]
        if side_c == 0:
            return at_s[side_s]
        return jnp.logical_and(at_s[side_s], at_c[side_c])

    def both(first, second):
        return second if first is True else jnp.logical_and(first, second)

    def when(act, *conditions):
        pl.when(functools.reduce(both, conditions, True))(act)

    def for_each(order, sign, act):
        for slot in order:
            side_s, side_c = SLOTS[slot]
            when(functools.partial(act, slot), there(sign * side_s, sign * side_c))

    not_last = jnp.logical_not(is_last)
    not_start = jnp.logical_not(is_start)

    halo[...] = jnp.zeros_like(halo)
    halo_last[...] = jnp.zeros_like(halo_last)
    relay[...] = jnp.zeros_like(relay)
    barrier = pltpu.get_barrier_semaphore()

    def greet(side_s, side_c):
        pl.semaphore_signal(barrier, inc=1, device_id=peer(side_s, side_c), device_id_type=MESH)

    def hello(side_s, side_c, *conditions):
        when(functools.partial(greet, side_s, side_c), at_s[side_s], *conditions)

    hello(0, RUN - 1, is_relay)
    hello(-1, 0)
    hello(1, 0)
    hello(0, 1, at_c[1], not_last)
    for side_s in (0, -1, 1):
        hello(side_s, -1, is_start)
        hello(side_s, RUN, is_relay)
    count_s = at_s[-1].astype(jnp.int32) + at_s[1].astype(jnp.int32)
    neighbours = (
        count_s
        + jnp.logical_and(at_c[-1], not_start).astype(jnp.int32)
        + (1 + count_s) * jnp.logical_or(is_last, is_start).astype(jnp.int32)
        + is_last.astype(jnp.int32)
    )
    loads = [
        pltpu.make_async_copy(hbm[i], vmem[i], load_sem.at[i]) for i in range(N_IN)
    ]
    order = [0, 9, 1, 2, 5, 3, 4, 10, 6, 7, 8]
    for i in order:
        loads[i].start()

    modes3[...] = jnp.zeros_like(modes3)
    modes12[...] = jnp.zeros_like(modes12)
    eigen[...] = jnp.zeros_like(eigen)

    loads[0].wait()

    def say_ready(kind):
        to = peer(0, (-1, 1 - RUN)[kind])
        pl.semaphore_signal(ready_sem.at[kind], inc=1, device_id=to, device_id_type=MESH)

    def hear_ready(kind):
        pl.semaphore_wait(ready_sem.at[kind], 1)

    pl.semaphore_wait(barrier, neighbours)
    when(functools.partial(say_ready, 1), is_last)
    when(functools.partial(say_ready, 0), at_c[-1], not_start)
    loads[9].wait()
    pres = split(pressure[...].reshape(OWN, 128))
    per = N1 * N1
    along = []
    for a in range(AB):
        high, low = (part[a * per : (a + 1) * per] for part in pres)
        along.append(dot(left[...], jnp.concatenate([high, low, high], axis=0)))
    grad_third = lane_product(pres, third[...])
    for i in (1, 2):
        loads[i].wait()
    for a in range(AB):
        rows = pl.ds(a * N1, N1)
        d0, d1, d2 = (geo_diag[k, rows].reshape(per, 128) for k in range(3))
        o0, o1, o2 = (geo_off[k, rows].reshape(per, 128) for k in range(3))
        g1, g2 = along[a][:per], along[a][per:]
        g3 = grad_third[a * per : (a + 1) * per]
        flux_first = d0 * g1 + o0 * g2 + o1 * g3
        flux_second = o0 * g1 + d1 * g2 + o2 * g3
        flux_third = o1 * g1 + o2 * g2 + d2 * g3
        high, low = split(jnp.concatenate([flux_first, flux_second], axis=0))
        own[pl.ds(a * per, per), :] = (
            dot(left_t[...], jnp.concatenate([high, high], axis=0))
            + dot(left_t[:, :128], low)
            + lane_product(split(flux_third), third_t[...])
        )
    for k, node in enumerate((6, 7, 0, 1)):
        stage[pl.ds(k * NF, NF), :] = own[pl.ds(node, NF, stride=N1), :]

    first_from = (
        stage.at[pl.ds(0, 48), :],
        stage.at[pl.ds(48, 48), :],
        own.at[pl.ds(OWN - 16, 16), :],
        own.at[pl.ds(0, 16), :],
        own.at[pl.ds(OWN - 16, 16), :],
        own.at[pl.ds(OWN - 16, 16), :],
        own.at[pl.ds(0, 16), :],
        own.at[pl.ds(0, 16), :],
    )
    sends = {}
    for slot, (side_s, side_c) in enumerate(SLOTS):
        sends[slot] = pltpu.make_async_remote_copy(
            src_ref=first_from[slot],
            dst_ref=halo.at[pl.ds(FIRST_AT[slot], FIRST_LEN[slot]), :],
            send_sem=send_sem.at[slot],
            recv_sem=recv_sem.at[slot],
            device_id=peer(-side_s, -side_c),
            device_id_type=MESH,
        )
    relayed = {}
    for slot in BEHIND:
        relayed[slot] = pltpu.make_async_remote_copy(
            src_ref=first_from[slot],
            dst_ref=relay.at[pl.ds(FIRST_AT[slot] - 48, FIRST_LEN[slot]), :],
            send_sem=send_sem.at[slot],
            recv_sem=relay_sem.at[BEHIND.index(slot)],
            device_id=peer(-SLOTS[slot][0], -RUN),
            device_id_type=MESH,
        )
    handed = pltpu.make_async_remote_copy(
        src_ref=relay,
        dst_ref=halo.at[pl.ds(48, RELAY_LEN), :],
        send_sem=forward_sem.at[0],
        recv_sem=forward_sem.at[1],
        device_id=peer(0, RUN - 1),
        device_id_type=MESH,
    )
    onward = {}
    for slot in (4, 5, 6, 7):
        side_s, side_c = SLOTS[slot]
        onward[slot] = pltpu.make_async_remote_copy(
            src_ref=halo.at[pl.ds(FIRST_AT[2 if side_s < 0 else 3], 16), :],
            dst_ref=halo.at[pl.ds(FIRST_AT[slot], 16), :],
            send_sem=send_sem.at[slot],
            recv_sem=recv_sem.at[slot],
            device_id=peer(0, -side_c),
            device_id_type=MESH,
        )
    when(sends[2].start, at_s[1])
    when(sends[3].start, at_s[-1])
    when(sends[1].start, at_c[-1], not_start)
    for slot in (4, 6, 0):
        when(sends[slot].start, is_last, at_s[-SLOTS[slot][0]])
    for slot in BEHIND:
        when(relayed[slot].start, is_start, at_s[-SLOTS[slot][0]])
    when(functools.partial(hear_ready, 0), at_c[1], not_last)
    when(sends[0].start, at_c[1], not_last)

    def hand_on(turn):
        for source in (2, 3):
            side = SLOTS[source][0]
            when(sends[source].wait_recv, turn, at_s[side])
            for slot in (4, 5, 6, 7):
                side_s, side_c = SLOTS[slot]
                if side_s == side:
                    allowed = not_last if side_c < 0 else not_start
                    when(onward[slot].start, turn, at_s[side], at_c[-side_c], allowed)

    hand_on(not_last)
    for slot in BEHIND:
        when(relayed[slot].wait_recv, is_relay, at_s[SLOTS[slot][0]])
    when(functools.partial(hear_ready, 1), is_relay)
    when(handed.start, is_relay)

    for i in order[4:]:
        loads[i].wait()
    for m in range(M):
        modes3[m * 16 : m * 16 + CB, 0:M] = modes_third[m]
        modes12[m * 8 : m * 8 + AB, 0:M] = modes_first[m]
        modes12[m * 8 + 3 : m * 8 + 4, 64 : 64 + M] = modes_second[m]
    for a in range(AB):
        eigen[a : a + 1, 0:M] = eigen_first[a : a + 1, :]
        eigen[a : a + 1, 64 : 64 + M] = eigen_second[...]
    eigen[8 : 8 + CB, 0:M] = eigen_third[...]

    spread = (iota((128, WIDE), 0) == (iota((128, WIDE), 1) & 15)).astype(F32).astype(BF16)
    same = (iota((CB * M, WIDE), 0) & 15) == (iota((CB * M, WIDE), 1) >> 4)
    fore = []
    back = []
    node, box = iota((128, WIDE), 0), iota((128, WIDE), 1) >> 4
    stays = jnp.logical_or(
        (node >> 3) == box, jnp.logical_or((node & 7) == 0, (node & 7) == 7)
    )
    for part in split(modes3[...]):
        diagonal = jnp.where(same, dot(part, spread), 0.0).astype(BF16)
        moved = dot(table(0, 2)[:, : CB * M], diagonal)
        fore.append(moved.astype(BF16))
        back.append(jnp.where(stays, moved, 0.0).astype(BF16))

    modes_parts = jnp.concatenate(split(modes12[...]), axis=0)
    picked = lax.dot_general(
        pick[...], modes_parts, (((1,), (1,)), ((), ())), preferred_element_type=F32
    )
    at_block = block_of(iota((ROWS, WIDE), 0)) == (iota((ROWS, WIDE), 1) & 7)
    by_p = jnp.where(at_block, picked, 0.0).astype(BF16)
    by_q = picked.astype(BF16)
    forward = dot(by_p, jnp.concatenate([table(2, 3)] * 2, axis=0)) * dot(
        by_q, jnp.concatenate([table(5, 3)] * 2, axis=0)
    )
    own_split = split(forward[:, :OWN])
    halo_split = split(forward[:, OWN:])

    relative = (iota((ROWS, WIDE), 1) >> 3) + 2 - N1 * block_of(iota((ROWS, WIDE), 0))
    keep = jnp.logical_and(relative != 0, relative != 11)
    square = jnp.where(keep, forward[:, :WIDE], 0.0)
    square = jnp.concatenate([square, jnp.zeros((DEEP - ROWS, WIDE), F32)], axis=0)
    turned = jnp.transpose(square)
    for k in range(3):
        kept[k] = turned[:, k * 128 : (k + 1) * 128]

    def kept_rows(rows):
        return jnp.concatenate([kept[k, rows, :] for k in range(3)], axis=1)

    back_own = split(kept_rows(pl.ds(0, OWN)))
    back_edge = split(
        jnp.concatenate(
            [
                kept_rows(pl.ds(7, NF, stride=N1)),
                kept_rows(pl.ds(0, NF, stride=N1)),
                kept_rows(pl.ds(OWN - 8, 8)),
                kept_rows(pl.ds(0, 8)),
            ],
            axis=0,
        )
    )

    third_eigen = eigen[8 : 8 + CB, :]
    for shift in (16, 32, 64):
        third_eigen = third_eigen + pltpu.roll(third_eigen, shift, 1)
    third_eigen = jnp.concatenate([third_eigen, third_eigen], axis=1)
    own_box = iota((CB, WIDE), 0) == (iota((CB, WIDE), 1) >> 4)
    lane_part = jnp.sum(jnp.where(own_box, third_eigen, 0.0), axis=0, keepdims=True)
    inverse = []
    edges = [0, STEP, 2 * STEP, ROWS]
    for a in range(AB):
        rows = slice(edges[a], edges[a + 1])
        row_part = jnp.sum(
            pick[...].astype(F32)[rows] * eigen[a : a + 1, :], axis=1, keepdims=True
        )
        total = row_part + lane_part
        inverse.append(1.0 / jnp.where(total > 0.0, total, 1.0))
    inverse = jnp.concatenate(inverse, axis=0)

    own_third = wide_product(split(own[...]), fore)
    spectral_own = product(own_split, split(own_third))

    hand_on(is_last)
    for slot in (0, 1, 4, 5, 6, 7):
        arrives = not_last if slot in BEHIND else True
        when(sends[slot].wait_recv, there(*SLOTS[slot]), arrives)
    pl.when(is_last)(handed.wait_recv)
    halo_third = wide_product(split(halo[...]), fore)
    spectral = (spectral_own + product(halo_split, split(halo_third))) * inverse
    spectral = split(
        jnp.concatenate([spectral, jnp.zeros((DEEP - ROWS, WIDE), F32)], axis=0)
    )
    stage_last[...] = product_nt(split(product(back_edge, spectral)), back)
    last = {}
    for slot, (side_s, side_c) in enumerate(SLOTS):
        last[slot] = pltpu.make_async_remote_copy(
            src_ref=stage_last.at[pl.ds(LAST_FROM[slot], LAST_LEN[slot]), :],
            dst_ref=halo_last.at[pl.ds(LAST_AT[slot], LAST_LEN[slot]), :],
            send_sem=send_last.at[slot],
            recv_sem=recv_last.at[slot],
            device_id=peer(-side_s, -side_c),
            device_id_type=MESH,
        )
    for_each(FAR_FIRST, -1, lambda slot: last[slot].start())

    sub = iota((8, 128), 0)

    def shifted(tile, to_top):
        moved = pltpu.roll(tile, 1 if to_top else 7, 0)
        return jnp.where(sub == (0 if to_top else 7), moved, 0.0)

    assembled[...] = own[...]
    for node, row in ((0, 24), (7, 48)):
        place = pl.ds(node, NF, stride=N1)
        assembled[place, :] = assembled[place, :] + halo[pl.ds(row, NF), :]

    def layer_beside(slot, at_prev, at_next, side):
        rows = 8 if side < 0 else 0
        base = halo[pl.ds(FIRST_AT[slot] + rows, 8), :]
        base = base + shifted(halo[pl.ds(FIRST_AT[at_prev] + rows, 8), :], True)
        return base + shifted(halo[pl.ds(FIRST_AT[at_next] + rows, 8), :], False)

    assembled[pl.ds(0, 8), :] = assembled[pl.ds(0, 8), :] + layer_beside(2, 4, 5, -1)
    assembled[pl.ds(OWN - 8, 8), :] = assembled[pl.ds(OWN - 8, 8), :] + layer_beside(3, 6, 7, 1)
    for a in range(AB - 1):
        at = (a * N1 + 7) * N1
        total = assembled[pl.ds(at, 8), :] + assembled[pl.ds(at + 8, 8), :]
        assembled[pl.ds(at, 8), :] = total
        assembled[pl.ds(at + 8, 8), :] = total
    value = assembled[...]
    lane = iota((OWN, 128), 1)
    from_left = jnp.where(jnp.logical_and((lane & 7) == 0, lane > 0), pltpu.roll(value, 1, 1), 0.0)
    from_right = jnp.where(
        jnp.logical_and((lane & 7) == 7, lane < 127), pltpu.roll(value, 127, 1), 0.0
    )
    op_ref[...] = (value + from_left + from_right).reshape(NF, N1, 128)

    solved[...] = product_nt(split(product(back_own, spectral)), back)

    for_each(range(8), 1, lambda slot: last[slot].wait_recv())
    for node, row in ((0, 0), (7, 24)):
        place = pl.ds(node, NF, stride=N1)
        solved[place, :] = solved[place, :] + halo_last[pl.ds(row, NF), :]

    def layer_last(slot, at_prev, at_next):
        base = halo_last[pl.ds(LAST_AT[slot], 8), :]
        base = base + shifted(halo_last[pl.ds(LAST_AT[at_prev], 8), :], True)
        return base + shifted(halo_last[pl.ds(LAST_AT[at_next], 8), :], False)

    solved[pl.ds(0, 8), :] = solved[pl.ds(0, 8), :] + layer_last(2, 4, 5)
    solved[pl.ds(OWN - 8, 8), :] = solved[pl.ds(OWN - 8, 8), :] + layer_last(3, 6, 7)
    pre_ref[...] = solved[...].reshape(NF, N1, 128)

    for_each(range(4), -1, lambda slot: sends[slot].wait_send())
    for slot in (4, 5, 6, 7):
        side_s, side_c = SLOTS[slot]
        direct = is_last if side_c < 0 else is_start
        straight = both(at_s[-side_s], direct)
        passed = both(at_s[side_s], jnp.logical_and(at_c[-side_c], jnp.logical_not(direct)))
        when(sends[slot].wait_send, jnp.logical_or(straight, passed))
    for_each(range(8), -1, lambda slot: last[slot].wait_send())
    pl.when(is_relay)(handed.wait_send)


def write_out(op_in, pre_in, op_out, pre_out, sem):
    copies = [
        pltpu.make_async_copy(source, target, sem.at[i])
        for i, (source, target) in enumerate(((op_in, op_out), (pre_in, pre_out)))
    ]
    for copy in copies:
        copy.start()
    for copy in copies:
        copy.wait()


def shards(*args):
    operands = list(args) + [jnp.asarray(t) for t in tables()]
    for i in (3, 4, 5):
        operands[i] = jnp.transpose(operands[i], (1, 0, 2))
    out = pltpu.VMEM((NF, N1, CB * N1), F32)
    held = pl.pallas_call(
        kernel,
        out_shape=(out, out),
        in_specs=[pl.BlockSpec(memory_space=pl.ANY)] * len(operands),
        out_specs=(pl.BlockSpec(memory_space=pltpu.VMEM),) * 2,
        scratch_shapes=[pltpu.VMEM(t.shape, t.dtype) for t in operands]
        + [
            pltpu.VMEM((OWN, 128), F32),
            pltpu.VMEM((96, 128), F32),
            pltpu.VMEM((HALO, 128), F32),
            pltpu.VMEM((64, 128), F32),
            pltpu.VMEM((96, 128), F32),
            pltpu.VMEM((OWN, 128), F32),
            pltpu.VMEM((OWN, 128), F32),
            pltpu.VMEM((3, WIDE, 128), F32),
            pltpu.VMEM((CB * M, 128), F32),
            pltpu.VMEM((128, 128), F32),
            pltpu.VMEM((32, 128), F32),
            pltpu.SemaphoreType.DMA((N_IN,)),
            pltpu.SemaphoreType.DMA((8,)),
            pltpu.SemaphoreType.DMA((8,)),
            pltpu.SemaphoreType.DMA((8,)),
            pltpu.SemaphoreType.DMA((8,)),
            pltpu.VMEM((RELAY_LEN, 128), F32),
            pltpu.SemaphoreType.DMA((3,)),
            pltpu.SemaphoreType.DMA((2,)),
            pltpu.SemaphoreType.REGULAR((2,)),
        ],
        compiler_params=pltpu.CompilerParams(collective_id=0, has_side_effects=True),
        name="pressure_step",
    )(*operands)
    held = [pltpu.with_memory_space_constraint(value, pltpu.VMEM) for value in held]
    out = jax.ShapeDtypeStruct((NF, N1, CB * N1), F32)
    return pl.pallas_call(
        write_out,
        out_shape=(out, out),
        in_specs=[pl.BlockSpec(memory_space=pltpu.VMEM)] * 2,
        out_specs=(pl.BlockSpec(memory_space=pl.ANY),) * 2,
        scratch_shapes=[pltpu.SemaphoreType.DMA((2,))],
        name="write_out",
    )(*held)


def solution(mesh):
    in_specs = (
        P("stream", "cross", None),
        P(None, "stream", "cross", None),
        P(None, "stream", "cross", None),
        P("stream", None, None),
        P("cross", None, None),
        P(),
        P("stream", None),
        P("cross", None),
        P(),
    )
    out_specs = (P("stream", "cross", None), P("stream", "cross", None))
    return jax.shard_map(shards, mesh=mesh, in_specs=in_specs, out_specs=out_specs, check_vma=False)
```

```python
import functools

import jax
import jax.numpy as jnp
import numpy as np
from jax import lax
from jax.experimental import pallas as pl
from jax.experimental.pallas import tpu as pltpu
from jax.sharding import PartitionSpec as P

N1 = 8
M = 10
AB = 3
CB = 16
NF = AB * N1
OWN = NF * N1
HALO = 192
COLS = OWN + HALO
STEP = 104
ROWS = 320
DEEP = 384
WIDE = 256
F32 = jnp.float32
BF16 = jnp.bfloat16
MESH = pl.DeviceIdType.MESH
N_IN = 11
RUN = 8
BEHIND = (1, 5, 7)
RELAY_LEN = 80

SLOTS = ((0, -1), (0, 1), (-1, 0), (1, 0), (-1, -1), (-1, 1), (1, -1), (1, 1))
FIRST_AT = (0, 48, 128, 144, 160, 96, 176, 112)
FIRST_LEN = (48, 48, 16, 16, 16, 16, 16, 16)
LAST_AT = (0, 24, 48, 56, 64, 72, 80, 88)
LAST_LEN = (24, 24, 8, 8, 8, 8, 8, 8)
LAST_FROM = (0, 24, 48, 56, 48, 48, 56, 56)
FAR_FIRST = (4, 5, 6, 7, 0, 1, 2, 3)


def legendre_values(nodes, degree):
    table = np.zeros((nodes.shape[0], degree + 1))
    table[:, 0] = 1.0
    table[:, 1] = nodes
    for order in range(2, degree + 1):
        table[:, order] = (
            (2 * order - 1) * nodes * table[:, order - 1] - (order - 1) * table[:, order - 2]
        ) / order
    return table


def derivative_table(points):
    degree = points - 1
    nodes = np.cos(np.pi * np.arange(points) / degree)
    for sweep in range(100):
        table = legendre_values(nodes, degree)
        nodes = nodes - (nodes * table[:, degree] - table[:, degree - 1]) / (
            points * table[:, degree]
        )
    gll_nodes = nodes[::-1]
    legendre_at = legendre_values(gll_nodes, degree)[:, degree]
    diff_table = np.zeros((points, points))
    for first_index in range(points):
        for second_index in range(points):
            if first_index != second_index:
                diff_table[first_index, second_index] = legendre_at[first_index] / (
                    legendre_at[second_index] * (gll_nodes[first_index] - gll_nodes[second_index])
                )
    diff_table[0, 0] = -degree * (degree + 1) / 4.0
    diff_table[degree, degree] = degree * (degree + 1) / 4.0
    return diff_table


LAYER_NODE = [0, 1, 1, 2, 3, 4, 5, 6, 7, 8, 8, 9]


def halves(table):
    high = table.astype(BF16)
    return high, (table - high.astype(np.float32)).astype(BF16)


def tables():
    diff = derivative_table(N1).astype(np.float32)
    eye8 = np.eye(N1, dtype=np.float32)
    left = np.concatenate([np.kron(diff, eye8), np.kron(eye8, diff)], axis=0)
    high, low = halves(left)
    left_all = np.concatenate([high, high, low], axis=1)
    left_t = np.concatenate([high.T, low.T], axis=1)
    zero = np.zeros((CB * N1, CB * N1), BF16)
    thirds = []
    for matrix in (diff.T, diff):
        high, low = halves(np.kron(np.eye(CB, dtype=np.float32), matrix))
        thirds.append(np.block([[high, low], [high, zero]]))
    gather = np.zeros((CB * N1, CB * M), np.float32)
    for c in range(CB):
        for layer in range(12):
            at = c * N1 + layer - 2
            if 0 <= at < CB * N1:
                gather[at, LAYER_NODE[layer] * CB + c] = 1.0
    pick = np.zeros((ROWS, 128), np.float32)
    for a in range(AB):
        for p in range(M):
            for q in range(M):
                pick[a * STEP + p * M + q, p] = 1.0
                pick[a * STEP + p * M + q, 64 + q] = 1.0
    first_layer = np.zeros(COLS, np.int32)
    second_layer = np.full(COLS, -1, np.int32)
    for f in range(NF):
        for j in range(N1):
            first_layer[f * N1 + j] = f + 2
            second_layer[f * N1 + j] = j + 2
    for slot, (side_s, side_c) in enumerate(SLOTS):
        for row in range(FIRST_LEN[slot]):
            col = OWN + FIRST_AT[slot] + row
            if side_s == 0:
                jj, f = divmod(row, NF)
                first_layer[col] = f + 2
                second_layer[col] = jj if side_c < 0 else 10 + jj
            else:
                l, j = divmod(row, N1)
                first_layer[col] = l if side_s < 0 else 26 + l
                if side_c == 0:
                    second_layer[col] = j + 2
                elif side_c < 0:
                    second_layer[col] = j - 6 if j >= 6 else -1
                else:
                    second_layer[col] = 10 + j if j < 2 else -1
    cols_first = np.zeros((128, COLS), np.float32)
    cols_second = np.zeros((128, COLS), np.float32)
    for col in range(COLS):
        for a in range(AB):
            layer = first_layer[col] - N1 * a
            if 0 <= layer < 12:
                cols_first[LAYER_NODE[layer] * 8 + a, col] = 1.0
        if second_layer[col] >= 0:
            cols_second[LAYER_NODE[second_layer[col]] * 8 + 3, col] = 1.0
    exact = [t.astype(BF16) for t in (gather, pick, cols_first, cols_second)]
    left_all = np.concatenate([left_all, np.zeros((128, 64), BF16)], axis=1)
    near = np.concatenate([left_all, left_t] + thirds, axis=0)
    gather, pick, cols_first, cols_second = exact
    gather = np.concatenate([gather, np.zeros((128, 96), BF16)], axis=1)
    wide = [t[:, k : k + 128] for t in (gather, cols_first, cols_second) for k in range(0, t.shape[1], 128)]
    return [near, np.concatenate([pick] + wide, axis=0)]


def dot(a, b):
    return lax.dot_general(a, b, (((1,), (0,)), ((), ())), preferred_element_type=F32)


def split(value):
    high = value.astype(BF16)
    return high, (value - high.astype(F32)).astype(BF16)


def product(a, b):
    rows = a[0].shape[0]
    half = rows // 32 * 16 or rows
    parts = []
    for begin, end in ((0, half), (half, rows)):
        if begin < end:
            high, low = a[0][begin:end], a[1][begin:end]
            both = dot(jnp.concatenate([high, low], axis=0), b[0])
            parts.append(both[: end - begin] + (both[end - begin :] + dot(high, b[1])))
    return jnp.concatenate(parts, axis=0)


def lane_product(a, table):
    both = dot(jnp.concatenate(a, axis=1), table)
    return both[:, :128] + both[:, 128:]


def wide_product(a, b):
    return dot(jnp.concatenate(a, axis=1), jnp.concatenate([b[0], b[0]], axis=0)) + dot(a[0], b[1])


def dot_nt(a, b):
    return lax.dot_general(a, b, (((1,), (1,)), ((), ())), preferred_element_type=F32)


def product_nt(a, b):
    rows = a[0].shape[0]
    both = dot_nt(jnp.concatenate(a, axis=0), b[0])
    return both[:rows] + (both[rows:] + dot_nt(a[0], b[1]))


def iota(shape, dimension):
    return lax.broadcasted_iota(jnp.int32, shape, dimension)


def block_of(rows):
    return (rows >= STEP).astype(jnp.int32) + (rows >= 2 * STEP).astype(jnp.int32)


def kernel(*refs):
    hbm = refs[:N_IN]
    op_ref, pre_ref = refs[N_IN : N_IN + 2]
    vmem = refs[N_IN + 2 : 2 * N_IN + 2]
    (
        own,
        stage,
        halo,
        stage_last,
        halo_last,
        assembled,
        solved,
        kept,
        modes3,
        modes12,
        eigen,
        load_sem,
        send_sem,
        recv_sem,
        send_last,
        recv_last,
        relay,
        relay_sem,
        forward_sem,
    ) = refs[2 * N_IN + 2 :]
    (
        pressure,
        geo_diag,
        geo_off,
        modes_first,
        modes_second,
        modes_third,
        eigen_first,
        eigen_second,
        eigen_third,
        near,
        far,
    ) = vmem
    left, left_t = near.at[0:128, 0:192], near.at[128:192, :]
    third, third_t = near.at[192:448, :], near.at[448:704, :]
    pick = far.at[0:ROWS, :]

    def table(first, count):
        parts = [far[ROWS + 128 * k : ROWS + 128 * (k + 1), :] for k in range(first, first + count)]
        return jnp.concatenate(parts, axis=1)

    n_s, n_c = lax.axis_size("stream"), lax.axis_size("cross")
    me_s, me_c = lax.axis_index("stream"), lax.axis_index("cross")

    def peer(side_s, side_c):
        return {
            "stream": lax.rem(me_s + side_s + n_s, n_s),
            "cross": lax.rem(me_c + side_c + n_c, n_c),
        }

    at_s = {-1: me_s > 0, 0: True, 1: me_s < n_s - 1}
    at_c = {-1: me_c > 0, 0: True, 1: me_c < n_c - 1}

    is_last = jnp.logical_and(lax.rem(me_c, RUN) == RUN - 1, me_c < n_c - 1)
    is_start = jnp.logical_and(lax.rem(me_c, RUN) == 0, me_c > 0)
    is_relay = jnp.logical_and(lax.rem(me_c, RUN) == 1, me_c + RUN - 1 < n_c)

    def both(first, second):
        return second if first is True else jnp.logical_and(first, second)

    def there(side_s, side_c):
        if side_s == 0:
            return at_c[side_c]
        if side_c == 0:
            return at_s[side_s]
        return jnp.logical_and(at_s[side_s], at_c[side_c])

    def for_each(order, sign, act):
        for slot in order:
            side_s, side_c = SLOTS[slot]
            pl.when(there(sign * side_s, sign * side_c))(functools.partial(act, slot))

    def to_relay(act):
        for slot in BEHIND:
            pl.when(both(at_s[-SLOTS[slot][0]], is_start))(functools.partial(act, slot))

    def at_relay(act):
        for slot in BEHIND:
            pl.when(both(at_s[SLOTS[slot][0]], is_relay))(functools.partial(act, slot))

    halo[...] = jnp.zeros_like(halo)
    halo_last[...] = jnp.zeros_like(halo_last)
    relay[...] = jnp.zeros_like(relay)
    barrier = pltpu.get_barrier_semaphore()

    def greet(side_s, side_c):
        pl.semaphore_signal(barrier, inc=1, device_id=peer(side_s, side_c), device_id_type=MESH)

    pl.when(is_last)(functools.partial(greet, 0, 2 - RUN))
    for side_s, side_c in SLOTS:
        here = there(side_s, side_c)
        if side_c > 0:
            here = jnp.logical_and(here, jnp.logical_not(is_last))
        pl.when(here)(functools.partial(greet, side_s, side_c))
    at_relay(lambda slot: greet(SLOTS[slot][0], RUN - 1))
    count_s = at_s[-1].astype(jnp.int32) + at_s[1].astype(jnp.int32)
    count_c = at_c[-1].astype(jnp.int32) + at_c[1].astype(jnp.int32)
    neighbours = count_s + count_c + count_s * count_c + is_relay.astype(jnp.int32)
    loads = [
        pltpu.make_async_copy(hbm[i], vmem[i], load_sem.at[i]) for i in range(N_IN)
    ]
    order = [0, 9, 1, 2, 5, 3, 4, 10, 6, 7, 8]
    for i in order:
        loads[i].start()

    modes3[...] = jnp.zeros_like(modes3)
    modes12[...] = jnp.zeros_like(modes12)
    eigen[...] = jnp.zeros_like(eigen)

    for i in (0, 9):
        loads[i].wait()
    pres = split(pressure[...].reshape(OWN, 128))
    per = N1 * N1
    along = []
    for a in range(AB):
        high, low = (part[a * per : (a + 1) * per] for part in pres)
        along.append(dot(left[...], jnp.concatenate([high, low, high], axis=0)))
    grad_third = lane_product(pres, third[...])
    for i in (1, 2):
        loads[i].wait()
    for a in range(AB):
        rows = pl.ds(a * N1, N1)
        d0, d1, d2 = (geo_diag[k, rows].reshape(per, 128) for k in range(3))
        o0, o1, o2 = (geo_off[k, rows].reshape(per, 128) for k in range(3))
        g1, g2 = along[a][:per], along[a][per:]
        g3 = grad_third[a * per : (a + 1) * per]
        flux_first = d0 * g1 + o0 * g2 + o1 * g3
        flux_second = o0 * g1 + d1 * g2 + o2 * g3
        flux_third = o1 * g1 + o2 * g2 + d2 * g3
        high, low = split(jnp.concatenate([flux_first, flux_second], axis=0))
        own[pl.ds(a * per, per), :] = (
            dot(left_t[...], jnp.concatenate([high, high], axis=0))
            + dot(left_t[:, :128], low)
            + lane_product(split(flux_third), third_t[...])
        )
    for k, node in enumerate((6, 7, 0, 1)):
        stage[pl.ds(k * NF, NF), :] = own[pl.ds(node, NF, stride=N1), :]

    pl.semaphore_wait(barrier, neighbours)
    first_from = (
        stage.at[pl.ds(0, 48), :],
        stage.at[pl.ds(48, 48), :],
        own.at[pl.ds(OWN - 16, 16), :],
        own.at[pl.ds(0, 16), :],
        own.at[pl.ds(OWN - 16, 16), :],
        own.at[pl.ds(OWN - 16, 16), :],
        own.at[pl.ds(0, 16), :],
        own.at[pl.ds(0, 16), :],
    )
    sends = {}
    for slot, (side_s, side_c) in enumerate(SLOTS):
        sends[slot] = pltpu.make_async_remote_copy(
            src_ref=first_from[slot],
            dst_ref=halo.at[pl.ds(FIRST_AT[slot], FIRST_LEN[slot]), :],
            send_sem=send_sem.at[slot],
            recv_sem=recv_sem.at[slot],
            device_id=peer(-side_s, -side_c),
            device_id_type=MESH,
        )
    relayed = {}
    for slot in BEHIND:
        relayed[slot] = pltpu.make_async_remote_copy(
            src_ref=first_from[slot],
            dst_ref=relay.at[pl.ds(FIRST_AT[slot] - 48, FIRST_LEN[slot]), :],
            send_sem=send_sem.at[slot],
            recv_sem=relay_sem.at[BEHIND.index(slot)],
            device_id=peer(-SLOTS[slot][0], 1 - RUN),
            device_id_type=MESH,
        )
    handed = pltpu.make_async_remote_copy(
        src_ref=relay,
        dst_ref=halo.at[pl.ds(48, RELAY_LEN), :],
        send_sem=forward_sem.at[0],
        recv_sem=forward_sem.at[1],
        device_id=peer(0, RUN - 2),
        device_id_type=MESH,
    )
    at_relay(lambda slot: relayed[slot].wait_recv())
    pl.when(is_relay)(handed.start)
    for slot in FAR_FIRST:
        side_s, side_c = SLOTS[slot]
        here = there(-side_s, -side_c)
        if slot in BEHIND:
            here = jnp.logical_and(here, jnp.logical_not(is_start))
        pl.when(here)(sends[slot].start)
    to_relay(lambda slot: relayed[slot].start())

    for i in order[4:]:
        loads[i].wait()
    for m in range(M):
        modes3[m * 16 : m * 16 + CB, 0:M] = modes_third[m]
        modes12[m * 8 : m * 8 + AB, 0:M] = modes_first[m]
        modes12[m * 8 + 3 : m * 8 + 4, 64 : 64 + M] = modes_second[m]
    for a in range(AB):
        eigen[a : a + 1, 0:M] = eigen_first[a : a + 1, :]
        eigen[a : a + 1, 64 : 64 + M] = eigen_second[...]
    eigen[8 : 8 + CB, 0:M] = eigen_third[...]

    spread = (iota((128, WIDE), 0) == (iota((128, WIDE), 1) & 15)).astype(F32).astype(BF16)
    same = (iota((CB * M, WIDE), 0) & 15) == (iota((CB * M, WIDE), 1) >> 4)
    fore = []
    back = []
    node, box = iota((128, WIDE), 0), iota((128, WIDE), 1) >> 4
    stays = jnp.logical_or(
        (node >> 3) == box, jnp.logical_or((node & 7) == 0, (node & 7) == 7)
    )
    for part in split(modes3[...]):
        diagonal = jnp.where(same, dot(part, spread), 0.0).astype(BF16)
        moved = dot(table(0, 2)[:, : CB * M], diagonal)
        fore.append(moved.astype(BF16))
        back.append(jnp.where(stays, moved, 0.0).astype(BF16))

    modes_parts = jnp.concatenate(split(modes12[...]), axis=0)
    picked = lax.dot_general(
        pick[...], modes_parts, (((1,), (1,)), ((), ())), preferred_element_type=F32
    )
    at_block = block_of(iota((ROWS, WIDE), 0)) == (iota((ROWS, WIDE), 1) & 7)
    by_p = jnp.where(at_block, picked, 0.0).astype(BF16)
    by_q = picked.astype(BF16)
    forward = dot(by_p, jnp.concatenate([table(2, 3)] * 2, axis=0)) * dot(
        by_q, jnp.concatenate([table(5, 3)] * 2, axis=0)
    )
    own_split = split(forward[:, :OWN])
    halo_split = split(forward[:, OWN:])

    relative = (iota((ROWS, WIDE), 1) >> 3) + 2 - N1 * block_of(iota((ROWS, WIDE), 0))
    keep = jnp.logical_and(relative != 0, relative != 11)
    square = jnp.where(keep, forward[:, :WIDE], 0.0)
    square = jnp.concatenate([square, jnp.zeros((DEEP - ROWS, WIDE), F32)], axis=0)
    turned = jnp.transpose(square)
    for k in range(3):
        kept[k] = turned[:, k * 128 : (k + 1) * 128]

    def kept_rows(rows):
        return jnp.concatenate([kept[k, rows, :] for k in range(3)], axis=1)

    back_own = split(kept_rows(pl.ds(0, OWN)))
    back_edge = split(
        jnp.concatenate(
            [
                kept_rows(pl.ds(7, NF, stride=N1)),
                kept_rows(pl.ds(0, NF, stride=N1)),
                kept_rows(pl.ds(OWN - 8, 8)),
                kept_rows(pl.ds(0, 8)),
            ],
            axis=0,
        )
    )

    third_eigen = eigen[8 : 8 + CB, :]
    for shift in (16, 32, 64):
        third_eigen = third_eigen + pltpu.roll(third_eigen, shift, 1)
    third_eigen = jnp.concatenate([third_eigen, third_eigen], axis=1)
    own_box = iota((CB, WIDE), 0) == (iota((CB, WIDE), 1) >> 4)
    lane_part = jnp.sum(jnp.where(own_box, third_eigen, 0.0), axis=0, keepdims=True)
    inverse = []
    edges = [0, STEP, 2 * STEP, ROWS]
    for a in range(AB):
        rows = slice(edges[a], edges[a + 1])
        row_part = jnp.sum(
            pick[...].astype(F32)[rows] * eigen[a : a + 1, :], axis=1, keepdims=True
        )
        total = row_part + lane_part
        inverse.append(1.0 / jnp.where(total > 0.0, total, 1.0))
    inverse = jnp.concatenate(inverse, axis=0)

    own_third = wide_product(split(own[...]), fore)
    spectral_own = product(own_split, split(own_third))

    for slot in range(8):
        here = there(*SLOTS[slot])
        if slot in BEHIND:
            here = jnp.logical_and(here, jnp.logical_not(is_last))
        pl.when(here)(sends[slot].wait_recv)
    pl.when(is_last)(handed.wait_recv)
    halo_third = wide_product(split(halo[...]), fore)
    spectral = (spectral_own + product(halo_split, split(halo_third))) * inverse
    spectral = split(
        jnp.concatenate([spectral, jnp.zeros((DEEP - ROWS, WIDE), F32)], axis=0)
    )
    stage_last[...] = product_nt(split(product(back_edge, spectral)), back)
    last = {}
    for slot, (side_s, side_c) in enumerate(SLOTS):
        last[slot] = pltpu.make_async_remote_copy(
            src_ref=stage_last.at[pl.ds(LAST_FROM[slot], LAST_LEN[slot]), :],
            dst_ref=halo_last.at[pl.ds(LAST_AT[slot], LAST_LEN[slot]), :],
            send_sem=send_last.at[slot],
            recv_sem=recv_last.at[slot],
            device_id=peer(-side_s, -side_c),
            device_id_type=MESH,
        )
    for_each(FAR_FIRST, -1, lambda slot: last[slot].start())

    sub = iota((8, 128), 0)

    def shifted(tile, to_top):
        moved = pltpu.roll(tile, 1 if to_top else 7, 0)
        return jnp.where(sub == (0 if to_top else 7), moved, 0.0)

    assembled[...] = own[...]
    for node, row in ((0, 24), (7, 48)):
        place = pl.ds(node, NF, stride=N1)
        assembled[place, :] = assembled[place, :] + halo[pl.ds(row, NF), :]

    def layer_beside(slot, at_prev, at_next, side):
        rows = 8 if side < 0 else 0
        base = halo[pl.ds(FIRST_AT[slot] + rows, 8), :]
        base = base + shifted(halo[pl.ds(FIRST_AT[at_prev] + rows, 8), :], True)
        return base + shifted(halo[pl.ds(FIRST_AT[at_next] + rows, 8), :], False)

    assembled[pl.ds(0, 8), :] = assembled[pl.ds(0, 8), :] + layer_beside(2, 4, 5, -1)
    assembled[pl.ds(OWN - 8, 8), :] = assembled[pl.ds(OWN - 8, 8), :] + layer_beside(3, 6, 7, 1)
    for a in range(AB - 1):
        at = (a * N1 + 7) * N1
        total = assembled[pl.ds(at, 8), :] + assembled[pl.ds(at + 8, 8), :]
        assembled[pl.ds(at, 8), :] = total
        assembled[pl.ds(at + 8, 8), :] = total
    value = assembled[...]
    lane = iota((OWN, 128), 1)
    from_left = jnp.where(jnp.logical_and((lane & 7) == 0, lane > 0), pltpu.roll(value, 1, 1), 0.0)
    from_right = jnp.where(
        jnp.logical_and((lane & 7) == 7, lane < 127), pltpu.roll(value, 127, 1), 0.0
    )
    op_ref[...] = (value + from_left + from_right).reshape(NF, N1, 128)

    solved[...] = product_nt(split(product(back_own, spectral)), back)

    for_each(range(8), 1, lambda slot: last[slot].wait_recv())
    for node, row in ((0, 0), (7, 24)):
        place = pl.ds(node, NF, stride=N1)
        solved[place, :] = solved[place, :] + halo_last[pl.ds(row, NF), :]

    def layer_last(slot, at_prev, at_next):
        base = halo_last[pl.ds(LAST_AT[slot], 8), :]
        base = base + shifted(halo_last[pl.ds(LAST_AT[at_prev], 8), :], True)
        return base + shifted(halo_last[pl.ds(LAST_AT[at_next], 8), :], False)

    solved[pl.ds(0, 8), :] = solved[pl.ds(0, 8), :] + layer_last(2, 4, 5)
    solved[pl.ds(OWN - 8, 8), :] = solved[pl.ds(OWN - 8, 8), :] + layer_last(3, 6, 7)
    pre_ref[...] = solved[...].reshape(NF, N1, 128)

    for_each(range(8), -1, lambda slot: sends[slot].wait_send())
    for_each(range(8), -1, lambda slot: last[slot].wait_send())
    pl.when(is_relay)(handed.wait_send)


def write_out(op_in, pre_in, op_out, pre_out, sem):
    copies = [
        pltpu.make_async_copy(source, target, sem.at[i])
        for i, (source, target) in enumerate(((op_in, op_out), (pre_in, pre_out)))
    ]
    for copy in copies:
        copy.start()
    for copy in copies:
        copy.wait()


def shards(*args):
    operands = list(args) + [jnp.asarray(t) for t in tables()]
    for i in (3, 4, 5):
        operands[i] = jnp.transpose(operands[i], (1, 0, 2))
    out = pltpu.VMEM((NF, N1, CB * N1), F32)
    held = pl.pallas_call(
        kernel,
        out_shape=(out, out),
        in_specs=[pl.BlockSpec(memory_space=pl.ANY)] * len(operands),
        out_specs=(pl.BlockSpec(memory_space=pltpu.VMEM),) * 2,
        scratch_shapes=[pltpu.VMEM(t.shape, t.dtype) for t in operands]
        + [
            pltpu.VMEM((OWN, 128), F32),
            pltpu.VMEM((96, 128), F32),
            pltpu.VMEM((HALO, 128), F32),
            pltpu.VMEM((64, 128), F32),
            pltpu.VMEM((96, 128), F32),
            pltpu.VMEM((OWN, 128), F32),
            pltpu.VMEM((OWN, 128), F32),
            pltpu.VMEM((3, WIDE, 128), F32),
            pltpu.VMEM((CB * M, 128), F32),
            pltpu.VMEM((128, 128), F32),
            pltpu.VMEM((32, 128), F32),
            pltpu.SemaphoreType.DMA((N_IN,)),
            pltpu.SemaphoreType.DMA((8,)),
            pltpu.SemaphoreType.DMA((8,)),
            pltpu.SemaphoreType.DMA((8,)),
            pltpu.SemaphoreType.DMA((8,)),
            pltpu.VMEM((RELAY_LEN, 128), F32),
            pltpu.SemaphoreType.DMA((3,)),
            pltpu.SemaphoreType.DMA((2,)),
        ],
        compiler_params=pltpu.CompilerParams(collective_id=0, has_side_effects=True),
        name="pressure_step",
    )(*operands)
    held = [pltpu.with_memory_space_constraint(value, pltpu.VMEM) for value in held]
    out = jax.ShapeDtypeStruct((NF, N1, CB * N1), F32)
    return pl.pallas_call(
        write_out,
        out_shape=(out, out),
        in_specs=[pl.BlockSpec(memory_space=pltpu.VMEM)] * 2,
        out_specs=(pl.BlockSpec(memory_space=pl.ANY),) * 2,
        scratch_shapes=[pltpu.SemaphoreType.DMA((2,))],
        name="write_out",
    )(*held)


def solution(mesh):
    in_specs = (
        P("stream", "cross", None),
        P(None, "stream", "cross", None),
        P(None, "stream", "cross", None),
        P("stream", None, None),
        P("cross", None, None),
        P(),
        P("stream", None),
        P("cross", None),
        P(),
    )
    out_specs = (P("stream", "cross", None), P("stream", "cross", None))
    return jax.shard_map(shards, mesh=mesh, in_specs=in_specs, out_specs=out_specs, check_vma=False)
```

```python
import functools

import jax
import jax.numpy as jnp
import numpy as np
from jax import lax
from jax.experimental import pallas as pl
from jax.experimental.pallas import tpu as pltpu
from jax.sharding import PartitionSpec as P

N1 = 8
M = 10
AB = 3
CB = 16
NF = AB * N1
OWN = NF * N1
HALO = 192
COLS = OWN + HALO
STEP = 104
ROWS = 320
DEEP = 384
WIDE = 256
F32 = jnp.float32
BF16 = jnp.bfloat16
MESH = pl.DeviceIdType.MESH
N_IN = 11
RUN = 8
BEHIND = (1, 5, 7)
RELAY_LEN = 80

SLOTS = ((0, -1), (0, 1), (-1, 0), (1, 0), (-1, -1), (-1, 1), (1, -1), (1, 1))
FIRST_AT = (0, 48, 128, 144, 160, 96, 176, 112)
FIRST_LEN = (48, 48, 16, 16, 16, 16, 16, 16)
LAST_AT = (0, 24, 48, 56, 64, 72, 80, 88)
LAST_LEN = (24, 24, 8, 8, 8, 8, 8, 8)
LAST_FROM = (0, 24, 48, 56, 48, 48, 56, 56)
FAR_FIRST = (4, 5, 6, 7, 0, 1, 2, 3)


def legendre_values(nodes, degree):
    table = np.zeros((nodes.shape[0], degree + 1))
    table[:, 0] = 1.0
    table[:, 1] = nodes
    for order in range(2, degree + 1):
        table[:, order] = (
            (2 * order - 1) * nodes * table[:, order - 1] - (order - 1) * table[:, order - 2]
        ) / order
    return table


def derivative_table(points):
    degree = points - 1
    nodes = np.cos(np.pi * np.arange(points) / degree)
    for sweep in range(100):
        table = legendre_values(nodes, degree)
        nodes = nodes - (nodes * table[:, degree] - table[:, degree - 1]) / (
            points * table[:, degree]
        )
    gll_nodes = nodes[::-1]
    legendre_at = legendre_values(gll_nodes, degree)[:, degree]
    diff_table = np.zeros((points, points))
    for first_index in range(points):
        for second_index in range(points):
            if first_index != second_index:
                diff_table[first_index, second_index] = legendre_at[first_index] / (
                    legendre_at[second_index] * (gll_nodes[first_index] - gll_nodes[second_index])
                )
    diff_table[0, 0] = -degree * (degree + 1) / 4.0
    diff_table[degree, degree] = degree * (degree + 1) / 4.0
    return diff_table


LAYER_NODE = [0, 1, 1, 2, 3, 4, 5, 6, 7, 8, 8, 9]


def halves(table):
    high = table.astype(BF16)
    return high, (table - high.astype(np.float32)).astype(BF16)


def tables():
    diff = derivative_table(N1).astype(np.float32)
    eye8 = np.eye(N1, dtype=np.float32)
    left = np.concatenate([np.kron(diff, eye8), np.kron(eye8, diff)], axis=0)
    high, low = halves(left)
    left_all = np.concatenate([high, high, low], axis=1)
    left_t = np.concatenate([high.T, low.T], axis=1)
    zero = np.zeros((CB * N1, CB * N1), BF16)
    thirds = []
    for matrix in (diff.T, diff):
        high, low = halves(np.kron(np.eye(CB, dtype=np.float32), matrix))
        thirds.append(np.block([[high, low], [high, zero]]))
    gather = np.zeros((CB * N1, CB * M), np.float32)
    for c in range(CB):
        for layer in range(12):
            at = c * N1 + layer - 2
            if 0 <= at < CB * N1:
                gather[at, LAYER_NODE[layer] * CB + c] = 1.0
    pick = np.zeros((ROWS, 128), np.float32)
    for a in range(AB):
        for p in range(M):
            for q in range(M):
                pick[a * STEP + p * M + q, p] = 1.0
                pick[a * STEP + p * M + q, 64 + q] = 1.0
    first_layer = np.zeros(COLS, np.int32)
    second_layer = np.full(COLS, -1, np.int32)
    for f in range(NF):
        for j in range(N1):
            first_layer[f * N1 + j] = f + 2
            second_layer[f * N1 + j] = j + 2
    for slot, (side_s, side_c) in enumerate(SLOTS):
        for row in range(FIRST_LEN[slot]):
            col = OWN + FIRST_AT[slot] + row
            if side_s == 0:
                jj, f = divmod(row, NF)
                first_layer[col] = f + 2
                second_layer[col] = jj if side_c < 0 else 10 + jj
            else:
                l, j = divmod(row, N1)
                first_layer[col] = l if side_s < 0 else 26 + l
                if side_c == 0:
                    second_layer[col] = j + 2
                elif side_c < 0:
                    second_layer[col] = j - 6 if j >= 6 else -1
                else:
                    second_layer[col] = 10 + j if j < 2 else -1
    cols_first = np.zeros((128, COLS), np.float32)
    cols_second = np.zeros((128, COLS), np.float32)
    for col in range(COLS):
        for a in range(AB):
            layer = first_layer[col] - N1 * a
            if 0 <= layer < 12:
                cols_first[LAYER_NODE[layer] * 8 + a, col] = 1.0
        if second_layer[col] >= 0:
            cols_second[LAYER_NODE[second_layer[col]] * 8 + 3, col] = 1.0
    exact = [t.astype(BF16) for t in (gather, pick, cols_first, cols_second)]
    left_all = np.concatenate([left_all, np.zeros((128, 64), BF16)], axis=1)
    near = np.concatenate([left_all, left_t] + thirds, axis=0)
    gather, pick, cols_first, cols_second = exact
    gather = np.concatenate([gather, np.zeros((128, 96), BF16)], axis=1)
    wide = [t[:, k : k + 128] for t in (gather, cols_first, cols_second) for k in range(0, t.shape[1], 128)]
    return [near, np.concatenate([pick] + wide, axis=0)]


def dot(a, b):
    return lax.dot_general(a, b, (((1,), (0,)), ((), ())), preferred_element_type=F32)


def split(value):
    high = value.astype(BF16)
    return high, (value - high.astype(F32)).astype(BF16)


def product(a, b):
    rows = a[0].shape[0]
    half = rows // 32 * 16 or rows
    parts = []
    for begin, end in ((0, half), (half, rows)):
        if begin < end:
            high, low = a[0][begin:end], a[1][begin:end]
            both = dot(jnp.concatenate([high, low], axis=0), b[0])
            parts.append(both[: end - begin] + (both[end - begin :] + dot(high, b[1])))
    return jnp.concatenate(parts, axis=0)


def lane_product(a, table):
    both = dot(jnp.concatenate(a, axis=1), table)
    return both[:, :128] + both[:, 128:]


def wide_product(a, b):
    return dot(jnp.concatenate(a, axis=1), jnp.concatenate([b[0], b[0]], axis=0)) + dot(a[0], b[1])


def dot_nt(a, b):
    return lax.dot_general(a, b, (((1,), (1,)), ((), ())), preferred_element_type=F32)


def product_nt(a, b):
    rows = a[0].shape[0]
    half = rows // 32 * 16
    parts = []
    for begin, end in ((0, half), (half, rows)):
        high, low = a[0][begin:end], a[1][begin:end]
        both = dot_nt(jnp.concatenate([high, low], axis=0), b[0])
        parts.append(both[: end - begin] + (both[end - begin :] + dot_nt(high, b[1])))
    return jnp.concatenate(parts, axis=0)


def iota(shape, dimension):
    return lax.broadcasted_iota(jnp.int32, shape, dimension)


def block_of(rows):
    return (rows >= STEP).astype(jnp.int32) + (rows >= 2 * STEP).astype(jnp.int32)


def kernel(*refs):
    hbm = refs[:N_IN]
    op_ref, pre_ref = refs[N_IN : N_IN + 2]
    vmem = refs[N_IN + 2 : 2 * N_IN + 2]
    (
        own,
        stage,
        halo,
        stage_last,
        halo_last,
        assembled,
        solved,
        kept,
        modes3,
        modes12,
        eigen,
        load_sem,
        send_sem,
        recv_sem,
        send_last,
        recv_last,
        relay,
        relay_sem,
        forward_sem,
    ) = refs[2 * N_IN + 2 :]
    (
        pressure,
        geo_diag,
        geo_off,
        modes_first,
        modes_second,
        modes_third,
        eigen_first,
        eigen_second,
        eigen_third,
        near,
        far,
    ) = vmem
    left, left_t = near.at[0:128, 0:192], near.at[128:192, :]
    third, third_t = near.at[192:448, :], near.at[448:704, :]
    pick = far.at[0:ROWS, :]

    def table(first, count):
        parts = [far[ROWS + 128 * k : ROWS + 128 * (k + 1), :] for k in range(first, first + count)]
        return jnp.concatenate(parts, axis=1)

    n_s, n_c = lax.axis_size("stream"), lax.axis_size("cross")
    me_s, me_c = lax.axis_index("stream"), lax.axis_index("cross")

    def peer(side_s, side_c):
        return {
            "stream": lax.rem(me_s + side_s + n_s, n_s),
            "cross": lax.rem(me_c + side_c + n_c, n_c),
        }

    at_s = {-1: me_s > 0, 0: True, 1: me_s < n_s - 1}
    at_c = {-1: me_c > 0, 0: True, 1: me_c < n_c - 1}

    is_last = jnp.logical_and(lax.rem(me_c, RUN) == RUN - 1, me_c < n_c - 1)
    is_start = jnp.logical_and(lax.rem(me_c, RUN) == 0, me_c > 0)
    is_relay = jnp.logical_and(lax.rem(me_c, RUN) == 1, me_c + RUN - 1 < n_c)

    def both(first, second):
        return second if first is True else jnp.logical_and(first, second)

    def there(side_s, side_c):
        if side_s == 0:
            return at_c[side_c]
        if side_c == 0:
            return at_s[side_s]
        return jnp.logical_and(at_s[side_s], at_c[side_c])

    def for_each(order, sign, act):
        for slot in order:
            side_s, side_c = SLOTS[slot]
            pl.when(there(sign * side_s, sign * side_c))(functools.partial(act, slot))

    def to_relay(act):
        for slot in BEHIND:
            pl.when(both(at_s[-SLOTS[slot][0]], is_start))(functools.partial(act, slot))

    def at_relay(act):
        for slot in BEHIND:
            pl.when(both(at_s[SLOTS[slot][0]], is_relay))(functools.partial(act, slot))

    halo[...] = jnp.zeros_like(halo)
    halo_last[...] = jnp.zeros_like(halo_last)
    relay[...] = jnp.zeros_like(relay)
    barrier = pltpu.get_barrier_semaphore()

    def greet(side_s, side_c):
        pl.semaphore_signal(barrier, inc=1, device_id=peer(side_s, side_c), device_id_type=MESH)

    pl.when(is_last)(functools.partial(greet, 0, 2 - RUN))
    for side_s, side_c in SLOTS[4:] + SLOTS[:4]:
        here = there(side_s, side_c)
        if side_c > 0:
            here = jnp.logical_and(here, jnp.logical_not(is_last))
        pl.when(here)(functools.partial(greet, side_s, side_c))
    at_relay(lambda slot: greet(SLOTS[slot][0], RUN - 1))
    count_s = at_s[-1].astype(jnp.int32) + at_s[1].astype(jnp.int32)
    count_c = at_c[-1].astype(jnp.int32) + at_c[1].astype(jnp.int32)
    neighbours = count_s + count_c + count_s * count_c + is_relay.astype(jnp.int32)
    loads = [
        pltpu.make_async_copy(hbm[i], vmem[i], load_sem.at[i]) for i in range(N_IN)
    ]
    order = [0, 9, 1, 2, 5, 3, 4, 10, 6, 7, 8]
    for i in order:
        loads[i].start()

    modes3[...] = jnp.zeros_like(modes3)
    modes12[...] = jnp.zeros_like(modes12)
    eigen[...] = jnp.zeros_like(eigen)

    for i in (0, 9):
        loads[i].wait()
    pres = split(pressure[...].reshape(OWN, 128))
    per = N1 * N1
    along = []
    for a in range(AB):
        high, low = (part[a * per : (a + 1) * per] for part in pres)
        along.append(dot(left[...], jnp.concatenate([high, low, high], axis=0)))
    grad_third = lane_product(pres, third[...])
    for i in (1, 2):
        loads[i].wait()
    for a in range(AB):
        rows = pl.ds(a * N1, N1)
        d0, d1, d2 = (geo_diag[k, rows].reshape(per, 128) for k in range(3))
        o0, o1, o2 = (geo_off[k, rows].reshape(per, 128) for k in range(3))
        g1, g2 = along[a][:per], along[a][per:]
        g3 = grad_third[a * per : (a + 1) * per]
        flux_first = d0 * g1 + o0 * g2 + o1 * g3
        flux_second = o0 * g1 + d1 * g2 + o2 * g3
        flux_third = o1 * g1 + o2 * g2 + d2 * g3
        high, low = split(jnp.concatenate([flux_first, flux_second], axis=0))
        own[pl.ds(a * per, per), :] = (
            dot(left_t[...], jnp.concatenate([high, high], axis=0))
            + dot(left_t[:, :128], low)
            + lane_product(split(flux_third), third_t[...])
        )
    for k, node in enumerate((6, 7, 0, 1)):
        stage[pl.ds(k * NF, NF), :] = own[pl.ds(node, NF, stride=N1), :]

    pl.semaphore_wait(barrier, neighbours)
    first_from = (
        stage.at[pl.ds(0, 48), :],
        stage.at[pl.ds(48, 48), :],
        own.at[pl.ds(OWN - 16, 16), :],
        own.at[pl.ds(0, 16), :],
        own.at[pl.ds(OWN - 16, 16), :],
        own.at[pl.ds(OWN - 16, 16), :],
        own.at[pl.ds(0, 16), :],
        own.at[pl.ds(0, 16), :],
    )
    sends = {}
    for slot, (side_s, side_c) in enumerate(SLOTS):
        sends[slot] = pltpu.make_async_remote_copy(
            src_ref=first_from[slot],
            dst_ref=halo.at[pl.ds(FIRST_AT[slot], FIRST_LEN[slot]), :],
            send_sem=send_sem.at[slot],
            recv_sem=recv_sem.at[slot],
            device_id=peer(-side_s, -side_c),
            device_id_type=MESH,
        )
    relayed = {}
    for slot in BEHIND:
        relayed[slot] = pltpu.make_async_remote_copy(
            src_ref=first_from[slot],
            dst_ref=relay.at[pl.ds(FIRST_AT[slot] - 48, FIRST_LEN[slot]), :],
            send_sem=send_sem.at[slot],
            recv_sem=relay_sem.at[BEHIND.index(slot)],
            device_id=peer(-SLOTS[slot][0], 1 - RUN),
            device_id_type=MESH,
        )
    handed = pltpu.make_async_remote_copy(
        src_ref=relay,
        dst_ref=halo.at[pl.ds(48, RELAY_LEN), :],
        send_sem=forward_sem.at[0],
        recv_sem=forward_sem.at[1],
        device_id=peer(0, RUN - 2),
        device_id_type=MESH,
    )
    at_relay(lambda slot: relayed[slot].wait_recv())
    pl.when(is_relay)(handed.start)
    for slot in FAR_FIRST:
        side_s, side_c = SLOTS[slot]
        here = there(-side_s, -side_c)
        if slot in BEHIND:
            here = jnp.logical_and(here, jnp.logical_not(is_start))
        pl.when(here)(sends[slot].start)
    to_relay(lambda slot: relayed[slot].start())

    for i in order[4:]:
        loads[i].wait()
    for m in range(M):
        modes3[m * 16 : m * 16 + CB, 0:M] = modes_third[m]
        modes12[m * 8 : m * 8 + AB, 0:M] = modes_first[m]
        modes12[m * 8 + 3 : m * 8 + 4, 64 : 64 + M] = modes_second[m]
    for a in range(AB):
        eigen[a : a + 1, 0:M] = eigen_first[a : a + 1, :]
        eigen[a : a + 1, 64 : 64 + M] = eigen_second[...]
    eigen[8 : 8 + CB, 0:M] = eigen_third[...]

    spread = (iota((128, WIDE), 0) == (iota((128, WIDE), 1) & 15)).astype(F32).astype(BF16)
    same = (iota((CB * M, WIDE), 0) & 15) == (iota((CB * M, WIDE), 1) >> 4)
    fore = []
    back = []
    node, box = iota((128, WIDE), 0), iota((128, WIDE), 1) >> 4
    stays = jnp.logical_or(
        (node >> 3) == box, jnp.logical_or((node & 7) == 0, (node & 7) == 7)
    )
    for part in split(modes3[...]):
        diagonal = jnp.where(same, dot(part, spread), 0.0).astype(BF16)
        moved = dot(table(0, 2)[:, : CB * M], diagonal)
        fore.append(moved.astype(BF16))
        back.append(jnp.where(stays, moved, 0.0).astype(BF16))

    modes_parts = jnp.concatenate(split(modes12[...]), axis=0)
    picked = lax.dot_general(
        pick[...], modes_parts, (((1,), (1,)), ((), ())), preferred_element_type=F32
    )
    at_block = block_of(iota((ROWS, WIDE), 0)) == (iota((ROWS, WIDE), 1) & 7)
    by_p = jnp.where(at_block, picked, 0.0).astype(BF16)
    by_q = picked.astype(BF16)
    forward = dot(by_p, jnp.concatenate([table(2, 3)] * 2, axis=0)) * dot(
        by_q, jnp.concatenate([table(5, 3)] * 2, axis=0)
    )
    own_split = split(forward[:, :OWN])
    halo_split = split(forward[:, OWN:])

    relative = (iota((ROWS, WIDE), 1) >> 3) + 2 - N1 * block_of(iota((ROWS, WIDE), 0))
    keep = jnp.logical_and(relative != 0, relative != 11)
    square = jnp.where(keep, forward[:, :WIDE], 0.0)
    square = jnp.concatenate([square, jnp.zeros((DEEP - ROWS, WIDE), F32)], axis=0)
    turned = jnp.transpose(square)
    for k in range(3):
        kept[k] = turned[:, k * 128 : (k + 1) * 128]

    def kept_rows(rows):
        return jnp.concatenate([kept[k, rows, :] for k in range(3)], axis=1)

    back_own = split(kept_rows(pl.ds(0, OWN)))
    back_edge = split(
        jnp.concatenate(
            [
                kept_rows(pl.ds(7, NF, stride=N1)),
                kept_rows(pl.ds(0, NF, stride=N1)),
                kept_rows(pl.ds(OWN - 8, 8)),
                kept_rows(pl.ds(0, 8)),
            ],
            axis=0,
        )
    )

    third_eigen = eigen[8 : 8 + CB, :]
    for shift in (16, 32, 64):
        third_eigen = third_eigen + pltpu.roll(third_eigen, shift, 1)
    third_eigen = jnp.concatenate([third_eigen, third_eigen], axis=1)
    own_box = iota((CB, WIDE), 0) == (iota((CB, WIDE), 1) >> 4)
    lane_part = jnp.sum(jnp.where(own_box, third_eigen, 0.0), axis=0, keepdims=True)
    inverse = []
    edges = [0, STEP, 2 * STEP, ROWS]
    for a in range(AB):
        rows = slice(edges[a], edges[a + 1])
        row_part = jnp.sum(
            pick[...].astype(F32)[rows] * eigen[a : a + 1, :], axis=1, keepdims=True
        )
        total = row_part + lane_part
        inverse.append(1.0 / jnp.where(total > 0.0, total, 1.0))
    inverse = jnp.concatenate(inverse, axis=0)

    own_third = wide_product(split(own[...]), fore)
    spectral_own = product(own_split, split(own_third))

    for slot in range(8):
        here = there(*SLOTS[slot])
        if slot in BEHIND:
            here = jnp.logical_and(here, jnp.logical_not(is_last))
        pl.when(here)(sends[slot].wait_recv)
    pl.when(is_last)(handed.wait_recv)
    halo_third = wide_product(split(halo[...]), fore)
    spectral = (spectral_own + product(halo_split, split(halo_third))) * inverse
    spectral = split(
        jnp.concatenate([spectral, jnp.zeros((DEEP - ROWS, WIDE), F32)], axis=0)
    )
    stage_last[...] = product_nt(split(product(back_edge, spectral)), back)
    last = {}
    for slot, (side_s, side_c) in enumerate(SLOTS):
        last[slot] = pltpu.make_async_remote_copy(
            src_ref=stage_last.at[pl.ds(LAST_FROM[slot], LAST_LEN[slot]), :],
            dst_ref=halo_last.at[pl.ds(LAST_AT[slot], LAST_LEN[slot]), :],
            send_sem=send_last.at[slot],
            recv_sem=recv_last.at[slot],
            device_id=peer(-side_s, -side_c),
            device_id_type=MESH,
        )
    for_each(FAR_FIRST, -1, lambda slot: last[slot].start())

    sub = iota((8, 128), 0)

    def shifted(tile, to_top):
        moved = pltpu.roll(tile, 1 if to_top else 7, 0)
        return jnp.where(sub == (0 if to_top else 7), moved, 0.0)

    assembled[...] = own[...]
    for node, row in ((0, 24), (7, 48)):
        place = pl.ds(node, NF, stride=N1)
        assembled[place, :] = assembled[place, :] + halo[pl.ds(row, NF), :]

    def layer_beside(slot, at_prev, at_next, side):
        rows = 8 if side < 0 else 0
        base = halo[pl.ds(FIRST_AT[slot] + rows, 8), :]
        base = base + shifted(halo[pl.ds(FIRST_AT[at_prev] + rows, 8), :], True)
        return base + shifted(halo[pl.ds(FIRST_AT[at_next] + rows, 8), :], False)

    assembled[pl.ds(0, 8), :] = assembled[pl.ds(0, 8), :] + layer_beside(2, 4, 5, -1)
    assembled[pl.ds(OWN - 8, 8), :] = assembled[pl.ds(OWN - 8, 8), :] + layer_beside(3, 6, 7, 1)
    for a in range(AB - 1):
        at = (a * N1 + 7) * N1
        total = assembled[pl.ds(at, 8), :] + assembled[pl.ds(at + 8, 8), :]
        assembled[pl.ds(at, 8), :] = total
        assembled[pl.ds(at + 8, 8), :] = total
    value = assembled[...]
    lane = iota((OWN, 128), 1)
    from_left = jnp.where(jnp.logical_and((lane & 7) == 0, lane > 0), pltpu.roll(value, 1, 1), 0.0)
    from_right = jnp.where(
        jnp.logical_and((lane & 7) == 7, lane < 127), pltpu.roll(value, 127, 1), 0.0
    )
    op_ref[...] = (value + from_left + from_right).reshape(NF, N1, 128)

    solved[...] = product_nt(split(product(back_own, spectral)), back)

    for_each(range(8), 1, lambda slot: last[slot].wait_recv())
    for node, row in ((0, 0), (7, 24)):
        place = pl.ds(node, NF, stride=N1)
        solved[place, :] = solved[place, :] + halo_last[pl.ds(row, NF), :]

    def layer_last(slot, at_prev, at_next):
        base = halo_last[pl.ds(LAST_AT[slot], 8), :]
        base = base + shifted(halo_last[pl.ds(LAST_AT[at_prev], 8), :], True)
        return base + shifted(halo_last[pl.ds(LAST_AT[at_next], 8), :], False)

    solved[pl.ds(0, 8), :] = solved[pl.ds(0, 8), :] + layer_last(2, 4, 5)
    solved[pl.ds(OWN - 8, 8), :] = solved[pl.ds(OWN - 8, 8), :] + layer_last(3, 6, 7)
    pre_ref[...] = solved[...].reshape(NF, N1, 128)

    for_each(range(8), -1, lambda slot: sends[slot].wait_send())
    for_each(range(8), -1, lambda slot: last[slot].wait_send())
    pl.when(is_relay)(handed.wait_send)


def write_out(op_in, pre_in, op_out, pre_out, sem):
    copies = [
        pltpu.make_async_copy(source, target, sem.at[i])
        for i, (source, target) in enumerate(((op_in, op_out), (pre_in, pre_out)))
    ]
    for copy in copies:
        copy.start()
    for copy in copies:
        copy.wait()


def shards(*args):
    operands = list(args) + [jnp.asarray(t) for t in tables()]
    for i in (3, 4, 5):
        operands[i] = jnp.transpose(operands[i], (1, 0, 2))
    out = pltpu.VMEM((NF, N1, CB * N1), F32)
    held = pl.pallas_call(
        kernel,
        out_shape=(out, out),
        in_specs=[pl.BlockSpec(memory_space=pl.ANY)] * len(operands),
        out_specs=(pl.BlockSpec(memory_space=pltpu.VMEM),) * 2,
        scratch_shapes=[pltpu.VMEM(t.shape, t.dtype) for t in operands]
        + [
            pltpu.VMEM((OWN, 128), F32),
            pltpu.VMEM((96, 128), F32),
            pltpu.VMEM((HALO, 128), F32),
            pltpu.VMEM((64, 128), F32),
            pltpu.VMEM((96, 128), F32),
            pltpu.VMEM((OWN, 128), F32),
            pltpu.VMEM((OWN, 128), F32),
            pltpu.VMEM((3, WIDE, 128), F32),
            pltpu.VMEM((CB * M, 128), F32),
            pltpu.VMEM((128, 128), F32),
            pltpu.VMEM((32, 128), F32),
            pltpu.SemaphoreType.DMA((N_IN,)),
            pltpu.SemaphoreType.DMA((8,)),
            pltpu.SemaphoreType.DMA((8,)),
            pltpu.SemaphoreType.DMA((8,)),
            pltpu.SemaphoreType.DMA((8,)),
            pltpu.VMEM((RELAY_LEN, 128), F32),
            pltpu.SemaphoreType.DMA((3,)),
            pltpu.SemaphoreType.DMA((2,)),
        ],
        compiler_params=pltpu.CompilerParams(collective_id=0, has_side_effects=True),
        name="pressure_step",
    )(*operands)
    held = [pltpu.with_memory_space_constraint(value, pltpu.VMEM) for value in held]
    out = jax.ShapeDtypeStruct((NF, N1, CB * N1), F32)
    return pl.pallas_call(
        write_out,
        out_shape=(out, out),
        in_specs=[pl.BlockSpec(memory_space=pltpu.VMEM)] * 2,
        out_specs=(pl.BlockSpec(memory_space=pl.ANY),) * 2,
        scratch_shapes=[pltpu.SemaphoreType.DMA((2,))],
        name="write_out",
    )(*held)


def solution(mesh):
    in_specs = (
        P("stream", "cross", None),
        P(None, "stream", "cross", None),
        P(None, "stream", "cross", None),
        P("stream", None, None),
        P("cross", None, None),
        P(),
        P("stream", None),
        P("cross", None),
        P(),
    )
    out_specs = (P("stream", "cross", None), P("stream", "cross", None))
    return jax.shard_map(shards, mesh=mesh, in_specs=in_specs, out_specs=out_specs, check_vma=False)
```
